32 devices in a mesh: fsdp: 8 (over z, x), sub: 4 (over y, core).
Axes of the slice: x: 2, y: 2, z: 4, core: 2. Of those that a mesh axis runs over, the one named last changes fastest.
Arguments:
- rows: bfloat16 [4096, 960], P(('fsdp', 'sub')), may hold values from -6 to 6
- cotangent: bfloat16 [4096, 960], P(('fsdp', 'sub')), may hold values from -6 to 6
- lengths: int32 [64], P(('fsdp', 'sub')), may hold values from 1 to 64, as said below
- gains: bfloat16 [1920], P('fsdp'), may hold values from 0.5 to 1.5
- attn_weight: bfloat16 [2457600], P(('fsdp', 'sub')), as said below
- gate_weight: bfloat16 [2457600], P(('fsdp', 'sub')), may hold values from -0.1875 to 0.1875
- up_weight: bfloat16 [2457600], P(('fsdp', 'sub')), may hold values from -0.1875 to 0.1875
- down_weight: bfloat16 [2457600], P(('fsdp', 'sub')), may hold values from -0.125 to 0.125
Outputs:
- output: bfloat16 [4096, 960], P(('fsdp', 'sub'))
- input_grad: float32 [4096, 960], P(('fsdp', 'sub'))
- attn_grad: float32 [2457600], P(('fsdp', 'sub'))
- gate_grad: float32 [2457600], P(('fsdp', 'sub'))
- up_grad: float32 [2457600], P(('fsdp', 'sub'))
- down_grad: float32 [2457600], P(('fsdp', 'sub'))
- gain_grad: float32 [1920], P('fsdp')
The draws below stay inside these ranges and needn't reach their ends.
Inputs may be any that keep to these rules, and one draw needn't show every extreme that they name: `lengths`: sequences of one device lie in its first slots in order; the rest are empty. Some sequence has exactly 64 tokens. `attn_weight`: its columns from 1600 on (the output projection's) have a larger scale than the others.
All inputs are finite; a program needn't handle non-finite values.
Results may differ from the reference program's by a relative error of at most 0.012.
Values may be sent and summed in bfloat16 or wider, within the bound.
No kernel may reach another device: no remote copies, remote signals or barrier semaphores. Data moves between devices by JAX's collectives and lax.ppermute only.
A program may use at most 256 MiB of HBM per device.

```python
import jax
import jax.numpy as jnp
from jax import lax

D = 960
KV = 5
HD = 64
FF = 2560
CAP = 128
GROUP = 3
LEN_MAX = 64
NSEQ = 64
TOKENS = 4096
N_FSDP = 8
N_SUB = 4


def draw_lengths(key, part):
    first, second = jax.random.split(jax.random.fold_in(key, 11))
    drawn = jax.random.randint(first, (NSEQ,), 1, LEN_MAX + 1, dtype=jnp.int32)
    chosen = jax.random.randint(second, (), 0, NSEQ, dtype=jnp.int32)
    places = jnp.arange(NSEQ, dtype=jnp.int32)
    return jnp.where(places == chosen, LEN_MAX, drawn).astype(jnp.int32)


def draw_attn_weight(key, part):
    first = jax.random.fold_in(key, 23)
    matrix = jax.random.normal(first, (D, FF), jnp.float32)
    columns = jnp.arange(FF, dtype=jnp.int32)
    widths = jnp.where(columns < D + 2 * KV * HD, 1.0, 5.0) / jnp.sqrt(jnp.float32(D))
    matrix = matrix * widths[None, :]
    return matrix.reshape(-1).astype(jnp.bfloat16)


def block_scale(stream_key, dims, cuts, least, high):
    def one(dim, blocks):
        draws = jax.random.uniform(jax.random.fold_in(jax.random.fold_in(stream_key, 6), dim), (blocks,), jnp.float32, least / len(cuts), high / len(cuts))
        return jnp.repeat(jnp.exp(draws), dims[dim] // blocks).reshape((-1,) + (1,) * (len(dims) - dim - 1))

    level = one(*cuts[0])
    for cut in cuts[1:]:
        level = level * one(*cut)
    return level


def scatter_about(stream_key, extent, spread, most, shards=(), kind=jnp.bfloat16):
    array = jax.random.normal(stream_key, extent, jnp.float32) * spread
    if len(shards) > 0:
        array = block_scale(stream_key, extent, shards, -0.22, 0.18) * array
    return jnp.clip(array, min=-most, max=most).astype(kind)


def setup_inputs(seed: int = 0) -> dict:
    seeds = jax.random.split(jax.random.key(seed), 9)
    return {
        "rows": scatter_about(seeds[0], (TOKENS, D), 1.0, 6.0, ((0, 32),)),
        "cotangent": scatter_about(seeds[1], (TOKENS, D), 1.0, 6.0, ((0, 32),)),
        "lengths": draw_lengths(jax.random.fold_in(seeds[8], 71), 0),
        "gains": jnp.clip(1.0 + 0.1 * jax.random.normal(seeds[3], (2 * D,), jnp.float32), 0.5, 1.5).astype(jnp.bfloat16),
        "attn_weight": draw_attn_weight(jax.random.fold_in(seeds[8], 71), 0),
        "gate_weight": scatter_about(seeds[5], (D * FF,), D ** -0.5, 0.1875, ((0, 32),)),
        "up_weight": scatter_about(seeds[6], (D * FF,), D ** -0.5, 0.1875, ((0, 32),)),
        "down_weight": scatter_about(seeds[7], (D * FF,), FF ** -0.5, 0.125, ((0, 32),)),
    }


EPS = 1e-05
THETA = 100000.0
NEG = -1e+30

def rope_tables(position, width):
    half = jnp.arange(width // 2, dtype=jnp.float32)
    inverse = jnp.exp(-(2.0 * half / width) * jnp.log(jnp.float32(THETA)))
    angle = position.astype(jnp.float32)[:, None] * inverse[None, :]
    cosine = jnp.concatenate([jnp.cos(angle), jnp.cos(angle)], axis=1)
    sine = jnp.concatenate([jnp.sin(angle), jnp.sin(angle)], axis=1)
    return (cosine, sine)

def rotate(values, cosine, sine):
    half = values.shape[-1] // 2
    turned = jnp.concatenate([-values[..., half:], values[..., :half]], axis=-1)
    return values * cosine + turned * sine

def unrotate(grads, cosine, sine):
    half = grads.shape[-1] // 2
    scaled = grads * sine
    return grads * cosine + jnp.concatenate([scaled[..., half:], -scaled[..., :half]], axis=-1)

def norm_forward(values):
    scale = lax.rsqrt(lax.optimization_barrier(jnp.mean(values * values, axis=1, keepdims=True)) + EPS)
    return (values * scale, scale)

def norm_backward(grad_in, normed, scale, gain):
    gain_term = lax.optimization_barrier(jnp.sum(grad_in * normed, axis=0))
    inner = grad_in * gain[None, :]
    back = scale * (inner - normed * lax.optimization_barrier(jnp.mean(inner * normed, axis=1, keepdims=True)))
    return (back, gain_term)

def layout(block_lengths, count):
    slots = jnp.arange(count, dtype=jnp.int32)
    first = block_lengths[0]
    second = block_lengths[1]
    segment = (slots >= first).astype(jnp.int32) + (slots >= first + second).astype(jnp.int32)
    position = slots - first * (segment >= 1).astype(jnp.int32) - second * (segment >= 2).astype(jnp.int32)
    live = (segment < 2).astype(jnp.float32)[:, None]
    allowed = (segment[:, None] == segment[None, :]) & (slots[None, :] <= slots[:, None])
    return (position, live, allowed)

def masked_scores(queries, keys, allowed):
    scores = jnp.einsum('qkgd,jkd->kgqj', queries.astype(jnp.float32), keys.astype(jnp.float32)) * HD ** (-0.5)
    return jnp.where(allowed[None, None], scores, NEG)

def block_pass(rows, cotangent, block_lengths, gains, attn_mat, gate_mat, up_mat, down_mat):
    count = rows.shape[0]
    q_width = D + 2 * KV * HD
    kv_width = KV * HD
    position, live, allowed = layout(block_lengths, count)
    cosine, sine = rope_tables(position, HD)
    gain_attn = gains[:D].astype(jnp.float32)
    gain_mlp = gains[D:].astype(jnp.float32)
    rows32 = rows.astype(jnp.float32)
    normed1, scale1 = norm_forward(rows32)
    input1 = (normed1 * gain_attn[None, :]).astype(jnp.bfloat16)
    projected = jnp.dot(input1, attn_mat[:, :q_width], preferred_element_type=jnp.float32)
    queries = rotate(projected[:, :D].reshape(count, KV, GROUP, HD), cosine[:, None, None, :], sine[:, None, None, :]).astype(jnp.bfloat16)
    keys = rotate(projected[:, D:D + kv_width].reshape(count, KV, HD), cosine[:, None, :], sine[:, None, :]).astype(jnp.bfloat16)
    values = projected[:, D + kv_width:].reshape(count, KV, HD).astype(jnp.bfloat16)
    scores = masked_scores(queries, keys, allowed)
    top = lax.optimization_barrier(jnp.max(scores, axis=-1, keepdims=True))
    expo = jnp.exp(scores - top)
    total = lax.optimization_barrier(jnp.sum(expo, axis=-1, keepdims=True))
    logsum = top + jnp.log(total)
    weights = (expo / total).astype(jnp.bfloat16)
    attended = jnp.einsum('kgqj,jkd->qkgd', weights.astype(jnp.float32), values.astype(jnp.float32)).reshape(count, D).astype(jnp.bfloat16)
    out_mat = attn_mat[:, q_width:]
    hidden1 = rows32 + jnp.dot(attended, out_mat.T, preferred_element_type=jnp.float32)
    normed2, scale2 = norm_forward(hidden1)
    input2 = (normed2 * gain_mlp[None, :]).astype(jnp.bfloat16)
    gate = jnp.dot(input2, gate_mat, preferred_element_type=jnp.float32)
    up = jnp.dot(input2, up_mat, preferred_element_type=jnp.float32)
    sigma = jax.nn.sigmoid(gate)
    active = gate * sigma
    hidden = (active * up).astype(jnp.bfloat16)
    result = hidden1 + jnp.dot(hidden, down_mat.T, preferred_element_type=jnp.float32)
    output = (live * result).astype(jnp.bfloat16)
    grad_out = live * cotangent.astype(jnp.float32)
    grad_outb = grad_out.astype(jnp.bfloat16)
    down_term = jnp.dot(grad_outb.T, hidden, preferred_element_type=jnp.float32)
    grad_hidden = jnp.dot(grad_outb, down_mat, preferred_element_type=jnp.float32)
    grad_gate = (grad_hidden * up * sigma * (1.0 + gate * (1.0 - sigma))).astype(jnp.bfloat16)
    grad_up = (grad_hidden * active).astype(jnp.bfloat16)
    gate_term = jnp.dot(input2.T, grad_gate, preferred_element_type=jnp.float32)
    up_term = jnp.dot(input2.T, grad_up, preferred_element_type=jnp.float32)
    grad_in2 = jnp.dot(grad_gate, gate_mat.T, preferred_element_type=jnp.float32) + jnp.dot(grad_up, up_mat.T, preferred_element_type=jnp.float32)
    back2, gain2_term = norm_backward(grad_in2, normed2, scale2, gain_mlp)
    grad_h1 = grad_out + back2
    grad_h1b = grad_h1.astype(jnp.bfloat16)
    out_term = jnp.dot(grad_h1b.T, attended, preferred_element_type=jnp.float32)
    grad_att = jnp.dot(grad_h1b, out_mat, preferred_element_type=jnp.float32).astype(jnp.bfloat16).reshape(count, KV, GROUP, HD)
    probs = jnp.exp(masked_scores(queries, keys, allowed) - logsum)
    probs_b = probs.astype(jnp.bfloat16)
    value_grad = jnp.einsum('kgqj,qkgd->jkd', probs_b.astype(jnp.float32), grad_att.astype(jnp.float32))
    prob_grad = jnp.einsum('qkgd,jkd->kgqj', grad_att.astype(jnp.float32), values.astype(jnp.float32))
    delta = lax.optimization_barrier(jnp.sum(probs * prob_grad, axis=-1, keepdims=True))
    score_grad = (probs * (prob_grad - delta) * HD ** (-0.5)).astype(jnp.bfloat16)
    query_grad = jnp.einsum('kgqj,jkd->qkgd', score_grad.astype(jnp.float32), keys.astype(jnp.float32))
    key_grad = jnp.einsum('kgqj,qkgd->jkd', score_grad.astype(jnp.float32), queries.astype(jnp.float32))
    query_grad = unrotate(query_grad, cosine[:, None, None, :], sine[:, None, None, :])
    key_grad = unrotate(key_grad, cosine[:, None, :], sine[:, None, :])
    proj_grad = jnp.concatenate([query_grad.reshape(count, D), key_grad.reshape(count, kv_width), value_grad.reshape(count, kv_width)], axis=1).astype(jnp.bfloat16)
    qkv_term = jnp.dot(input1.T, proj_grad, preferred_element_type=jnp.float32)
    grad_in1 = jnp.dot(proj_grad, attn_mat[:, :q_width].T, preferred_element_type=jnp.float32)
    back1, gain1_term = norm_backward(grad_in1, normed1, scale1, gain_attn)
    input_grad = grad_h1 + back1
    attn_term = jnp.concatenate([qkv_term, out_term], axis=1)
    gain_term = jnp.concatenate([gain1_term, gain2_term])
    return (output, input_grad, attn_term, gate_term, up_term, down_term, gain_term)

def reference(rows, cotangent, lengths, gains, attn_weight, gate_weight, up_weight, down_weight):
    blocks = N_FSDP * N_SUB
    attn_mat = attn_weight.reshape(D, FF)
    gate_mat = gate_weight.reshape(D, FF)
    up_mat = up_weight.reshape(D, FF)
    down_mat = down_weight.reshape(D, FF)

    def visit(carry, pieces):
        block_rows, block_cot, block_lengths = pieces
        output, input_grad, attn_term, gate_term, up_term, down_term, gain_term = block_pass(block_rows, block_cot, block_lengths, gains, attn_mat, gate_mat, up_mat, down_mat)
        carry = (carry[0] + attn_term, carry[1] + gate_term, carry[2] + up_term, carry[3] + down_term, carry[4] + gain_term)
        return (carry, (output, input_grad))
    zeros = jnp.zeros((D, FF), jnp.float32)
    start = (zeros, zeros, zeros, zeros, jnp.zeros((2 * D,), jnp.float32))
    sums, (outputs, grads) = lax.scan(visit, start, (rows.reshape(blocks, CAP, D), cotangent.reshape(blocks, CAP, D), lengths.reshape(blocks, 2)))
    return (outputs.reshape(TOKENS, D), grads.reshape(TOKENS, D), sums[0].reshape(-1), sums[1].reshape(-1), sums[2].reshape(-1), sums[3].reshape(-1), sums[4])
```

```python
import jax
import jax.numpy as jnp
from jax import lax
from jax.sharding import PartitionSpec as P

D = 960
KV = 5
HD = 64
FF = 2560
GROUP = 3


EPS = 1e-05
THETA = 100000.0
NEG = -1e30
piece_width = 64


def rope_tables(position, width):
    half = jnp.arange(width // 2, dtype=jnp.float32)
    inverse = jnp.exp(-(2.0 * half / width) * jnp.log(jnp.float32(THETA)))
    angle = position.astype(jnp.float32)[:, None] * inverse[None, :]
    cosine = jnp.concatenate([jnp.cos(angle), jnp.cos(angle)], axis=1)
    sine = jnp.concatenate([jnp.sin(angle), jnp.sin(angle)], axis=1)
    return (cosine, sine)


def rotate(values, cosine, sine):
    half = values.shape[-1] // 2
    turned = jnp.concatenate([-values[..., half:], values[..., :half]], axis=-1)
    return values * cosine + turned * sine


def unrotate(grads, cosine, sine):
    half = grads.shape[-1] // 2
    scaled = grads * sine
    return grads * cosine + jnp.concatenate([scaled[..., half:], -scaled[..., :half]], axis=-1)


def norm_forward(values):
    scale = lax.rsqrt(jnp.mean(values * values, axis=1, keepdims=True) + EPS)
    return (values * scale, scale)


def norm_backward(grad_in, normed, scale, gain):
    gain_term = jnp.sum(grad_in * normed, axis=0)
    inner = grad_in * gain[None, :]
    back = scale * (inner - normed * jnp.mean(inner * normed, axis=1, keepdims=True))
    return (back, gain_term)


def layout(block_lengths, count):
    slots = jnp.arange(count, dtype=jnp.int32)
    first = block_lengths[0]
    second = block_lengths[1]
    segment = (slots >= first).astype(jnp.int32) + (slots >= first + second).astype(jnp.int32)
    position = (
        slots - first * (segment >= 1).astype(jnp.int32) - second * (segment >= 2).astype(jnp.int32)
    )
    live = (segment < 2).astype(jnp.float32)[:, None]
    allowed = (segment[:, None] == segment[None, :]) & (slots[None, :] <= slots[:, None])
    return (position, live, allowed)


def masked_scores(queries, keys, allowed):
    scores = jnp.einsum(
        "qkgd,jkd->kgqj", queries, keys, preferred_element_type=jnp.float32
    ) * HD ** (-0.5)
    return jnp.where(allowed[None, None], scores, NEG)


def attend(projected, cosine, sine, allowed, count):
    kv_width = KV * HD
    queries = rotate(
        projected[:, :D].reshape(count, KV, GROUP, HD),
        cosine[:, None, None, :],
        sine[:, None, None, :],
    ).astype(jnp.bfloat16)
    keys = rotate(
        projected[:, D : D + kv_width].reshape(count, KV, HD), cosine[:, None, :], sine[:, None, :]
    ).astype(jnp.bfloat16)
    values = projected[:, D + kv_width :].reshape(count, KV, HD).astype(jnp.bfloat16)
    scores = masked_scores(queries, keys, allowed)
    top = jnp.max(scores, axis=-1, keepdims=True)
    expo = jnp.exp(scores - top)
    total = jnp.sum(expo, axis=-1, keepdims=True)
    logsum = top + jnp.log(total)
    weights = (expo / total).astype(jnp.bfloat16)
    attended = (
        jnp.einsum("kgqj,jkd->qkgd", weights, values, preferred_element_type=jnp.float32)
        .reshape(count, D)
        .astype(jnp.bfloat16)
    )
    return (queries, keys, values, logsum, attended)


def attend_back(grad_att, queries, keys, values, logsum, allowed, cosine, sine, count):
    kv_width = KV * HD
    probs = jnp.exp(masked_scores(queries, keys, allowed) - logsum)
    probs_b = probs.astype(jnp.bfloat16)
    value_grad = jnp.einsum("kgqj,qkgd->jkd", probs_b, grad_att, preferred_element_type=jnp.float32)
    prob_grad = jnp.einsum("qkgd,jkd->kgqj", grad_att, values, preferred_element_type=jnp.float32)
    delta = jnp.sum(probs * prob_grad, axis=-1, keepdims=True)
    score_grad = (probs * (prob_grad - delta) * HD ** (-0.5)).astype(jnp.bfloat16)
    query_grad = jnp.einsum("kgqj,jkd->qkgd", score_grad, keys, preferred_element_type=jnp.float32)
    key_grad = jnp.einsum("kgqj,qkgd->jkd", score_grad, queries, preferred_element_type=jnp.float32)
    query_grad = unrotate(query_grad, cosine[:, None, None, :], sine[:, None, None, :])
    key_grad = unrotate(key_grad, cosine[:, None, :], sine[:, None, :])
    return jnp.concatenate(
        [
            query_grad.reshape(count, D),
            key_grad.reshape(count, kv_width),
            value_grad.reshape(count, kv_width),
        ],
        axis=1,
    ).astype(jnp.bfloat16)


def collect(attn_flat, gate_flat, up_flat, down_flat):
    whole = (
        lax.all_gather(attn_flat, ("fsdp", "sub"), axis=0, tiled=True),
        lax.all_gather(gate_flat, ("fsdp", "sub"), axis=0, tiled=True),
        lax.all_gather(up_flat, ("fsdp", "sub"), axis=0, tiled=True),
        lax.all_gather(down_flat, ("fsdp", "sub"), axis=0, tiled=True),
    )
    return tuple((piece.reshape(D, FF) for piece in whole))


def flat_terms(pair_lists, count):
    results = []
    for pairs in pair_lists:
        blocks = [
            jnp.dot(left.T, right, preferred_element_type=jnp.float32) for left, right in pairs
        ]
        joined = blocks[0] if len(blocks) == 1 else jnp.concatenate(blocks, axis=1)
        results.append(joined.reshape(-1).reshape(count, piece_width))
    return jnp.concatenate(results, axis=1)


def split_owned(owned):
    return tuple(
        (
            owned[:, index * piece_width : (index + 1) * piece_width].reshape(-1)
            for index in range(4)
        )
    )


def spread(pair_lists):
    share = D * FF // (piece_width * lax.axis_size("fsdp") * lax.axis_size("sub"))
    owned = lax.psum_scatter(
        flat_terms(pair_lists, share * lax.axis_size(("fsdp", "sub"))),
        ("fsdp", "sub"),
        scatter_dimension=0,
        tiled=True,
    )
    return split_owned(owned)


def flat_path(
    rows32,
    cotangent,
    live,
    allowed,
    cosine,
    sine,
    gain_attn,
    gain_mlp,
    normed1,
    scale1,
    input1,
    flats,
):
    count = rows32.shape[0]
    q_width = D + 2 * KV * HD
    attn_mat, gate_mat, up_mat, down_mat = collect(flats[0], flats[1], flats[2], flats[3])
    projected = jnp.dot(input1, attn_mat[:, :q_width], preferred_element_type=jnp.float32)
    queries, keys, values, logsum, attended = attend(projected, cosine, sine, allowed, count)
    hidden1 = rows32 + jnp.dot(
        attended, attn_mat[:, q_width:].T, preferred_element_type=jnp.float32
    )
    normed2, scale2 = norm_forward(hidden1)
    input2 = (normed2 * gain_mlp[None, :]).astype(jnp.bfloat16)
    gate = jnp.dot(input2, gate_mat, preferred_element_type=jnp.float32)
    up = jnp.dot(input2, up_mat, preferred_element_type=jnp.float32)
    sigma = jax.nn.sigmoid(gate)
    active = gate * sigma
    hidden = (active * up).astype(jnp.bfloat16)
    result = hidden1 + jnp.dot(hidden, down_mat.T, preferred_element_type=jnp.float32)
    output = (live * result).astype(jnp.bfloat16)
    attn_back, gate_back, up_back, down_back = collect(flats[0], flats[1], flats[2], flats[3])
    grad_out = live * cotangent.astype(jnp.float32)
    grad_outb = grad_out.astype(jnp.bfloat16)
    grad_hidden = jnp.dot(grad_outb, down_back, preferred_element_type=jnp.float32)
    grad_gate = (grad_hidden * up * sigma * (1.0 + gate * (1.0 - sigma))).astype(jnp.bfloat16)
    grad_up = (grad_hidden * active).astype(jnp.bfloat16)
    grad_in2 = jnp.dot(grad_gate, gate_back.T, preferred_element_type=jnp.float32) + jnp.dot(
        grad_up, up_back.T, preferred_element_type=jnp.float32
    )
    back2, gain2_term = norm_backward(grad_in2, normed2, scale2, gain_mlp)
    grad_h1 = grad_out + back2
    grad_h1b = grad_h1.astype(jnp.bfloat16)
    grad_att = (
        jnp.dot(grad_h1b, attn_back[:, q_width:], preferred_element_type=jnp.float32)
        .astype(jnp.bfloat16)
        .reshape(count, KV, GROUP, HD)
    )
    proj_grad = attend_back(grad_att, queries, keys, values, logsum, allowed, cosine, sine, count)
    grad_in1 = jnp.dot(proj_grad, attn_back[:, :q_width].T, preferred_element_type=jnp.float32)
    back1, gain1_term = norm_backward(grad_in1, normed1, scale1, gain_attn)
    input_grad = grad_h1 + back1
    pair_lists = (
        ((input1, proj_grad), (grad_h1b, attended)),
        ((input2, grad_gate),),
        ((input2, grad_up),),
        ((grad_outb, hidden),),
    )
    owned = spread(pair_lists)
    return (output, input_grad, owned, gain1_term, gain2_term)


def plain_body(rows, cotangent, lengths, gains, attn_weight, gate_weight, up_weight, down_weight):
    count = rows.shape[0]
    position, live, allowed = layout(lengths, count)
    cosine, sine = rope_tables(position, HD)
    full_gains = lax.all_gather(gains, "fsdp", axis=0, tiled=True).astype(jnp.float32)
    gain_attn = full_gains[:D]
    gain_mlp = full_gains[D:]
    rows32 = rows.astype(jnp.float32)
    normed1, scale1 = norm_forward(rows32)
    input1 = (normed1 * gain_attn[None, :]).astype(jnp.bfloat16)
    flats = (attn_weight, gate_weight, up_weight, down_weight)
    output, input_grad, owned, gain1_term, gain2_term = flat_path(
        rows32,
        cotangent,
        live,
        allowed,
        cosine,
        sine,
        gain_attn,
        gain_mlp,
        normed1,
        scale1,
        input1,
        flats,
    )
    gain_total = lax.psum(jnp.concatenate([gain1_term, gain2_term]), ("fsdp", "sub"))
    share = gains.shape[0]
    gain_grad = lax.dynamic_slice_in_dim(gain_total, lax.axis_index("fsdp") * share, share)
    return (output, input_grad, owned[0], owned[1], owned[2], owned[3], gain_grad)


def bits_of(size):
    return [1 << k for k in range(size.bit_length() - 1)]


def swap(value, stage):
    axis, bit = stage
    return lax.ppermute(value, axis, [(i, i ^ bit) for i in range(lax.axis_size(axis))])


def gather_block(block, far, near, last):
    rows, width = block.shape
    held = block[None]
    for stage in far:
        held = jnp.concatenate([held, swap(held, stage)], axis=0)
    halves = []
    for h in range(2):
        half = held[:, :, h * (width // 2) : (h + 1) * (width // 2)]
        count = half.shape[0]
        if h == 0:
            half = jnp.concatenate([half, swap(half, near[0])], axis=0)
            half = jnp.concatenate([half, swap(half, near[1])], axis=0)
        else:
            half = jnp.stack([half, swap(half, near[1])], axis=0)
            half = jnp.stack([half, swap(half, near[0])], axis=1)
            half = half.reshape(4 * count, rows, width // 2)
        for stage in last:
            half = jnp.concatenate([half, swap(half, stage)], axis=0)
        halves.append(half.reshape(-1, width // 2))
    return halves


def add_pair(kept, came):
    return (kept.astype(jnp.float32) + came.astype(jnp.float32)).astype(jnp.bfloat16)


def reduce_halves(halves, rows, far, near, last):
    done = []
    for h, half in enumerate(halves):
        width = half.shape[1]
        held = half.reshape(-1, rows, width)
        for stage in reversed(last):
            mid = held.shape[0] // 2
            held = add_pair(held[:mid], swap(held[mid:], stage))
        if h == 0:
            for stage in (near[1], near[0]):
                mid = held.shape[0] // 2
                held = add_pair(held[:mid], swap(held[mid:], stage))
        else:
            held = held.reshape(2, 2, -1, rows, width)
            held = add_pair(held[:, 0], swap(held[:, 1], near[0]))
            held = add_pair(held[0], swap(held[1], near[1]))
        for stage in reversed(far):
            mid = held.shape[0] // 2
            held = add_pair(held[:mid], swap(held[mid:], stage))
        done.append(held.reshape(rows, width))
    return done


def body(rows, cotangent, lengths, gains, attn_weight, gate_weight, up_weight, down_weight):
    count = rows.shape[0]
    n_fsdp = lax.axis_size("fsdp")
    n_sub = lax.axis_size("sub")
    n_all = n_fsdp * n_sub
    own = D // n_all
    padded = -(-(own + 1) // 16) * 16
    wide = n_all * padded
    half_ff = FF // 2
    share = gains.shape[0]
    kv_width = KV * HD
    my_fsdp = lax.axis_index("fsdp")
    my_sub = lax.axis_index("sub")
    fsdp_bits = bits_of(n_fsdp)
    sub_bits = bits_of(n_sub)
    far = [("fsdp", bit) for bit in fsdp_bits[1:]]
    near = [("fsdp", fsdp_bits[0]), ("sub", sub_bits[-1])]
    last = [("sub", bit) for bit in reversed(sub_bits[:-1])]
    order = far + near + last

    column = jnp.arange(wide, dtype=jnp.int32)
    place = column // padded
    inner = column % padded
    block_fsdp = jnp.zeros_like(column)
    block_sub = jnp.zeros_like(column)
    for k, (axis, bit) in enumerate(order):
        digit = ((place >> k) & 1) * bit
        if axis == "fsdp":
            block_fsdp = block_fsdp + digit
        else:
            block_sub = block_sub + digit
    owner = (block_fsdp ^ my_fsdp) * n_sub + (block_sub ^ my_sub)
    real = inner < own
    source = jnp.where(real, owner * own + inner, -1)
    spread_mat = (jnp.arange(D, dtype=jnp.int32)[:, None] == source[None, :]).astype(jnp.bfloat16)
    real_f = real.astype(jnp.float32)[None, :]

    def padded_block(flat):
        return jnp.pad(flat.reshape(own, FF), ((0, padded - own), (0, 0)))

    attn_block = padded_block(attn_weight)
    attn_block = attn_block.at[own, :share].set(gains)
    attn_q, attn_o = gather_block(attn_block, far, near, last)
    gate_w = gather_block(padded_block(gate_weight), far, near, last)
    up_w = gather_block(padded_block(up_weight), far, near, last)
    down_w = gather_block(padded_block(down_weight), far, near, last)

    fsdp_places = [0] * n_fsdp
    for p in range(n_all):
        f = sum(((p >> k) & 1) * bit for k, (axis, bit) in enumerate(order) if axis == "fsdp")
        s = sum(((p >> k) & 1) * bit for k, (axis, bit) in enumerate(order) if axis == "sub")
        if s == 0:
            fsdp_places[f] = p
    pieces = attn_q.reshape(n_all, padded, half_ff)[:, own, :share]
    pieces = pieces[jnp.array(fsdp_places)]
    turn = (
        (jnp.arange(n_fsdp)[:, None] ^ my_fsdp) == jnp.arange(n_fsdp)[None, :]
    ).astype(jnp.bfloat16)
    full_gains = jnp.dot(turn, pieces, preferred_element_type=jnp.float32).reshape(2, D)
    gains_p = jnp.dot(
        full_gains.astype(jnp.bfloat16), spread_mat, preferred_element_type=jnp.float32
    )
    gain_attn = gains_p[0]
    gain_mlp = gains_p[1]

    position, live, allowed = layout(lengths, count)
    cosine, sine = rope_tables(position, HD)

    def norm(values):
        mean = jnp.sum(values * values, axis=1, keepdims=True) / D
        scale = lax.rsqrt(mean + EPS)
        return values * scale, scale

    def norm_back(grad_in, normed, scale, gain):
        gain_term = jnp.sum(grad_in * normed, axis=0)
        inner_g = grad_in * gain[None, :]
        mean = jnp.sum(inner_g * normed, axis=1, keepdims=True) / D
        return scale * (inner_g - normed * mean), gain_term

    def mm(a, b):
        return jnp.dot(a, b, preferred_element_type=jnp.float32)

    def mm_t(a, b):
        return lax.dot_general(a, b, (((1,), (1,)), ((), ())), preferred_element_type=jnp.float32)

    def term(a, b):
        return lax.dot_general(
            a, b, (((0,), (0,)), ((), ())), preferred_element_type=jnp.float32
        ).astype(jnp.bfloat16)

    rows32 = mm(rows, spread_mat)
    grad_out = live * mm(cotangent, spread_mat)
    normed1, scale1 = norm(rows32)
    input1 = (normed1 * gain_attn[None, :]).astype(jnp.bfloat16)
    projected = jnp.concatenate([mm(input1, attn_q), mm(input1, attn_o[:, :kv_width])], axis=1)
    queries, keys, values, logsum, attended = attend(projected, cosine, sine, allowed, count)
    out_mat = attn_o[:, kv_width:]
    hidden1 = rows32 + mm_t(attended, out_mat)
    normed2, scale2 = norm(hidden1)
    input2 = (normed2 * gain_mlp[None, :]).astype(jnp.bfloat16)
    grad_outb = grad_out.astype(jnp.bfloat16)
    result = hidden1
    grad_in2 = jnp.zeros_like(hidden1)
    gate_terms, up_terms, down_terms = [], [], []
    for h in range(2):
        gate = mm(input2, gate_w[h])
        up = mm(input2, up_w[h])
        sigma = jax.nn.sigmoid(gate)
        active = gate * sigma
        hidden = (active * up).astype(jnp.bfloat16)
        down_terms.append(term(grad_outb, hidden))
        result = result + mm_t(hidden, down_w[h])
        grad_hidden = mm(grad_outb, down_w[h])
        grad_gate = (grad_hidden * up * sigma * (1.0 + gate * (1.0 - sigma))).astype(jnp.bfloat16)
        grad_up = (grad_hidden * active).astype(jnp.bfloat16)
        gate_terms.append(term(input2, grad_gate))
        up_terms.append(term(input2, grad_up))
        grad_in2 = grad_in2 + mm_t(grad_gate, gate_w[h]) + mm_t(grad_up, up_w[h])
    output = mm_t((live * result).astype(jnp.bfloat16), spread_mat).astype(jnp.bfloat16)
    back2, gain2_term = norm_back(grad_in2, normed2, scale2, gain_mlp)
    grad_h1 = grad_out + back2
    grad_h1b = grad_h1.astype(jnp.bfloat16)
    grad_att = mm(grad_h1b, out_mat).astype(jnp.bfloat16).reshape(count, KV, GROUP, HD)
    proj_grad = attend_back(grad_att, queries, keys, values, logsum, allowed, cosine, sine, count)
    grad_in1 = mm_t(proj_grad[:, :half_ff], attn_q) * real_f + mm_t(
        proj_grad[:, half_ff:], attn_o[:, :kv_width]
    )
    back1, gain1_term = norm_back(grad_in1, normed1, scale1, gain_attn)
    input_grad = lax.dot_general(
        grad_h1 + back1,
        spread_mat.astype(jnp.float32),
        (((1,), (1,)), ((), ())),
        precision=lax.Precision.HIGHEST,
    )
    gain_terms = lax.dot_general(
        jnp.stack([gain1_term, gain2_term]),
        spread_mat.astype(jnp.float32),
        (((1,), (1,)), ((), ())),
        precision=lax.Precision.HIGHEST,
    ).reshape(n_fsdp, share)
    gain_terms = jnp.dot(turn.astype(jnp.float32), gain_terms, precision=lax.Precision.HIGHEST)
    place_fsdp = [0] * n_all
    for p in range(n_all):
        place_fsdp[p] = sum(
            ((p >> k) & 1) * bit for k, (axis, bit) in enumerate(order) if axis == "fsdp"
        )
    gain_rows = gain_terms[jnp.array(place_fsdp)].astype(jnp.bfloat16)
    q_term = term(input1, proj_grad[:, :half_ff]).reshape(n_all, padded, half_ff)
    q_term = q_term.at[:, own, :share].set(gain_rows).reshape(wide, half_ff)
    o_term = jnp.concatenate(
        [term(input1, proj_grad[:, half_ff:]), term(grad_h1b, attended)], axis=1
    )

    def owned(halves):
        return reduce_halves(halves, padded, far, near, last)

    def flat(halves):
        joined = jnp.concatenate([half[:own] for half in halves], axis=1)
        return joined.astype(jnp.float32).reshape(-1)

    down_own = owned(down_terms)
    gate_own = owned(gate_terms)
    up_own = owned(up_terms)
    attn_own = owned([q_term, o_term])
    gain_grad = attn_own[0][own, :share].astype(jnp.float32)
    return (
        output,
        input_grad,
        flat(attn_own),
        flat(gate_own),
        flat(up_own),
        flat(down_own),
        gain_grad,
    )


def solution(mesh):
    n_fsdp, n_sub = mesh.shape["fsdp"], mesh.shape["sub"]
    n_all = n_fsdp * n_sub
    by_rows = (
        D % n_all == 0 and n_all & (n_all - 1) == 0 and n_fsdp > 1 and n_sub > 1 and 2 * D // n_fsdp <= FF // 2
    )
    in_specs = (
        P(("fsdp", "sub"), None),
        P(("fsdp", "sub"), None),
        P(("fsdp", "sub")),
        P("fsdp"),
        P(("fsdp", "sub")),
        P(("fsdp", "sub")),
        P(("fsdp", "sub")),
        P(("fsdp", "sub")),
    )
    out_specs = (
        P(("fsdp", "sub"), None),
        P(("fsdp", "sub"), None),
        P(("fsdp", "sub")),
        P(("fsdp", "sub")),
        P(("fsdp", "sub")),
        P(("fsdp", "sub")),
        P("fsdp"),
    )
    return jax.shard_map(body if by_rows else plain_body, mesh=mesh, in_specs=in_specs, out_specs=out_specs, check_vma=False)
```

```python
import jax
import jax.numpy as jnp
from jax import lax
from jax.experimental import pallas as pl
from jax.experimental.pallas import tpu as pltpu
from jax.sharding import PartitionSpec as P

D = 960
KV = 5
HD = 64
FF = 2560
GROUP = 3


EPS = 1e-05
THETA = 100000.0
NEG = -1e30
piece_width = 64


def rope_tables(position, width):
    half = jnp.arange(width // 2, dtype=jnp.float32)
    inverse = jnp.exp(-(2.0 * half / width) * jnp.log(jnp.float32(THETA)))
    angle = position.astype(jnp.float32)[:, None] * inverse[None, :]
    cosine = jnp.concatenate([jnp.cos(angle), jnp.cos(angle)], axis=1)
    sine = jnp.concatenate([jnp.sin(angle), jnp.sin(angle)], axis=1)
    return (cosine, sine)


def rotate(values, cosine, sine):
    half = values.shape[-1] // 2
    turned = jnp.concatenate([-values[..., half:], values[..., :half]], axis=-1)
    return values * cosine + turned * sine


def unrotate(grads, cosine, sine):
    half = grads.shape[-1] // 2
    scaled = grads * sine
    return grads * cosine + jnp.concatenate([scaled[..., half:], -scaled[..., :half]], axis=-1)


def norm_forward(values):
    scale = lax.rsqrt(jnp.mean(values * values, axis=1, keepdims=True) + EPS)
    return (values * scale, scale)


def norm_backward(grad_in, normed, scale, gain):
    gain_term = jnp.sum(grad_in * normed, axis=0)
    inner = grad_in * gain[None, :]
    back = scale * (inner - normed * jnp.mean(inner * normed, axis=1, keepdims=True))
    return (back, gain_term)


def layout(block_lengths, count):
    slots = jnp.arange(count, dtype=jnp.int32)
    first = block_lengths[0]
    second = block_lengths[1]
    segment = (slots >= first).astype(jnp.int32) + (slots >= first + second).astype(jnp.int32)
    position = (
        slots - first * (segment >= 1).astype(jnp.int32) - second * (segment >= 2).astype(jnp.int32)
    )
    live = (segment < 2).astype(jnp.float32)[:, None]
    allowed = (segment[:, None] == segment[None, :]) & (slots[None, :] <= slots[:, None])
    return (position, live, allowed)


def masked_scores(queries, keys, allowed):
    scores = jnp.einsum(
        "qkgd,jkd->kgqj", queries, keys, preferred_element_type=jnp.float32
    ) * HD ** (-0.5)
    return jnp.where(allowed[None, None], scores, NEG)


def attend(projected, cosine, sine, allowed, count):
    kv_width = KV * HD
    queries = rotate(
        projected[:, :D].reshape(count, KV, GROUP, HD),
        cosine[:, None, None, :],
        sine[:, None, None, :],
    ).astype(jnp.bfloat16)
    keys = rotate(
        projected[:, D : D + kv_width].reshape(count, KV, HD), cosine[:, None, :], sine[:, None, :]
    ).astype(jnp.bfloat16)
    values = projected[:, D + kv_width :].reshape(count, KV, HD).astype(jnp.bfloat16)
    scores = masked_scores(queries, keys, allowed)
    top = jnp.max(scores, axis=-1, keepdims=True)
    expo = jnp.exp(scores - top)
    total = jnp.sum(expo, axis=-1, keepdims=True)
    logsum = top + jnp.log(total)
    weights = (expo / total).astype(jnp.bfloat16)
    attended = (
        jnp.einsum("kgqj,jkd->qkgd", weights, values, preferred_element_type=jnp.float32)
        .reshape(count, D)
        .astype(jnp.bfloat16)
    )
    return (queries, keys, values, logsum, attended)


def attend_back(grad_att, queries, keys, values, logsum, allowed, cosine, sine, count):
    kv_width = KV * HD
    probs = jnp.exp(masked_scores(queries, keys, allowed) - logsum)
    probs_b = probs.astype(jnp.bfloat16)
    value_grad = jnp.einsum("kgqj,qkgd->jkd", probs_b, grad_att, preferred_element_type=jnp.float32)
    prob_grad = jnp.einsum("qkgd,jkd->kgqj", grad_att, values, preferred_element_type=jnp.float32)
    delta = jnp.sum(probs * prob_grad, axis=-1, keepdims=True)
    score_grad = (probs * (prob_grad - delta) * HD ** (-0.5)).astype(jnp.bfloat16)
    query_grad = jnp.einsum("kgqj,jkd->qkgd", score_grad, keys, preferred_element_type=jnp.float32)
    key_grad = jnp.einsum("kgqj,qkgd->jkd", score_grad, queries, preferred_element_type=jnp.float32)
    query_grad = unrotate(query_grad, cosine[:, None, None, :], sine[:, None, None, :])
    key_grad = unrotate(key_grad, cosine[:, None, :], sine[:, None, :])
    return jnp.concatenate(
        [
            query_grad.reshape(count, D),
            key_grad.reshape(count, kv_width),
            value_grad.reshape(count, kv_width),
        ],
        axis=1,
    ).astype(jnp.bfloat16)


def collect(attn_flat, gate_flat, up_flat, down_flat):
    whole = (
        lax.all_gather(attn_flat, ("fsdp", "sub"), axis=0, tiled=True),
        lax.all_gather(gate_flat, ("fsdp", "sub"), axis=0, tiled=True),
        lax.all_gather(up_flat, ("fsdp", "sub"), axis=0, tiled=True),
        lax.all_gather(down_flat, ("fsdp", "sub"), axis=0, tiled=True),
    )
    return tuple((piece.reshape(D, FF) for piece in whole))


def flat_terms(pair_lists, count):
    results = []
    for pairs in pair_lists:
        blocks = [
            jnp.dot(left.T, right, preferred_element_type=jnp.float32) for left, right in pairs
        ]
        joined = blocks[0] if len(blocks) == 1 else jnp.concatenate(blocks, axis=1)
        results.append(joined.reshape(-1).reshape(count, piece_width))
    return jnp.concatenate(results, axis=1)


def split_owned(owned):
    return tuple(
        (
            owned[:, index * piece_width : (index + 1) * piece_width].reshape(-1)
            for index in range(4)
        )
    )


def spread(pair_lists):
    share = D * FF // (piece_width * lax.axis_size("fsdp") * lax.axis_size("sub"))
    owned = lax.psum_scatter(
        flat_terms(pair_lists, share * lax.axis_size(("fsdp", "sub"))),
        ("fsdp", "sub"),
        scatter_dimension=0,
        tiled=True,
    )
    return split_owned(owned)


def flat_path(
    rows32,
    cotangent,
    live,
    allowed,
    cosine,
    sine,
    gain_attn,
    gain_mlp,
    normed1,
    scale1,
    input1,
    flats,
):
    count = rows32.shape[0]
    q_width = D + 2 * KV * HD
    attn_mat, gate_mat, up_mat, down_mat = collect(flats[0], flats[1], flats[2], flats[3])
    projected = jnp.dot(input1, attn_mat[:, :q_width], preferred_element_type=jnp.float32)
    queries, keys, values, logsum, attended = attend(projected, cosine, sine, allowed, count)
    hidden1 = rows32 + jnp.dot(
        attended, attn_mat[:, q_width:].T, preferred_element_type=jnp.float32
    )
    normed2, scale2 = norm_forward(hidden1)
    input2 = (normed2 * gain_mlp[None, :]).astype(jnp.bfloat16)
    gate = jnp.dot(input2, gate_mat, preferred_element_type=jnp.float32)
    up = jnp.dot(input2, up_mat, preferred_element_type=jnp.float32)
    sigma = jax.nn.sigmoid(gate)
    active = gate * sigma
    hidden = (active * up).astype(jnp.bfloat16)
    result = hidden1 + jnp.dot(hidden, down_mat.T, preferred_element_type=jnp.float32)
    output = (live * result).astype(jnp.bfloat16)
    attn_back, gate_back, up_back, down_back = collect(flats[0], flats[1], flats[2], flats[3])
    grad_out = live * cotangent.astype(jnp.float32)
    grad_outb = grad_out.astype(jnp.bfloat16)
    grad_hidden = jnp.dot(grad_outb, down_back, preferred_element_type=jnp.float32)
    grad_gate = (grad_hidden * up * sigma * (1.0 + gate * (1.0 - sigma))).astype(jnp.bfloat16)
    grad_up = (grad_hidden * active).astype(jnp.bfloat16)
    grad_in2 = jnp.dot(grad_gate, gate_back.T, preferred_element_type=jnp.float32) + jnp.dot(
        grad_up, up_back.T, preferred_element_type=jnp.float32
    )
    back2, gain2_term = norm_backward(grad_in2, normed2, scale2, gain_mlp)
    grad_h1 = grad_out + back2
    grad_h1b = grad_h1.astype(jnp.bfloat16)
    grad_att = (
        jnp.dot(grad_h1b, attn_back[:, q_width:], preferred_element_type=jnp.float32)
        .astype(jnp.bfloat16)
        .reshape(count, KV, GROUP, HD)
    )
    proj_grad = attend_back(grad_att, queries, keys, values, logsum, allowed, cosine, sine, count)
    grad_in1 = jnp.dot(proj_grad, attn_back[:, :q_width].T, preferred_element_type=jnp.float32)
    back1, gain1_term = norm_backward(grad_in1, normed1, scale1, gain_attn)
    input_grad = grad_h1 + back1
    pair_lists = (
        ((input1, proj_grad), (grad_h1b, attended)),
        ((input2, grad_gate),),
        ((input2, grad_up),),
        ((grad_outb, hidden),),
    )
    owned = spread(pair_lists)
    return (output, input_grad, owned, gain1_term, gain2_term)


def plain_body(rows, cotangent, lengths, gains, attn_weight, gate_weight, up_weight, down_weight):
    count = rows.shape[0]
    position, live, allowed = layout(lengths, count)
    cosine, sine = rope_tables(position, HD)
    full_gains = lax.all_gather(gains, "fsdp", axis=0, tiled=True).astype(jnp.float32)
    gain_attn = full_gains[:D]
    gain_mlp = full_gains[D:]
    rows32 = rows.astype(jnp.float32)
    normed1, scale1 = norm_forward(rows32)
    input1 = (normed1 * gain_attn[None, :]).astype(jnp.bfloat16)
    flats = (attn_weight, gate_weight, up_weight, down_weight)
    output, input_grad, owned, gain1_term, gain2_term = flat_path(
        rows32,
        cotangent,
        live,
        allowed,
        cosine,
        sine,
        gain_attn,
        gain_mlp,
        normed1,
        scale1,
        input1,
        flats,
    )
    gain_total = lax.psum(jnp.concatenate([gain1_term, gain2_term]), ("fsdp", "sub"))
    share = gains.shape[0]
    gain_grad = lax.dynamic_slice_in_dim(gain_total, lax.axis_index("fsdp") * share, share)
    return (output, input_grad, owned[0], owned[1], owned[2], owned[3], gain_grad)


BF = jnp.bfloat16
F32 = jnp.float32


def swap(value, axis, bit):
    return lax.ppermute(value, axis, [(i, i ^ bit) for i in range(lax.axis_size(axis))])


def after(value, *done):
    return lax.optimization_barrier((value, *done))[0]


def add2(kept, came):
    return (kept.astype(F32) + came.astype(F32)).astype(BF)


def pick(value, index, axis):
    return lax.dynamic_index_in_dim(value, index, axis, keepdims=False)


def put2(own, came, bit, axis):
    first = bit == 0
    return jnp.stack([jnp.where(first, own, came), jnp.where(first, came, own)], axis=axis)


def mm(a, b):
    return jnp.dot(a, b, preferred_element_type=F32)


def mm_t(a, b):
    return lax.dot_general(a, b, (((1,), (1,)), ((), ())), preferred_element_type=F32)


def term(a, b):
    return lax.dot_general(a, b, (((0,), (0,)), ((), ())), preferred_element_type=F32).astype(BF)


def dot_f(a, b):
    return lax.dot_general(a, b, (((1,), (0,)), ((), ())), preferred_element_type=F32)


def dot_t(a, b):
    return lax.dot_general(a, b, (((1,), (1,)), ((), ())), preferred_element_type=F32)


def dot_0(a, b):
    return lax.dot_general(a, b, (((0,), (0,)), ((), ())), preferred_element_type=F32)


def norm_rows(values):
    mean = jnp.sum(values * values, axis=1, keepdims=True) * (1.0 / D)
    scale = lax.rsqrt(mean + EPS)
    return values * scale, scale


def norm_rows_back(grad_in, normed, scale, gain):
    gain_term = jnp.sum(grad_in * normed, axis=0, keepdims=True)
    inner = grad_in * gain
    mean = jnp.sum(inner * normed, axis=1, keepdims=True) * (1.0 / D)
    return scale * (inner - normed * mean), gain_term


def first_half(shape):
    return lax.broadcasted_iota(jnp.int32, shape, 1) % HD < HD // 2


def gain_masks(owner, my_fsdp, n_fsdp, own, share):
    wide = owner.shape[1]
    per = share // own
    place = lax.broadcasted_iota(jnp.int32, (n_fsdp, wide), 0) ^ my_fsdp
    group = owner // per
    return place == group, place == group + n_fsdp // 2


def slot_matrix(owner, inner, own, share):
    per = share // own
    slot = jnp.where(inner < own, owner % per * own + inner, -1)
    return (lax.broadcasted_iota(jnp.int32, (share, owner.shape[1]), 0) == slot).astype(F32).astype(BF)


def make_forward(n_fsdp, own, padded, share):
    kv_width = KV * HD

    def kernel(
        place_ref, rows_ref, pieces_ref, owner_ref, inner_ref, cos_ref, sin_ref, seg_ref,
        attn_q_ref, attn_o_ref,
        input1_ref, qk_ref, v_ref, logsum_ref, att_ref, hidden1_ref, input2_ref, gains_ref,
    ):
        owner = owner_ref[...]
        first, second = gain_masks(owner, place_ref[0], n_fsdp, own, share)
        spots = dot_f(pieces_ref[...], slot_matrix(owner, inner_ref[...], own, share))
        gain1 = jnp.sum(jnp.where(first, spots, 0.0), axis=0, keepdims=True)
        gain2 = jnp.sum(jnp.where(second, spots, 0.0), axis=0, keepdims=True)
        gains_ref[0:1, :] = gain1
        gains_ref[1:2, :] = gain2
        rows = rows_ref[...]
        normed, _ = norm_rows(rows)
        input1 = (normed * gain1).astype(BF)
        input1_ref[...] = input1
        projected = dot_f(input1, attn_q_ref[...])
        cosine = cos_ref[...]
        sine = sin_ref[...]
        low = first_half(cosine.shape)
        for i in range(projected.shape[1] // 128):
            part = projected[:, 128 * i : 128 * (i + 1)]
            turned = jnp.where(low, -pltpu.roll(part, 96, 1), pltpu.roll(part, 32, 1))
            qk_ref[:, 128 * i : 128 * (i + 1)] = (part * cosine + turned * sine).astype(BF)
        values = dot_f(input1, attn_o_ref[:, :384]).astype(BF)
        v_ref[...] = values
        allowed = seg_ref[...] > 0.0
        att_ref[:, :384] = jnp.zeros((rows.shape[0], 384), BF)
        for k in range(KV):
            keys = qk_ref[:, D + HD * k : D + HD * (k + 1)]
            value = values[:, HD * k : HD * (k + 1)]
            for g in range(GROUP):
                h = GROUP * k + g
                queries = qk_ref[:, HD * h : HD * (h + 1)]
                scores = jnp.where(allowed, dot_t(queries, keys) * HD ** (-0.5), NEG)
                top = jnp.max(scores, axis=1, keepdims=True)
                expo = jnp.exp(scores - top)
                total = jnp.sum(expo, axis=1, keepdims=True)
                logsum_ref[:, h : h + 1] = top + jnp.log(total)
                weights = (expo / total).astype(BF)
                att_ref[:, kv_width + HD * h : kv_width + HD * (h + 1)] = dot_f(weights, value).astype(BF)
        hidden1 = rows + dot_t(att_ref[...], attn_o_ref[...])
        hidden1_ref[...] = hidden1
        normed2, _ = norm_rows(hidden1)
        input2_ref[...] = (normed2 * gain2).astype(BF)

    return kernel


def make_backward(n_fsdp, own, padded, share):
    kv_width = KV * HD

    def kernel(
        place_ref, grad_a_ref, grad_b_ref, grad_out_ref, hidden1_ref, rows_ref, gains_ref, owner_ref, inner_ref,
        spots_ref, cos_ref, sin_ref, seg_ref, input1_ref, qk_ref, v_ref, logsum_ref, att_ref,
        attn_q_ref, attn_o_ref,
        q_term_ref, o_term_ref, input_grad_ref,
        left_ref, right_ref, turn_ref,
    ):
        count = rows_ref.shape[0]
        wide = rows_ref.shape[1]
        gain1 = gains_ref[0:1, :]
        gain2 = gains_ref[1:2, :]
        grad_in2 = grad_a_ref[...].astype(F32) + grad_b_ref[...].astype(F32)
        normed2, scale2 = norm_rows(hidden1_ref[...])
        back2, gain2_term = norm_rows_back(grad_in2, normed2, scale2, gain2)
        grad_h1 = grad_out_ref[...].astype(F32) + back2
        grad_h1b = grad_h1.astype(BF)
        left_ref[:count, :] = input1_ref[...]
        left_ref[count:, :] = grad_h1b
        right_ref[:count, :] = jnp.zeros((count, right_ref.shape[1]), BF)
        right_ref[count:, :] = att_ref[...]
        grad_att = dot_f(grad_h1b, attn_o_ref[...]).astype(BF)
        allowed = seg_ref[...] > 0.0
        for k in range(KV):
            keys = qk_ref[:, D + HD * k : D + HD * (k + 1)]
            value = v_ref[:, HD * k : HD * (k + 1)]
            value_grad = jnp.zeros((count, HD), F32)
            key_grad = jnp.zeros((count, HD), F32)
            for g in range(GROUP):
                h = GROUP * k + g
                queries = qk_ref[:, HD * h : HD * (h + 1)]
                grad = grad_att[:, kv_width + HD * h : kv_width + HD * (h + 1)]
                scores = jnp.where(allowed, dot_t(queries, keys) * HD ** (-0.5), NEG)
                probs = jnp.exp(scores - logsum_ref[:, h : h + 1])
                value_grad = value_grad + dot_0(probs.astype(BF), grad)
                prob_grad = dot_t(grad, value)
                delta = jnp.sum(probs * prob_grad, axis=1, keepdims=True)
                score_grad = (probs * (prob_grad - delta) * HD ** (-0.5)).astype(BF)
                turn_ref[:, HD * h : HD * (h + 1)] = dot_f(score_grad, keys)
                key_grad = key_grad + dot_0(score_grad, queries)
            turn_ref[:, D + HD * k : D + HD * (k + 1)] = key_grad
            right_ref[:count, HD * k : HD * (k + 1)] = value_grad.astype(BF)
        cosine = cos_ref[...]
        sine = sin_ref[...]
        low = first_half(cosine.shape)
        pieces = []
        for i in range(turn_ref.shape[1] // 128):
            part = turn_ref[:, 128 * i : 128 * (i + 1)]
            scaled = part * sine
            turned = jnp.where(low, pltpu.roll(scaled, 96, 1), -pltpu.roll(scaled, 32, 1))
            pieces.append((part * cosine + turned).astype(BF))
        proj_grad = jnp.concatenate(pieces, axis=1)
        o_term_ref[...] = dot_0(left_ref[...], right_ref[...]).astype(BF)
        owner = owner_ref[...]
        inner = inner_ref[...]
        grad_in1 = dot_t(proj_grad, attn_q_ref[...]) * jnp.where(inner < own, 1.0, 0.0) + dot_t(
            right_ref[:count, :], attn_o_ref[...]
        )
        normed1, scale1 = norm_rows(rows_ref[...])
        back1, gain1_term = norm_rows_back(grad_in1, normed1, scale1, gain1)
        input_grad_ref[...] = grad_h1 + back1
        first, second = gain_masks(owner, place_ref[0], n_fsdp, own, share)
        both = jnp.where(first, gain1_term, 0.0) + jnp.where(second, gain2_term, 0.0)
        gain_rows = dot_t(both.astype(BF), slot_matrix(owner, inner, own, share)).astype(BF)
        q_term = dot_0(input1_ref[...], proj_grad)
        q_term_ref[...] = q_term.astype(BF)
        q_term_ref[:, :share] = (q_term[:, :share] + dot_f(spots_ref[...], gain_rows)).astype(BF)

    return kernel


VMEM = pl.BlockSpec(memory_space=pltpu.VMEM)
SMEM = pl.BlockSpec(memory_space=pltpu.SMEM)


def run_kernel(kernel, outs, args, scratch=(), name=None):
    return pl.pallas_call(
        kernel,
        out_shape=[jax.ShapeDtypeStruct(shape, kind) for shape, kind in outs],
        in_specs=[SMEM] + [VMEM] * (len(args) - 1),
        out_specs=[VMEM] * len(outs),
        scratch_shapes=scratch,
        compiler_params=pltpu.CompilerParams(vmem_limit_bytes=56 << 20),
        cost_estimate=pl.CostEstimate(flops=1000, transcendentals=0, bytes_accessed=1000),
        name=name,
    )(*args)


def body(rows, cotangent, lengths, gains, attn_weight, gate_weight, up_weight, down_weight):
    count = rows.shape[0]
    n_fsdp = lax.axis_size("fsdp")
    n_sub = lax.axis_size("sub")
    n_all = n_fsdp * n_sub
    n_far = n_fsdp // 2
    own = D // n_all
    padded = -(-(own + 1) // 16) * 16
    wide = n_all * padded
    half_ff = FF // 2
    quarter = FF // 4
    share = gains.shape[0]
    kv_width = KV * HD
    my_fsdp = lax.axis_index("fsdp")
    my_sub = lax.axis_index("sub")
    my_y = my_sub // 2
    my_c = my_sub % 2

    column = jnp.arange(wide, dtype=jnp.int32)
    place = column // padded
    inner = column % padded
    rel = (place // n_sub) % n_far * 2 + place // (n_sub * n_far)
    real = inner < own
    source = jnp.where(real, ((rel ^ my_fsdp) * n_sub + place % n_sub) * own + inner, -1)
    spread_mat = (jnp.arange(D, dtype=jnp.int32)[:, None] == source[None, :]).astype(BF)

    def padded_block(flat):
        return jnp.pad(flat.reshape(own, FF), ((0, padded - own), (0, 0)))

    def far_gather(block):
        return jnp.stack([block] + [swap(block, "fsdp", 2 * k) for k in range(1, n_far)], axis=0)

    def columns(value, index, width):
        return lax.dynamic_slice_in_dim(value, index * width, width, axis=value.ndim - 1)

    position, live, allowed = layout(lengths, count)
    cosine, sine = rope_tables(position, HD)
    cosine = jnp.concatenate([cosine, cosine], axis=1)
    sine = jnp.concatenate([sine, sine], axis=1)
    seg = allowed.astype(F32)
    rows32 = mm(rows, spread_mat)
    grad_outb = (live * mm(cotangent, spread_mat)).astype(BF)

    def group_tokens(value):
        value = jnp.stack([value, swap(value, "sub", 2)])
        return jnp.stack([value, swap(value, "sub", 1)]).reshape(4 * count, wide)

    def group_half(value):
        value = value.astype(BF).reshape(2, 2 * count, wide)
        value = add2(value[0], swap(value[1], "sub", 1)).reshape(2, count, wide)
        return value[0], swap(value[1], "sub", 2)

    attn_block = padded_block(attn_weight)
    attn_block = attn_block.at[own, :share].set(gains)
    attn_far = far_gather(attn_block)
    mlp_block = jnp.stack([padded_block(w) for w in (gate_weight, up_weight, down_weight)])
    came = swap(columns(mlp_block, 1 - my_y, half_ff), "sub", 2)
    mlp_block = put2(columns(mlp_block, my_y, half_ff), came, my_y, 1)
    came = swap(columns(mlp_block, 1 - my_c, quarter), "sub", 1)
    mlp_block = put2(columns(mlp_block, my_c, quarter), came, my_c, 2)
    mlp_block = mlp_block.reshape(3, n_sub * padded, quarter)
    cot_all = group_tokens(grad_outb)
    attn_far, mlp_block, cot_all = lax.optimization_barrier((attn_far, mlp_block, cot_all))

    half0 = attn_far[:, :, :half_ff]
    half1 = attn_far[:, :, half_ff:]
    gate_up = [mlp_block[:2]]
    half0 = jnp.stack([half0, swap(half0, "fsdp", 1)])
    half1 = put2(half1, swap(half1, "sub", 2), my_y, 1)
    gate_up.append(swap(mlp_block[:2], "fsdp", 2))
    half0, half1, gate_up = lax.optimization_barrier((half0, half1, gate_up))

    gate_up = gate_up + [swap(gate_up[0], "fsdp", 2 * k) for k in range(2, 3)]
    half0 = put2(half0, swap(half0, "sub", 2), my_y, 2)
    half1 = jnp.stack([half1, swap(half1, "fsdp", 1)])
    half0, half1, gate_up, down_w = lax.optimization_barrier((half0, half1, gate_up, mlp_block[2:]))

    attn_q = put2(half0, swap(half0, "sub", 1), my_c, 3).reshape(wide, half_ff)
    attn_o = put2(half1, swap(half1, "sub", 1), my_c, 3).reshape(wide, half_ff)
    gate_up = gate_up + [swap(gate_up[0], "fsdp", 2 * k) for k in range(3, n_far)]
    attn_q, attn_o, down_w = lax.optimization_barrier((attn_q, attn_o, down_w))
    gate_up = jnp.stack(gate_up)
    gate_up_came = swap(gate_up, "fsdp", 1)
    down_w = far_gather(down_w)

    by_fsdp = [(f % 2) * n_far * n_sub + (f // 2) * n_sub for f in range(n_fsdp)]
    pieces = attn_q.reshape(n_all, padded, half_ff)
    pieces = jnp.stack([pieces[p, own, :share] for p in by_fsdp])
    my_place = my_fsdp.reshape(1)
    owner = (((rel ^ my_fsdp) * n_sub + place % n_sub))[None, :]
    tables = (owner, inner[None, :])
    angles = (cosine, sine, seg)
    sizes = (n_fsdp, own, padded, share)
    tall = (count, wide)
    forward = run_kernel(
        make_forward(*sizes),
        [
            (tall, BF),
            ((count, half_ff), BF),
            ((count, 384), BF),
            ((count, KV * GROUP), F32),
            ((count, half_ff), BF),
            (tall, F32),
            (tall, BF),
            ((2, wide), F32),
        ],
        (my_place, rows32, pieces, *tables, *angles, attn_q, attn_o),
        name="attn_forward",
    )
    input1, qk, values, logsum, attended, hidden1, input2, gains_p = forward
    in2_all = group_tokens(input2)
    gate_up_came = after(gate_up_came, input2)
    gate_w = jnp.stack([gate_up[:, 0], gate_up_came[:, 0]]).reshape(wide, quarter)
    up_w = jnp.stack([gate_up[:, 1], gate_up_came[:, 1]]).reshape(wide, quarter)
    down_w = after(down_w, gate_up_came)
    down_came = swap(down_w, "fsdp", 1)
    gate = mm(in2_all, gate_w)
    up = mm(in2_all, up_w)
    sigma = jax.nn.sigmoid(gate)
    active = gate * sigma
    hidden = (active * up).astype(BF)
    down_came = after(down_came, hidden)
    down_w = jnp.stack([down_w, down_came]).reshape(wide, quarter)
    down_term = term(cot_all, hidden)
    grad_hidden = mm(cot_all, down_w)
    grad_gate = (grad_hidden * up * sigma * (1.0 + gate * (1.0 - sigma))).astype(BF)
    grad_up = (grad_hidden * active).astype(BF)
    grad_in2 = group_half(mm_t(grad_gate, gate_w) + mm_t(grad_up, up_w))
    gate_term = term(in2_all, grad_gate)
    up_term = term(in2_all, grad_up)
    result = group_half(after(mm_t(hidden, down_w), *grad_in2))
    of_place = [(p // n_sub) % n_far * 2 + p // (n_sub * n_far) for p in range(n_all)]
    at_spot = jnp.where(inner == own, jnp.array(of_place)[place], -1)
    spots = (at_spot[:, None] == jnp.arange(n_fsdp)[None, :]).astype(BF)
    q_term, o_term, input_grad = run_kernel(
        make_backward(*sizes),
        [((wide, half_ff), BF), ((wide, half_ff), BF), (tall, F32)],
        (
            my_place, *grad_in2, grad_outb, hidden1, rows32, gains_p, *tables, spots, *angles,
            input1, qk, values, logsum, attended, attn_q, attn_o,
        ),
        scratch=[
            pltpu.VMEM((2 * count, wide), BF),
            pltpu.VMEM((2 * count, half_ff), BF),
            pltpu.VMEM((count, half_ff), F32),
        ],
        name="attn_backward",
    )
    result = hidden1 + result[0].astype(F32) + result[1].astype(F32)
    output = mm_t((live * result).astype(BF), spread_mat).astype(BF)
    input_grad = lax.dot_general(
        input_grad,
        spread_mat.astype(F32),
        (((1,), (1,)), ((), ())),
        precision=lax.Precision.HIGHEST,
    )

    def far_sum(held, axis, *done):
        parts = [lax.index_in_dim(held, 0, axis, keepdims=False)]
        for k in range(1, n_far):
            parts.append(swap(lax.index_in_dim(held, k, axis, keepdims=False), "fsdp", 2 * k))
        parts = after(parts, *done)
        total = parts[0].astype(F32)
        for part in parts[1:]:
            total = total + part.astype(F32)
        return total.astype(BF)

    def sub_return(held):
        came = swap(pick(held, 1 - my_c, 2), "sub", 1)
        mine = pick(held, my_c, 2)
        first = my_c == 0
        held = jnp.concatenate(
            [jnp.where(first, mine, came), jnp.where(first, came, mine)], axis=-1
        )
        came = swap(pick(held, 1 - my_y, 1), "sub", 2)
        mine = pick(held, my_y, 1)
        first = my_y == 0
        return jnp.concatenate(
            [jnp.where(first, mine, came), jnp.where(first, came, mine)], axis=-1
        )

    def mlp_sum(terms, near_done, far_done):
        k = len(terms)
        held = jnp.stack(terms).reshape(k, 2, n_far, n_sub * padded, quarter)
        held = add2(held[:, 0], after(swap(held[:, 1], "fsdp", 1), *near_done))
        held = far_sum(held, 1, *far_done).reshape(k, 2, 2, padded, quarter)
        return sub_return(held)

    def core_sum(held):
        held = held.reshape(2, n_far, 2, 2, padded, half_ff)
        return add2(pick(held, my_c, 3), swap(pick(held, 1 - my_c, 3), "sub", 1))

    def x_sum(held):
        return add2(held[0], swap(held[1], "fsdp", 1))

    def y_sum(held, axis):
        return add2(pick(held, my_y, axis), swap(pick(held, 1 - my_y, axis), "sub", 2))

    o_held = x_sum(core_sum(o_term))
    q_held = y_sum(core_sum(q_term), 2)
    down_own = mlp_sum([down_term], grad_in2, [q_term])
    gate_up_own = mlp_sum([gate_term, up_term], [q_term], [o_held, q_held])
    o_own = far_sum(y_sum(o_held, 1), 0)
    q_own = far_sum(x_sum(q_held), 0)
    gain_grad = q_own[own, :share].astype(F32)
    attn_own = jnp.concatenate([q_own, o_own], axis=1)

    def flat(mine):
        return mine[:own].astype(F32).reshape(-1)

    return (
        output,
        input_grad,
        flat(attn_own),
        flat(gate_up_own[0]),
        flat(gate_up_own[1]),
        flat(down_own[0]),
        gain_grad,
    )


def solution(mesh):
    n_fsdp, n_sub = mesh.shape["fsdp"], mesh.shape["sub"]
    n_all = n_fsdp * n_sub
    by_rows = (
        n_fsdp == 8 and
        D % n_all == 0 and n_fsdp & (n_fsdp - 1) == 0 and n_fsdp > 1 and n_sub == 4 and D // n_fsdp % (D // n_all) == 0
    )
    in_specs = (
        P(("fsdp", "sub"), None),
        P(("fsdp", "sub"), None),
        P(("fsdp", "sub")),
        P("fsdp"),
        P(("fsdp", "sub")),
        P(("fsdp", "sub")),
        P(("fsdp", "sub")),
        P(("fsdp", "sub")),
    )
    out_specs = (
        P(("fsdp", "sub"), None),
        P(("fsdp", "sub"), None),
        P(("fsdp", "sub")),
        P(("fsdp", "sub")),
        P(("fsdp", "sub")),
        P(("fsdp", "sub")),
        P("fsdp"),
    )
    return jax.shard_map(body if by_rows else plain_body, mesh=mesh, in_specs=in_specs, out_specs=out_specs, check_vma=False)
```

```python
import jax
import jax.numpy as jnp
from jax import lax
from jax.experimental import pallas as pl
from jax.experimental.pallas import tpu as pltpu
from jax.sharding import PartitionSpec as P

D = 960
KV = 5
HD = 64
FF = 2560
GROUP = 3


EPS = 1e-05
THETA = 100000.0
NEG = -1e30
piece_width = 64


def rope_tables(position, width):
    half = jnp.arange(width // 2, dtype=jnp.float32)
    inverse = jnp.exp(-(2.0 * half / width) * jnp.log(jnp.float32(THETA)))
    angle = position.astype(jnp.float32)[:, None] * inverse[None, :]
    cosine = jnp.concatenate([jnp.cos(angle), jnp.cos(angle)], axis=1)
    sine = jnp.concatenate([jnp.sin(angle), jnp.sin(angle)], axis=1)
    return (cosine, sine)


def rotate(values, cosine, sine):
    half = values.shape[-1] // 2
    turned = jnp.concatenate([-values[..., half:], values[..., :half]], axis=-1)
    return values * cosine + turned * sine


def unrotate(grads, cosine, sine):
    half = grads.shape[-1] // 2
    scaled = grads * sine
    return grads * cosine + jnp.concatenate([scaled[..., half:], -scaled[..., :half]], axis=-1)


def norm_forward(values):
    scale = lax.rsqrt(jnp.mean(values * values, axis=1, keepdims=True) + EPS)
    return (values * scale, scale)


def norm_backward(grad_in, normed, scale, gain):
    gain_term = jnp.sum(grad_in * normed, axis=0)
    inner = grad_in * gain[None, :]
    back = scale * (inner - normed * jnp.mean(inner * normed, axis=1, keepdims=True))
    return (back, gain_term)


def layout(block_lengths, count):
    slots = jnp.arange(count, dtype=jnp.int32)
    first = block_lengths[0]
    second = block_lengths[1]
    segment = (slots >= first).astype(jnp.int32) + (slots >= first + second).astype(jnp.int32)
    position = (
        slots - first * (segment >= 1).astype(jnp.int32) - second * (segment >= 2).astype(jnp.int32)
    )
    live = (segment < 2).astype(jnp.float32)[:, None]
    allowed = (segment[:, None] == segment[None, :]) & (slots[None, :] <= slots[:, None])
    return (position, live, allowed)


def masked_scores(queries, keys, allowed):
    scores = jnp.einsum(
        "qkgd,jkd->kgqj", queries, keys, preferred_element_type=jnp.float32
    ) * HD ** (-0.5)
    return jnp.where(allowed[None, None], scores, NEG)


def attend(projected, cosine, sine, allowed, count):
    kv_width = KV * HD
    queries = rotate(
        projected[:, :D].reshape(count, KV, GROUP, HD),
        cosine[:, None, None, :],
        sine[:, None, None, :],
    ).astype(jnp.bfloat16)
    keys = rotate(
        projected[:, D : D + kv_width].reshape(count, KV, HD), cosine[:, None, :], sine[:, None, :]
    ).astype(jnp.bfloat16)
    values = projected[:, D + kv_width :].reshape(count, KV, HD).astype(jnp.bfloat16)
    scores = masked_scores(queries, keys, allowed)
    top = jnp.max(scores, axis=-1, keepdims=True)
    expo = jnp.exp(scores - top)
    total = jnp.sum(expo, axis=-1, keepdims=True)
    logsum = top + jnp.log(total)
    weights = (expo / total).astype(jnp.bfloat16)
    attended = (
        jnp.einsum("kgqj,jkd->qkgd", weights, values, preferred_element_type=jnp.float32)
        .reshape(count, D)
        .astype(jnp.bfloat16)
    )
    return (queries, keys, values, logsum, attended)


def attend_back(grad_att, queries, keys, values, logsum, allowed, cosine, sine, count):
    kv_width = KV * HD
    probs = jnp.exp(masked_scores(queries, keys, allowed) - logsum)
    probs_b = probs.astype(jnp.bfloat16)
    value_grad = jnp.einsum("kgqj,qkgd->jkd", probs_b, grad_att, preferred_element_type=jnp.float32)
    prob_grad = jnp.einsum("qkgd,jkd->kgqj", grad_att, values, preferred_element_type=jnp.float32)
    delta = jnp.sum(probs * prob_grad, axis=-1, keepdims=True)
    score_grad = (probs * (prob_grad - delta) * HD ** (-0.5)).astype(jnp.bfloat16)
    query_grad = jnp.einsum("kgqj,jkd->qkgd", score_grad, keys, preferred_element_type=jnp.float32)
    key_grad = jnp.einsum("kgqj,qkgd->jkd", score_grad, queries, preferred_element_type=jnp.float32)
    query_grad = unrotate(query_grad, cosine[:, None, None, :], sine[:, None, None, :])
    key_grad = unrotate(key_grad, cosine[:, None, :], sine[:, None, :])
    return jnp.concatenate(
        [
            query_grad.reshape(count, D),
            key_grad.reshape(count, kv_width),
            value_grad.reshape(count, kv_width),
        ],
        axis=1,
    ).astype(jnp.bfloat16)


def collect(attn_flat, gate_flat, up_flat, down_flat):
    whole = (
        lax.all_gather(attn_flat, ("fsdp", "sub"), axis=0, tiled=True),
        lax.all_gather(gate_flat, ("fsdp", "sub"), axis=0, tiled=True),
        lax.all_gather(up_flat, ("fsdp", "sub"), axis=0, tiled=True),
        lax.all_gather(down_flat, ("fsdp", "sub"), axis=0, tiled=True),
    )
    return tuple((piece.reshape(D, FF) for piece in whole))


def flat_terms(pair_lists, count):
    results = []
    for pairs in pair_lists:
        blocks = [
            jnp.dot(left.T, right, preferred_element_type=jnp.float32) for left, right in pairs
        ]
        joined = blocks[0] if len(blocks) == 1 else jnp.concatenate(blocks, axis=1)
        results.append(joined.reshape(-1).reshape(count, piece_width))
    return jnp.concatenate(results, axis=1)


def split_owned(owned):
    return tuple(
        (
            owned[:, index * piece_width : (index + 1) * piece_width].reshape(-1)
            for index in range(4)
        )
    )


def spread(pair_lists):
    share = D * FF // (piece_width * lax.axis_size("fsdp") * lax.axis_size("sub"))
    owned = lax.psum_scatter(
        flat_terms(pair_lists, share * lax.axis_size(("fsdp", "sub"))),
        ("fsdp", "sub"),
        scatter_dimension=0,
        tiled=True,
    )
    return split_owned(owned)


def flat_path(
    rows32,
    cotangent,
    live,
    allowed,
    cosine,
    sine,
    gain_attn,
    gain_mlp,
    normed1,
    scale1,
    input1,
    flats,
):
    count = rows32.shape[0]
    q_width = D + 2 * KV * HD
    attn_mat, gate_mat, up_mat, down_mat = collect(flats[0], flats[1], flats[2], flats[3])
    projected = jnp.dot(input1, attn_mat[:, :q_width], preferred_element_type=jnp.float32)
    queries, keys, values, logsum, attended = attend(projected, cosine, sine, allowed, count)
    hidden1 = rows32 + jnp.dot(
        attended, attn_mat[:, q_width:].T, preferred_element_type=jnp.float32
    )
    normed2, scale2 = norm_forward(hidden1)
    input2 = (normed2 * gain_mlp[None, :]).astype(jnp.bfloat16)
    gate = jnp.dot(input2, gate_mat, preferred_element_type=jnp.float32)
    up = jnp.dot(input2, up_mat, preferred_element_type=jnp.float32)
    sigma = jax.nn.sigmoid(gate)
    active = gate * sigma
    hidden = (active * up).astype(jnp.bfloat16)
    result = hidden1 + jnp.dot(hidden, down_mat.T, preferred_element_type=jnp.float32)
    output = (live * result).astype(jnp.bfloat16)
    attn_back, gate_back, up_back, down_back = collect(flats[0], flats[1], flats[2], flats[3])
    grad_out = live * cotangent.astype(jnp.float32)
    grad_outb = grad_out.astype(jnp.bfloat16)
    grad_hidden = jnp.dot(grad_outb, down_back, preferred_element_type=jnp.float32)
    grad_gate = (grad_hidden * up * sigma * (1.0 + gate * (1.0 - sigma))).astype(jnp.bfloat16)
    grad_up = (grad_hidden * active).astype(jnp.bfloat16)
    grad_in2 = jnp.dot(grad_gate, gate_back.T, preferred_element_type=jnp.float32) + jnp.dot(
        grad_up, up_back.T, preferred_element_type=jnp.float32
    )
    back2, gain2_term = norm_backward(grad_in2, normed2, scale2, gain_mlp)
    grad_h1 = grad_out + back2
    grad_h1b = grad_h1.astype(jnp.bfloat16)
    grad_att = (
        jnp.dot(grad_h1b, attn_back[:, q_width:], preferred_element_type=jnp.float32)
        .astype(jnp.bfloat16)
        .reshape(count, KV, GROUP, HD)
    )
    proj_grad = attend_back(grad_att, queries, keys, values, logsum, allowed, cosine, sine, count)
    grad_in1 = jnp.dot(proj_grad, attn_back[:, :q_width].T, preferred_element_type=jnp.float32)
    back1, gain1_term = norm_backward(grad_in1, normed1, scale1, gain_attn)
    input_grad = grad_h1 + back1
    pair_lists = (
        ((input1, proj_grad), (grad_h1b, attended)),
        ((input2, grad_gate),),
        ((input2, grad_up),),
        ((grad_outb, hidden),),
    )
    owned = spread(pair_lists)
    return (output, input_grad, owned, gain1_term, gain2_term)


def plain_body(rows, cotangent, lengths, gains, attn_weight, gate_weight, up_weight, down_weight):
    count = rows.shape[0]
    position, live, allowed = layout(lengths, count)
    cosine, sine = rope_tables(position, HD)
    full_gains = lax.all_gather(gains, "fsdp", axis=0, tiled=True).astype(jnp.float32)
    gain_attn = full_gains[:D]
    gain_mlp = full_gains[D:]
    rows32 = rows.astype(jnp.float32)
    normed1, scale1 = norm_forward(rows32)
    input1 = (normed1 * gain_attn[None, :]).astype(jnp.bfloat16)
    flats = (attn_weight, gate_weight, up_weight, down_weight)
    output, input_grad, owned, gain1_term, gain2_term = flat_path(
        rows32,
        cotangent,
        live,
        allowed,
        cosine,
        sine,
        gain_attn,
        gain_mlp,
        normed1,
        scale1,
        input1,
        flats,
    )
    gain_total = lax.psum(jnp.concatenate([gain1_term, gain2_term]), ("fsdp", "sub"))
    share = gains.shape[0]
    gain_grad = lax.dynamic_slice_in_dim(gain_total, lax.axis_index("fsdp") * share, share)
    return (output, input_grad, owned[0], owned[1], owned[2], owned[3], gain_grad)


BF = jnp.bfloat16
F32 = jnp.float32


def swap(value, axis, bit):
    return lax.ppermute(value, axis, [(i, i ^ bit) for i in range(lax.axis_size(axis))])


def meet(*values):
    return lax.optimization_barrier(values)


def after(value, *done):
    return lax.optimization_barrier((value, *done))[0]


def add2(kept, came):
    return (kept.astype(F32) + came.astype(F32)).astype(BF)


def far_pair(value, axis, odd):
    shape = value.shape
    value = value.reshape(shape[:axis] + (shape[axis] // 2, 2) + shape[axis + 1 :])
    return lax.index_in_dim(value, odd, axis + 1, keepdims=False)


def pick(value, index, axis):
    return lax.dynamic_index_in_dim(value, index, axis, keepdims=False)


def put2(own, came, bit, axis):
    first = bit == 0
    return jnp.stack([jnp.where(first, own, came), jnp.where(first, came, own)], axis=axis)


def mm(a, b):
    return jnp.dot(a, b, preferred_element_type=F32)


def mm_t(a, b):
    return lax.dot_general(a, b, (((1,), (1,)), ((), ())), preferred_element_type=F32)


def term(a, b):
    return lax.dot_general(a, b, (((0,), (0,)), ((), ())), preferred_element_type=F32).astype(BF)


def dot_f(a, b):
    return lax.dot_general(a, b, (((1,), (0,)), ((), ())), preferred_element_type=F32)


def dot_t(a, b):
    return lax.dot_general(a, b, (((1,), (1,)), ((), ())), preferred_element_type=F32)


def dot_0(a, b):
    return lax.dot_general(a, b, (((0,), (0,)), ((), ())), preferred_element_type=F32)


def norm_rows(values):
    mean = jnp.sum(values * values, axis=1, keepdims=True) * (1.0 / D)
    scale = lax.rsqrt(mean + EPS)
    return values * scale, scale


def norm_rows_back(grad_in, normed, scale, gain):
    gain_term = jnp.sum(grad_in * normed, axis=0, keepdims=True)
    inner = grad_in * gain
    mean = jnp.sum(inner * normed, axis=1, keepdims=True) * (1.0 / D)
    return scale * (inner - normed * mean), gain_term


def first_half(shape):
    return lax.broadcasted_iota(jnp.int32, shape, 1) % HD < HD // 2


def gain_masks(owner, my_fsdp, n_fsdp, own, share):
    wide = owner.shape[1]
    per = share // own
    place = lax.broadcasted_iota(jnp.int32, (n_fsdp, wide), 0) ^ my_fsdp
    group = owner // per
    return place == group, place == group + n_fsdp // 2


def slot_matrix(owner, inner, own, height):
    per = D * 2 // 8 // own
    slot = jnp.where(inner < own, owner % per * own + inner, -1)
    return (lax.broadcasted_iota(jnp.int32, (height, owner.shape[1]), 0) == slot).astype(F32).astype(BF)


def make_forward(n_fsdp, own, padded, share, by_fsdp):
    kv_width = KV * HD

    def kernel(
        place_ref, rows_ref, owner_ref, inner_ref, cos_ref, sin_ref, seg_ref,
        own_q_ref, came_q_ref, own_o_ref, came_o_ref,
        input1_ref, qk_ref, v_ref, logsum_ref, att_ref, hidden1_ref, input2_ref, gains_ref, attn_q_ref, attn_o_ref,
    ):
        core = place_ref[1]
        for p in range(own_q_ref.shape[0] // padded):
            here = pl.ds(pl.multiple_of((2 * p + core) * padded, padded), padded)
            there = pl.ds(pl.multiple_of((2 * p + 1 - core) * padded, padded), padded)
            block = slice(p * padded, (p + 1) * padded)
            attn_q_ref[here, :] = own_q_ref[block, :]
            attn_q_ref[there, :] = came_q_ref[block, :]
            attn_o_ref[here, :] = own_o_ref[block, :]
            attn_o_ref[there, :] = came_o_ref[block, :]
        pieces = jnp.concatenate(
            [attn_q_ref[p * padded + own : p * padded + own + 1, :share].astype(F32) for p in by_fsdp], axis=0
        ).astype(BF)
        owner = owner_ref[...]
        first, second = gain_masks(owner, place_ref[0], n_fsdp, own, share)
        spots = dot_f(pieces, slot_matrix(owner, inner_ref[...], own, share))
        gain1 = jnp.sum(jnp.where(first, spots, 0.0), axis=0, keepdims=True)
        gain2 = jnp.sum(jnp.where(second, spots, 0.0), axis=0, keepdims=True)
        gains_ref[0:1, :] = gain1
        gains_ref[1:2, :] = gain2
        rows = rows_ref[...]
        normed, _ = norm_rows(rows)
        input1 = (normed * gain1).astype(BF)
        input1_ref[...] = input1
        projected = dot_f(input1, attn_q_ref[...])
        cosine = cos_ref[...]
        sine = sin_ref[...]
        low = first_half(cosine.shape)
        for i in range(projected.shape[1] // 128):
            part = projected[:, 128 * i : 128 * (i + 1)]
            turned = jnp.where(low, -pltpu.roll(part, 96, 1), pltpu.roll(part, 32, 1))
            qk_ref[:, 128 * i : 128 * (i + 1)] = (part * cosine + turned * sine).astype(BF)
        values = dot_f(input1, attn_o_ref[:, :384]).astype(BF)
        v_ref[...] = values
        allowed = seg_ref[...] > 0.0
        att_ref[:, :384] = jnp.zeros((rows.shape[0], 384), BF)
        for k in range(KV):
            keys = qk_ref[:, D + HD * k : D + HD * (k + 1)]
            value = values[:, HD * k : HD * (k + 1)]
            for g in range(GROUP):
                h = GROUP * k + g
                queries = qk_ref[:, HD * h : HD * (h + 1)]
                scores = jnp.where(allowed, dot_t(queries, keys) * HD ** (-0.5), NEG)
                top = jnp.max(scores, axis=1, keepdims=True)
                expo = jnp.exp(scores - top)
                total = jnp.sum(expo, axis=1, keepdims=True)
                logsum_ref[:, h : h + 1] = top + jnp.log(total)
                weights = (expo / total).astype(BF)
                att_ref[:, kv_width + HD * h : kv_width + HD * (h + 1)] = dot_f(weights, value).astype(BF)
        hidden1 = rows + dot_t(att_ref[...], attn_o_ref[...])
        hidden1_ref[...] = hidden1
        normed2, _ = norm_rows(hidden1)
        input2_ref[...] = (normed2 * gain2).astype(BF)

    return kernel


def make_backward(n_fsdp, own, padded, share):
    kv_width = KV * HD

    def kernel(
        place_ref, grad_a_ref, grad_b_ref, grad_out_ref, hidden1_ref, rows_ref, gains_ref, owner_ref, inner_ref,
        spots_ref, cos_ref, sin_ref, seg_ref, input1_ref, qk_ref, v_ref, logsum_ref, att_ref,
        attn_q_ref, attn_o_ref,
        q_term_ref, o_term_ref, input_grad_ref,
        left_ref, right_ref, turn_ref,
    ):
        count = rows_ref.shape[0]
        wide = rows_ref.shape[1]
        core = place_ref[1]
        gain1 = gains_ref[0:1, :]
        gain2 = gains_ref[1:2, :]
        grad_in2 = grad_a_ref[...].astype(F32) + grad_b_ref[...].astype(F32)
        normed2, scale2 = norm_rows(hidden1_ref[...])
        back2, gain2_term = norm_rows_back(grad_in2, normed2, scale2, gain2)
        grad_h1 = grad_out_ref[...].astype(F32) + back2
        grad_h1b = grad_h1.astype(BF)
        left_ref[:count, :] = input1_ref[...]
        left_ref[count:, :] = grad_h1b
        right_ref[:count, :] = jnp.zeros((count, right_ref.shape[1]), BF)
        right_ref[count:, :] = att_ref[...]
        grad_att = dot_f(grad_h1b, attn_o_ref[...]).astype(BF)
        allowed = seg_ref[...] > 0.0
        for k in range(KV):
            keys = qk_ref[:, D + HD * k : D + HD * (k + 1)]
            value = v_ref[:, HD * k : HD * (k + 1)]
            value_grad = jnp.zeros((count, HD), F32)
            key_grad = jnp.zeros((count, HD), F32)
            for g in range(GROUP):
                h = GROUP * k + g
                queries = qk_ref[:, HD * h : HD * (h + 1)]
                grad = grad_att[:, kv_width + HD * h : kv_width + HD * (h + 1)]
                scores = jnp.where(allowed, dot_t(queries, keys) * HD ** (-0.5), NEG)
                probs = jnp.exp(scores - logsum_ref[:, h : h + 1])
                value_grad = value_grad + dot_0(probs.astype(BF), grad)
                prob_grad = dot_t(grad, value)
                delta = jnp.sum(probs * prob_grad, axis=1, keepdims=True)
                score_grad = (probs * (prob_grad - delta) * HD ** (-0.5)).astype(BF)
                turn_ref[:, HD * h : HD * (h + 1)] = dot_f(score_grad, keys)
                key_grad = key_grad + dot_0(score_grad, queries)
            turn_ref[:, D + HD * k : D + HD * (k + 1)] = key_grad
            right_ref[:count, HD * k : HD * (k + 1)] = value_grad.astype(BF)
        cosine = cos_ref[...]
        sine = sin_ref[...]
        low = first_half(cosine.shape)
        pieces = []
        for i in range(turn_ref.shape[1] // 128):
            part = turn_ref[:, 128 * i : 128 * (i + 1)]
            scaled = part * sine
            turned = jnp.where(low, pltpu.roll(scaled, 96, 1), -pltpu.roll(scaled, 32, 1))
            pieces.append((part * cosine + turned).astype(BF))
        proj_grad = jnp.concatenate(pieces, axis=1)
        o_term = dot_0(left_ref[...], right_ref[...]).astype(BF)
        owner = owner_ref[...]
        inner = inner_ref[...]
        grad_in1 = dot_t(proj_grad, attn_q_ref[...]) * jnp.where(inner < own, 1.0, 0.0) + dot_t(
            right_ref[:count, :], attn_o_ref[...]
        )
        normed1, scale1 = norm_rows(rows_ref[...])
        back1, gain1_term = norm_rows_back(grad_in1, normed1, scale1, gain1)
        input_grad_ref[...] = grad_h1 + back1
        first, second = gain_masks(owner, place_ref[0], n_fsdp, own, share)
        both = jnp.where(first, gain1_term, 0.0) + jnp.where(second, gain2_term, 0.0)
        gain_rows = dot_t(both.astype(BF), slot_matrix(owner, inner, own, 256)).astype(BF)
        q_term = dot_0(input1_ref[...], proj_grad)
        q_start = (q_term[:, :256] + dot_f(spots_ref[...], gain_rows)).astype(BF)
        q_term = q_term.astype(BF)
        for p in range(wide // padded):
            rel = p % 2 ^ core
            block = slice(p * padded, (p + 1) * padded)
            to = slice(p // 2 * padded, (p // 2 + 1) * padded)
            q_term_ref[rel, to, :256] = q_start[block, :]
            q_term_ref[rel, to, 256:] = q_term[block, 256:]
            o_term_ref[rel, to, :] = o_term[block, :]

    return kernel


VMEM = pl.BlockSpec(memory_space=pltpu.VMEM)
SMEM = pl.BlockSpec(memory_space=pltpu.SMEM)


def run_kernel(kernel, outs, args, scratch=(), name=None):
    return pl.pallas_call(
        kernel,
        out_shape=[jax.ShapeDtypeStruct(shape, kind) for shape, kind in outs],
        in_specs=[SMEM] + [VMEM] * (len(args) - 1),
        out_specs=[VMEM] * len(outs),
        scratch_shapes=scratch,
        compiler_params=pltpu.CompilerParams(vmem_limit_bytes=56 << 20),
        cost_estimate=pl.CostEstimate(flops=1000, transcendentals=0, bytes_accessed=1000),
        name=name,
    )(*args)


def body(rows, cotangent, lengths, gains, attn_weight, gate_weight, up_weight, down_weight):
    count = rows.shape[0]
    n_fsdp = lax.axis_size("fsdp")
    n_sub = lax.axis_size("sub")
    n_all = n_fsdp * n_sub
    n_far = n_fsdp // 2
    own = D // n_all
    padded = -(-(own + 1) // 16) * 16
    wide = n_all * padded
    half_ff = FF // 2
    quarter = FF // 4
    share = gains.shape[0]
    kv_width = KV * HD
    my_fsdp = lax.axis_index("fsdp")
    my_sub = lax.axis_index("sub")
    my_y = my_sub // 2
    my_c = my_sub % 2

    column = jnp.arange(wide, dtype=jnp.int32)
    place = column // padded
    inner = column % padded
    rel = (place // n_sub) % n_far * 2 + place // (n_sub * n_far)
    real = inner < own
    source = jnp.where(real, ((rel ^ my_fsdp) * n_sub + place % n_sub) * own + inner, -1)
    spread_mat = (jnp.arange(D, dtype=jnp.int32)[:, None] == source[None, :]).astype(BF)

    def padded_block(flat):
        return jnp.pad(flat.reshape(own, FF), ((0, padded - own), (0, 0)))

    def columns(value, index, width):
        return lax.dynamic_slice_in_dim(value, index * width, width, axis=value.ndim - 1)

    position, live, allowed = layout(lengths, count)
    cosine, sine = rope_tables(position, HD)
    cosine = jnp.concatenate([cosine, cosine], axis=1)
    sine = jnp.concatenate([sine, sine], axis=1)
    seg = allowed.astype(F32)
    rows32 = mm(rows, spread_mat)
    grad_outb = (live * mm(cotangent, spread_mat)).astype(BF)

    of_place = [(p // n_sub) % n_far * 2 + p // (n_sub * n_far) for p in range(n_all)]
    at_spot = jnp.where(inner == own, jnp.array(of_place)[place], -1)
    spots = (at_spot[:, None] == jnp.arange(n_fsdp)[None, :]).astype(BF)
    owner = ((rel ^ my_fsdp) * n_sub + place % n_sub)[None, :]

    attn_block = padded_block(attn_weight)
    attn_block = attn_block.at[own, :share].set(gains)
    far = [swap(attn_block, "fsdp", 2 * k) for k in range(1, n_far)]
    mlp_block = jnp.stack([padded_block(w) for w in (gate_weight, up_weight, down_weight)])
    came = swap(columns(mlp_block, 1 - my_y, half_ff), "sub", 2)
    mlp_block = put2(columns(mlp_block, my_y, half_ff), came, my_y, 1)
    came = swap(columns(mlp_block, 1 - my_c, quarter), "sub", 1)
    mlp_block = put2(columns(mlp_block, my_c, quarter), came, my_c, 2)
    mlp_block = mlp_block.reshape(3, n_sub * padded, quarter)
    far, mlp_block = meet(far, mlp_block)

    attn_far = jnp.stack([attn_block] + list(far))
    half0 = attn_far[:, :, :half_ff]
    half1 = attn_far[:, :, half_ff:]
    gate_up = mlp_block[:2]
    down = mlp_block[2]
    x0, y1, near = swap(half0, "fsdp", 1), swap(half1, "sub", 2), swap(gate_up, "fsdp", 2)
    tables = (owner, inner[None, :])
    angles = (cosine, sine, seg)
    half0, half1, gate_up, down, x0, y1, near, rows32, grad_outb, spots, tables, angles = meet(
        half0, half1, gate_up, down, x0, y1, near, rows32, grad_outb, spots, tables, angles
    )

    half0 = jnp.stack([half0, x0])
    half1 = put2(half1, y1, my_y, 1)
    y0, x1, third = swap(half0, "sub", 2), swap(half1, "fsdp", 1), swap(gate_up, "fsdp", 4)
    half0, half1, gate_up, down, near, y0, x1, third, grad_outb = meet(
        half0, half1, gate_up, down, near, y0, x1, third, grad_outb
    )

    half0 = put2(half0, y0, my_y, 2).reshape(wide // 2, half_ff)
    half1 = jnp.stack([half1, x1]).reshape(wide // 2, half_ff)
    c0, c1, last = swap(half0, "sub", 1), swap(half1, "sub", 1), swap(third, "fsdp", 2)
    down_x = swap(down, "fsdp", 1)
    cot_y = swap(grad_outb, "sub", 2)
    half0, half1, c0, c1, gate_up, near, third, last, down, down_x, cot_y = meet(
        half0, half1, c0, c1, gate_up, near, third, last, down, down_x, cot_y
    )

    gate_up = jnp.stack([gate_up, near, third, last])
    gate_up_x = swap(gate_up, "fsdp", 1)
    down = jnp.stack([down, down_x])
    down_far = swap(down, "fsdp", 4)
    by_fsdp = [(f % 2) * n_far * n_sub + (f // 2) * n_sub for f in range(n_fsdp)]
    my_place = jnp.stack([my_fsdp, my_c])
    tall = (count, wide)
    forward = run_kernel(
        make_forward(n_fsdp, own, padded, share, by_fsdp),
        [
            (tall, BF),
            ((count, half_ff), BF),
            ((count, 384), BF),
            ((count, KV * GROUP), F32),
            ((count, half_ff), BF),
            (tall, F32),
            (tall, BF),
            ((2, wide), F32),
            ((wide, half_ff), BF),
            ((wide, half_ff), BF),
        ],
        (my_place, rows32, *tables, *angles, half0, c0, half1, c1),
        name="attn_forward",
    )
    input1, qk, values, logsum, attended, hidden1, input2, gains_p, attn_q, attn_o = forward

    in2_y = swap(input2, "sub", 2)
    input2, in2_y, down_far, cot_y = meet(input2, in2_y, down_far, cot_y)
    down = jnp.stack([down, down_far])
    down_near = swap(down, "fsdp", 2)
    in2_all = jnp.stack([input2, in2_y])
    cot_all = jnp.stack([grad_outb, cot_y])
    in2_c, cot_c = swap(in2_all, "sub", 1), swap(cot_all, "sub", 1)
    in2_c, cot_c, gate_up_x = meet(in2_c, cot_c, gate_up_x)
    in2_all = jnp.stack([in2_all, in2_c]).reshape(4 * count, wide)
    cot_all = jnp.stack([cot_all, cot_c]).reshape(4 * count, wide)
    gate_w = jnp.stack([gate_up[:, 0], gate_up_x[:, 0]]).reshape(wide, quarter)
    up_w = jnp.stack([gate_up[:, 1], gate_up_x[:, 1]]).reshape(wide, quarter)
    gate = mm(in2_all, gate_w)
    up = mm(in2_all, up_w)
    sigma = jax.nn.sigmoid(gate)
    active = gate * sigma
    hidden = (active * up).astype(BF)
    down_term = term(cot_all, hidden)
    down_near = after(down_near, hidden)
    down_w = jnp.stack([down, down_near])
    down_w = down_w.transpose(2, 1, 0, 3, 4).reshape(wide, quarter)
    down_term = down_term.reshape(2, n_far, n_sub * padded, quarter)
    down_x_came = swap(down_term[1], "fsdp", 1)
    grad_hidden = mm(cot_all, down_w)
    grad_gate = (grad_hidden * up * sigma * (1.0 + gate * (1.0 - sigma))).astype(BF)
    grad_up = (grad_hidden * active).astype(BF)
    grad_in2 = (mm_t(grad_gate, gate_w) + mm_t(grad_up, up_w)).astype(BF).reshape(2, 2 * count, wide)
    gate_up_term = jnp.stack([term(in2_all, grad_gate), term(in2_all, grad_up)])
    gate_up_term = gate_up_term.reshape(2, 2, n_far, n_sub * padded, quarter)
    result = mm_t(hidden, down_w).astype(BF).reshape(2, 2 * count, wide)

    came = swap(grad_in2[1], "sub", 1)
    came, down_x_came = meet(came, down_x_came)
    grad_in2 = add2(grad_in2[0], came).reshape(2, count, wide)
    grad_in2_y = swap(grad_in2[1], "sub", 2)
    gate_up_x_came = swap(gate_up_term[:, 1], "fsdp", 1)
    down_held = add2(down_term[0], down_x_came)
    down_near_came = swap(far_pair(down_held, 0, 1), "fsdp", 2)
    q_term, o_term, input_grad = run_kernel(
        make_backward(n_fsdp, own, padded, share),
        [((2, wide // 2, half_ff), BF), ((2, wide // 2, half_ff), BF), (tall, F32)],
        (
            my_place, grad_in2[0], grad_in2_y, grad_outb, hidden1, rows32, gains_p, *tables, spots, *angles,
            input1, qk, values, logsum, attended, attn_q, attn_o,
        ),
        scratch=[
            pltpu.VMEM((2 * count, wide), BF),
            pltpu.VMEM((2 * count, half_ff), BF),
            pltpu.VMEM((count, half_ff), F32),
        ],
        name="attn_backward",
    )

    q_c, o_c = swap(q_term[1], "sub", 1), swap(o_term[1], "sub", 1)
    res_c = swap(after(result[1], q_term), "sub", 1)
    q_c, o_c, res_c, down_near_came, gate_up_x_came = meet(q_c, o_c, res_c, down_near_came, gate_up_x_came)

    full = (2, n_far, 2, padded, half_ff)
    q_held = add2(q_term[0], q_c).reshape(full)
    o_held = add2(o_term[0], o_c).reshape(full)
    q_y = swap(pick(q_held, 1 - my_y, 2), "sub", 2)
    o_x = swap(o_held[1], "fsdp", 1)
    gate_up_held = add2(gate_up_term[:, 0], gate_up_x_came)
    gate_up_near = swap(far_pair(gate_up_held, 1, 1), "fsdp", 2)
    down_held = add2(far_pair(down_held, 0, 0), down_near_came)
    input_grad = after(input_grad, q_c)
    input_grad = lax.dot_general(
        input_grad,
        spread_mat.astype(F32),
        (((1,), (1,)), ((), ())),
        precision=lax.Precision.HIGHEST,
    )
    q_y, o_x, gate_up_near, input_grad, down_held = meet(q_y, o_x, gate_up_near, input_grad, down_held)

    q_held = add2(pick(q_held, my_y, 2), q_y)
    o_held = add2(o_held[0], o_x)
    q_x = swap(q_held[1], "fsdp", 1)
    o_y = swap(pick(o_held, 1 - my_y, 1), "sub", 2)
    down_far_came = swap(down_held[1], "fsdp", 4)
    gate_up_held = add2(far_pair(gate_up_held, 1, 0), gate_up_near)
    q_x, o_y, down_far_came = meet(q_x, o_y, down_far_came)

    q_held = add2(q_held[0], q_x)
    o_held = add2(pick(o_held, my_y, 1), o_y)
    attn_held = jnp.concatenate([q_held, o_held], axis=-1)
    attn_near = swap(far_pair(attn_held, 0, 1), "fsdp", 2)
    gate_up_far = swap(gate_up_held[:, 1], "fsdp", 4)
    result = add2(result[0], res_c).reshape(2, count, wide)
    res_y = swap(result[1], "sub", 2)
    attn_near, res_y = meet(attn_near, res_y)
    attn_held = add2(far_pair(attn_held, 0, 0), attn_near)
    attn_far = swap(attn_held[1], "fsdp", 4)
    result = hidden1 + result[0].astype(F32) + res_y.astype(F32)
    output = mm_t((live * result).astype(BF), spread_mat).astype(BF)
    down_own = add2(down_held[0], down_far_came)[None]
    mlp_own = jnp.concatenate([add2(gate_up_held[:, 0], gate_up_far), down_own])
    mlp_own = mlp_own.reshape(3, 2, 2, padded, quarter)

    def sub_return(held):
        came = swap(pick(held, 1 - my_c, 2), "sub", 1)
        mine = pick(held, my_c, 2)
        first = my_c == 0
        held = jnp.concatenate(
            [jnp.where(first, mine, came), jnp.where(first, came, mine)], axis=-1
        )
        came = swap(pick(held, 1 - my_y, 1), "sub", 2)
        mine = pick(held, my_y, 1)
        first = my_y == 0
        return jnp.concatenate(
            [jnp.where(first, mine, came), jnp.where(first, came, mine)], axis=-1
        )

    mlp_own = sub_return(mlp_own)
    attn_own = add2(attn_held[0], attn_far)
    gain_grad = attn_own[own, :share].astype(F32)

    def flat(mine):
        return mine[:own].astype(F32).reshape(-1)

    return (
        output,
        input_grad,
        flat(attn_own),
        flat(mlp_own[0]),
        flat(mlp_own[1]),
        flat(mlp_own[2]),
        gain_grad,
    )


def solution(mesh):
    n_fsdp, n_sub = mesh.shape["fsdp"], mesh.shape["sub"]
    n_all = n_fsdp * n_sub
    by_rows = (
        n_fsdp == 8 and D % n_all == 0 and n_fsdp & (n_fsdp - 1) == 0 and n_fsdp > 1 and n_sub == 4 and D // n_fsdp % (D // n_all) == 0
    )
    in_specs = (
        P(("fsdp", "sub"), None),
        P(("fsdp", "sub"), None),
        P(("fsdp", "sub")),
        P("fsdp"),
        P(("fsdp", "sub")),
        P(("fsdp", "sub")),
        P(("fsdp", "sub")),
        P(("fsdp", "sub")),
    )
    out_specs = (
        P(("fsdp", "sub"), None),
        P(("fsdp", "sub"), None),
        P(("fsdp", "sub")),
        P(("fsdp", "sub")),
        P(("fsdp", "sub")),
        P(("fsdp", "sub")),
        P("fsdp"),
    )
    return jax.shard_map(body if by_rows else plain_body, mesh=mesh, in_specs=in_specs, out_specs=out_specs, check_vma=False)
```

```python
import jax
import jax.numpy as jnp
from jax import lax
from jax.experimental import pallas as pl
from jax.experimental.pallas import tpu as pltpu
from jax.sharding import PartitionSpec as P

D = 960
KV = 5
HD = 64
FF = 2560
GROUP = 3


EPS = 1e-05
THETA = 100000.0
NEG = -1e30
piece_width = 64


def rope_tables(position, width):
    half = jnp.arange(width // 2, dtype=jnp.float32)
    inverse = jnp.exp(-(2.0 * half / width) * jnp.log(jnp.float32(THETA)))
    angle = position.astype(jnp.float32)[:, None] * inverse[None, :]
    cosine = jnp.concatenate([jnp.cos(angle), jnp.cos(angle)], axis=1)
    sine = jnp.concatenate([jnp.sin(angle), jnp.sin(angle)], axis=1)
    return (cosine, sine)


def rotate(values, cosine, sine):
    half = values.shape[-1] // 2
    turned = jnp.concatenate([-values[..., half:], values[..., :half]], axis=-1)
    return values * cosine + turned * sine


def unrotate(grads, cosine, sine):
    half = grads.shape[-1] // 2
    scaled = grads * sine
    return grads * cosine + jnp.concatenate([scaled[..., half:], -scaled[..., :half]], axis=-1)


def norm_forward(values):
    scale = lax.rsqrt(jnp.mean(values * values, axis=1, keepdims=True) + EPS)
    return (values * scale, scale)


def norm_backward(grad_in, normed, scale, gain):
    gain_term = jnp.sum(grad_in * normed, axis=0)
    inner = grad_in * gain[None, :]
    back = scale * (inner - normed * jnp.mean(inner * normed, axis=1, keepdims=True))
    return (back, gain_term)


def layout(block_lengths, count):
    slots = jnp.arange(count, dtype=jnp.int32)
    first = block_lengths[0]
    second = block_lengths[1]
    segment = (slots >= first).astype(jnp.int32) + (slots >= first + second).astype(jnp.int32)
    position = (
        slots - first * (segment >= 1).astype(jnp.int32) - second * (segment >= 2).astype(jnp.int32)
    )
    live = (segment < 2).astype(jnp.float32)[:, None]
    allowed = (segment[:, None] == segment[None, :]) & (slots[None, :] <= slots[:, None])
    return (position, live, allowed)


def masked_scores(queries, keys, allowed):
    scores = jnp.einsum(
        "qkgd,jkd->kgqj", queries, keys, preferred_element_type=jnp.float32
    ) * HD ** (-0.5)
    return jnp.where(allowed[None, None], scores, NEG)


def attend(projected, cosine, sine, allowed, count):
    kv_width = KV * HD
    queries = rotate(
        projected[:, :D].reshape(count, KV, GROUP, HD),
        cosine[:, None, None, :],
        sine[:, None, None, :],
    ).astype(jnp.bfloat16)
    keys = rotate(
        projected[:, D : D + kv_width].reshape(count, KV, HD), cosine[:, None, :], sine[:, None, :]
    ).astype(jnp.bfloat16)
    values = projected[:, D + kv_width :].reshape(count, KV, HD).astype(jnp.bfloat16)
    scores = masked_scores(queries, keys, allowed)
    top = jnp.max(scores, axis=-1, keepdims=True)
    expo = jnp.exp(scores - top)
    total = jnp.sum(expo, axis=-1, keepdims=True)
    logsum = top + jnp.log(total)
    weights = (expo / total).astype(jnp.bfloat16)
    attended = (
        jnp.einsum("kgqj,jkd->qkgd", weights, values, preferred_element_type=jnp.float32)
        .reshape(count, D)
        .astype(jnp.bfloat16)
    )
    return (queries, keys, values, logsum, attended)


def attend_back(grad_att, queries, keys, values, logsum, allowed, cosine, sine, count):
    kv_width = KV * HD
    probs = jnp.exp(masked_scores(queries, keys, allowed) - logsum)
    probs_b = probs.astype(jnp.bfloat16)
    value_grad = jnp.einsum("kgqj,qkgd->jkd", probs_b, grad_att, preferred_element_type=jnp.float32)
    prob_grad = jnp.einsum("qkgd,jkd->kgqj", grad_att, values, preferred_element_type=jnp.float32)
    delta = jnp.sum(probs * prob_grad, axis=-1, keepdims=True)
    score_grad = (probs * (prob_grad - delta) * HD ** (-0.5)).astype(jnp.bfloat16)
    query_grad = jnp.einsum("kgqj,jkd->qkgd", score_grad, keys, preferred_element_type=jnp.float32)
    key_grad = jnp.einsum("kgqj,qkgd->jkd", score_grad, queries, preferred_element_type=jnp.float32)
    query_grad = unrotate(query_grad, cosine[:, None, None, :], sine[:, None, None, :])
    key_grad = unrotate(key_grad, cosine[:, None, :], sine[:, None, :])
    return jnp.concatenate(
        [
            query_grad.reshape(count, D),
            key_grad.reshape(count, kv_width),
            value_grad.reshape(count, kv_width),
        ],
        axis=1,
    ).astype(jnp.bfloat16)


def collect(attn_flat, gate_flat, up_flat, down_flat):
    whole = (
        lax.all_gather(attn_flat, ("fsdp", "sub"), axis=0, tiled=True),
        lax.all_gather(gate_flat, ("fsdp", "sub"), axis=0, tiled=True),
        lax.all_gather(up_flat, ("fsdp", "sub"), axis=0, tiled=True),
        lax.all_gather(down_flat, ("fsdp", "sub"), axis=0, tiled=True),
    )
    return tuple((piece.reshape(D, FF) for piece in whole))


def flat_terms(pair_lists, count):
    results = []
    for pairs in pair_lists:
        blocks = [
            jnp.dot(left.T, right, preferred_element_type=jnp.float32) for left, right in pairs
        ]
        joined = blocks[0] if len(blocks) == 1 else jnp.concatenate(blocks, axis=1)
        results.append(joined.reshape(-1).reshape(count, piece_width))
    return jnp.concatenate(results, axis=1)


def split_owned(owned):
    return tuple(
        (
            owned[:, index * piece_width : (index + 1) * piece_width].reshape(-1)
            for index in range(4)
        )
    )


def spread(pair_lists):
    share = D * FF // (piece_width * lax.axis_size("fsdp") * lax.axis_size("sub"))
    owned = lax.psum_scatter(
        flat_terms(pair_lists, share * lax.axis_size(("fsdp", "sub"))),
        ("fsdp", "sub"),
        scatter_dimension=0,
        tiled=True,
    )
    return split_owned(owned)


def flat_path(
    rows32,
    cotangent,
    live,
    allowed,
    cosine,
    sine,
    gain_attn,
    gain_mlp,
    normed1,
    scale1,
    input1,
    flats,
):
    count = rows32.shape[0]
    q_width = D + 2 * KV * HD
    attn_mat, gate_mat, up_mat, down_mat = collect(flats[0], flats[1], flats[2], flats[3])
    projected = jnp.dot(input1, attn_mat[:, :q_width], preferred_element_type=jnp.float32)
    queries, keys, values, logsum, attended = attend(projected, cosine, sine, allowed, count)
    hidden1 = rows32 + jnp.dot(
        attended, attn_mat[:, q_width:].T, preferred_element_type=jnp.float32
    )
    normed2, scale2 = norm_forward(hidden1)
    input2 = (normed2 * gain_mlp[None, :]).astype(jnp.bfloat16)
    gate = jnp.dot(input2, gate_mat, preferred_element_type=jnp.float32)
    up = jnp.dot(input2, up_mat, preferred_element_type=jnp.float32)
    sigma = jax.nn.sigmoid(gate)
    active = gate * sigma
    hidden = (active * up).astype(jnp.bfloat16)
    result = hidden1 + jnp.dot(hidden, down_mat.T, preferred_element_type=jnp.float32)
    output = (live * result).astype(jnp.bfloat16)
    attn_back, gate_back, up_back, down_back = collect(flats[0], flats[1], flats[2], flats[3])
    grad_out = live * cotangent.astype(jnp.float32)
    grad_outb = grad_out.astype(jnp.bfloat16)
    grad_hidden = jnp.dot(grad_outb, down_back, preferred_element_type=jnp.float32)
    grad_gate = (grad_hidden * up * sigma * (1.0 + gate * (1.0 - sigma))).astype(jnp.bfloat16)
    grad_up = (grad_hidden * active).astype(jnp.bfloat16)
    grad_in2 = jnp.dot(grad_gate, gate_back.T, preferred_element_type=jnp.float32) + jnp.dot(
        grad_up, up_back.T, preferred_element_type=jnp.float32
    )
    back2, gain2_term = norm_backward(grad_in2, normed2, scale2, gain_mlp)
    grad_h1 = grad_out + back2
    grad_h1b = grad_h1.astype(jnp.bfloat16)
    grad_att = (
        jnp.dot(grad_h1b, attn_back[:, q_width:], preferred_element_type=jnp.float32)
        .astype(jnp.bfloat16)
        .reshape(count, KV, GROUP, HD)
    )
    proj_grad = attend_back(grad_att, queries, keys, values, logsum, allowed, cosine, sine, count)
    grad_in1 = jnp.dot(proj_grad, attn_back[:, :q_width].T, preferred_element_type=jnp.float32)
    back1, gain1_term = norm_backward(grad_in1, normed1, scale1, gain_attn)
    input_grad = grad_h1 + back1
    pair_lists = (
        ((input1, proj_grad), (grad_h1b, attended)),
        ((input2, grad_gate),),
        ((input2, grad_up),),
        ((grad_outb, hidden),),
    )
    owned = spread(pair_lists)
    return (output, input_grad, owned, gain1_term, gain2_term)


def plain_body(rows, cotangent, lengths, gains, attn_weight, gate_weight, up_weight, down_weight):
    count = rows.shape[0]
    position, live, allowed = layout(lengths, count)
    cosine, sine = rope_tables(position, HD)
    full_gains = lax.all_gather(gains, "fsdp", axis=0, tiled=True).astype(jnp.float32)
    gain_attn = full_gains[:D]
    gain_mlp = full_gains[D:]
    rows32 = rows.astype(jnp.float32)
    normed1, scale1 = norm_forward(rows32)
    input1 = (normed1 * gain_attn[None, :]).astype(jnp.bfloat16)
    flats = (attn_weight, gate_weight, up_weight, down_weight)
    output, input_grad, owned, gain1_term, gain2_term = flat_path(
        rows32,
        cotangent,
        live,
        allowed,
        cosine,
        sine,
        gain_attn,
        gain_mlp,
        normed1,
        scale1,
        input1,
        flats,
    )
    gain_total = lax.psum(jnp.concatenate([gain1_term, gain2_term]), ("fsdp", "sub"))
    share = gains.shape[0]
    gain_grad = lax.dynamic_slice_in_dim(gain_total, lax.axis_index("fsdp") * share, share)
    return (output, input_grad, owned[0], owned[1], owned[2], owned[3], gain_grad)


BF = jnp.bfloat16
F32 = jnp.float32


def swap(value, axis, bit):
    return lax.ppermute(value, axis, [(i, i ^ bit) for i in range(lax.axis_size(axis))])


def meet(*values):
    return lax.optimization_barrier(values)


def after(value, *done):
    return lax.optimization_barrier((value, *done))[0]


def add2(kept, came):
    return (kept.astype(F32) + came.astype(F32)).astype(BF)


def far_pair(value, axis, odd):
    shape = value.shape
    value = value.reshape(shape[:axis] + (shape[axis] // 2, 2) + shape[axis + 1 :])
    return lax.index_in_dim(value, odd, axis + 1, keepdims=False)


def pick(value, index, axis):
    return lax.dynamic_index_in_dim(value, index, axis, keepdims=False)


def put2(own, came, bit, axis):
    first = bit == 0
    return jnp.stack([jnp.where(first, own, came), jnp.where(first, came, own)], axis=axis)


def mm(a, b):
    return jnp.dot(a, b, preferred_element_type=F32)


def mm_t(a, b):
    return lax.dot_general(a, b, (((1,), (1,)), ((), ())), preferred_element_type=F32)


def term(a, b):
    return lax.dot_general(a, b, (((0,), (0,)), ((), ())), preferred_element_type=F32).astype(BF)


def dot_f(a, b):
    return lax.dot_general(a, b, (((1,), (0,)), ((), ())), preferred_element_type=F32)


def dot_t(a, b):
    return lax.dot_general(a, b, (((1,), (1,)), ((), ())), preferred_element_type=F32)


def dot_0(a, b):
    return lax.dot_general(a, b, (((0,), (0,)), ((), ())), preferred_element_type=F32)


def norm_rows(values):
    mean = jnp.sum(values * values, axis=1, keepdims=True) * (1.0 / D)
    scale = lax.rsqrt(mean + EPS)
    return values * scale, scale


def norm_rows_back(grad_in, normed, scale, gain):
    gain_term = jnp.sum(grad_in * normed, axis=0, keepdims=True)
    inner = grad_in * gain
    mean = jnp.sum(inner * normed, axis=1, keepdims=True) * (1.0 / D)
    return scale * (inner - normed * mean), gain_term


def first_half(shape):
    return lax.broadcasted_iota(jnp.int32, shape, 1) % HD < HD // 2


def gain_masks(owner, my_fsdp, n_fsdp, own, share):
    wide = owner.shape[1]
    per = share // own
    place = lax.broadcasted_iota(jnp.int32, (n_fsdp, wide), 0) ^ my_fsdp
    group = owner // per
    return place == group, place == group + n_fsdp // 2


def slot_matrix(owner, inner, own, height):
    per = D * 2 // 8 // own
    slot = jnp.where(inner < own, owner % per * own + inner, -1)
    return (lax.broadcasted_iota(jnp.int32, (height, owner.shape[1]), 0) == slot).astype(F32).astype(BF)


def make_forward(n_fsdp, own, padded, share, by_fsdp):
    kv_width = KV * HD

    def kernel(
        place_ref, rows_ref, owner_ref, inner_ref, cos_ref, sin_ref, seg_ref,
        own_q_ref, came_q_ref, own_o_ref, came_o_ref,
        input1_ref, qk_ref, v_ref, logsum_ref, att_ref, hidden1_ref, input2_ref, gains_ref, attn_q_ref, attn_o_ref,
    ):
        core = place_ref[1]
        for p in range(own_q_ref.shape[0] // padded):
            here = pl.ds(pl.multiple_of((2 * p + core) * padded, padded), padded)
            there = pl.ds(pl.multiple_of((2 * p + 1 - core) * padded, padded), padded)
            block = slice(p * padded, (p + 1) * padded)
            attn_q_ref[here, :] = own_q_ref[block, :]
            attn_q_ref[there, :] = came_q_ref[block, :]
            attn_o_ref[here, :] = own_o_ref[block, :]
            attn_o_ref[there, :] = came_o_ref[block, :]
        pieces = jnp.concatenate(
            [attn_q_ref[p * padded + own : p * padded + own + 1, :share].astype(F32) for p in by_fsdp], axis=0
        ).astype(BF)
        owner = owner_ref[...]
        first, second = gain_masks(owner, place_ref[0], n_fsdp, own, share)
        spots = dot_f(pieces, slot_matrix(owner, inner_ref[...], own, share))
        gain1 = jnp.sum(jnp.where(first, spots, 0.0), axis=0, keepdims=True)
        gain2 = jnp.sum(jnp.where(second, spots, 0.0), axis=0, keepdims=True)
        gains_ref[0:1, :] = gain1
        gains_ref[1:2, :] = gain2
        rows = rows_ref[...]
        normed, _ = norm_rows(rows)
        input1 = (normed * gain1).astype(BF)
        input1_ref[...] = input1
        projected = dot_f(input1, attn_q_ref[...])
        cosine = cos_ref[...]
        sine = sin_ref[...]
        low = first_half(cosine.shape)
        for i in range(projected.shape[1] // 128):
            part = projected[:, 128 * i : 128 * (i + 1)]
            turned = jnp.where(low, -pltpu.roll(part, 96, 1), pltpu.roll(part, 32, 1))
            qk_ref[:, 128 * i : 128 * (i + 1)] = (part * cosine + turned * sine).astype(BF)
        values = dot_f(input1, attn_o_ref[:, :384]).astype(BF)
        v_ref[...] = values
        allowed = seg_ref[...] > 0.0
        att_ref[:, :384] = jnp.zeros((rows.shape[0], 384), BF)
        for k in range(KV):
            keys = qk_ref[:, D + HD * k : D + HD * (k + 1)]
            value = values[:, HD * k : HD * (k + 1)]
            for g in range(GROUP):
                h = GROUP * k + g
                queries = qk_ref[:, HD * h : HD * (h + 1)]
                scores = jnp.where(allowed, dot_t(queries, keys) * HD ** (-0.5), NEG)
                top = jnp.max(scores, axis=1, keepdims=True)
                expo = jnp.exp(scores - top)
                total = jnp.sum(expo, axis=1, keepdims=True)
                logsum_ref[:, h : h + 1] = top + jnp.log(total)
                weights = (expo / total).astype(BF)
                att_ref[:, kv_width + HD * h : kv_width + HD * (h + 1)] = dot_f(weights, value).astype(BF)
        hidden1 = rows + dot_t(att_ref[...], attn_o_ref[...])
        hidden1_ref[...] = hidden1
        normed2, _ = norm_rows(hidden1)
        input2_ref[...] = (normed2 * gain2).astype(BF)

    return kernel


def make_backward(n_fsdp, own, padded, share):
    kv_width = KV * HD

    def kernel(
        place_ref, grad_a_ref, grad_b_ref, grad_out_ref, hidden1_ref, rows_ref, gains_ref, owner_ref, inner_ref,
        spots_ref, cos_ref, sin_ref, seg_ref, input1_ref, qk_ref, v_ref, logsum_ref, att_ref,
        attn_q_ref, attn_o_ref,
        q_keep_ref, q_send_ref, o_keep_ref, o_send_ref, input_grad_ref,
        left_ref, right_ref, turn_ref,
    ):
        count = rows_ref.shape[0]
        wide = rows_ref.shape[1]
        core = place_ref[1]
        gain1 = gains_ref[0:1, :]
        gain2 = gains_ref[1:2, :]
        grad_in2 = grad_a_ref[...].astype(F32) + grad_b_ref[...].astype(F32)
        normed2, scale2 = norm_rows(hidden1_ref[...])
        back2, gain2_term = norm_rows_back(grad_in2, normed2, scale2, gain2)
        grad_h1 = grad_out_ref[...].astype(F32) + back2
        grad_h1b = grad_h1.astype(BF)
        left_ref[:count, :] = input1_ref[...]
        left_ref[count:, :] = grad_h1b
        right_ref[:count, :] = jnp.zeros((count, right_ref.shape[1]), BF)
        right_ref[count:, :] = att_ref[...]
        grad_att = dot_f(grad_h1b, attn_o_ref[...]).astype(BF)
        allowed = seg_ref[...] > 0.0
        for k in range(KV):
            keys = qk_ref[:, D + HD * k : D + HD * (k + 1)]
            value = v_ref[:, HD * k : HD * (k + 1)]
            value_grad = jnp.zeros((count, HD), F32)
            key_grad = jnp.zeros((count, HD), F32)
            for g in range(GROUP):
                h = GROUP * k + g
                queries = qk_ref[:, HD * h : HD * (h + 1)]
                grad = grad_att[:, kv_width + HD * h : kv_width + HD * (h + 1)]
                scores = jnp.where(allowed, dot_t(queries, keys) * HD ** (-0.5), NEG)
                probs = jnp.exp(scores - logsum_ref[:, h : h + 1])
                value_grad = value_grad + dot_0(probs.astype(BF), grad)
                prob_grad = dot_t(grad, value)
                delta = jnp.sum(probs * prob_grad, axis=1, keepdims=True)
                score_grad = (probs * (prob_grad - delta) * HD ** (-0.5)).astype(BF)
                turn_ref[:, HD * h : HD * (h + 1)] = dot_f(score_grad, keys)
                key_grad = key_grad + dot_0(score_grad, queries)
            turn_ref[:, D + HD * k : D + HD * (k + 1)] = key_grad
            right_ref[:count, HD * k : HD * (k + 1)] = value_grad.astype(BF)
        cosine = cos_ref[...]
        sine = sin_ref[...]
        low = first_half(cosine.shape)
        pieces = []
        for i in range(turn_ref.shape[1] // 128):
            part = turn_ref[:, 128 * i : 128 * (i + 1)]
            scaled = part * sine
            turned = jnp.where(low, pltpu.roll(scaled, 96, 1), -pltpu.roll(scaled, 32, 1))
            pieces.append((part * cosine + turned).astype(BF))
        proj_grad = jnp.concatenate(pieces, axis=1)
        o_term = dot_0(left_ref[...], right_ref[...]).astype(BF)
        owner = owner_ref[...]
        inner = inner_ref[...]
        grad_in1 = dot_t(proj_grad, attn_q_ref[...]) * jnp.where(inner < own, 1.0, 0.0) + dot_t(
            right_ref[:count, :], attn_o_ref[...]
        )
        normed1, scale1 = norm_rows(rows_ref[...])
        back1, gain1_term = norm_rows_back(grad_in1, normed1, scale1, gain1)
        input_grad_ref[...] = grad_h1 + back1
        first, second = gain_masks(owner, place_ref[0], n_fsdp, own, share)
        both = jnp.where(first, gain1_term, 0.0) + jnp.where(second, gain2_term, 0.0)
        gain_rows = dot_t(both.astype(BF), slot_matrix(owner, inner, own, 256)).astype(BF)
        q_term = dot_0(input1_ref[...], proj_grad)
        q_start = (q_term[:, :256] + dot_f(spots_ref[...], gain_rows)).astype(BF)
        q_term = q_term.astype(BF)
        q_term = jnp.concatenate([q_start, q_term[:, 256:]], axis=1)
        low_core = core == 0
        for p in range(wide // padded // 2):
            even = slice(2 * p * padded, (2 * p + 1) * padded)
            odd = slice((2 * p + 1) * padded, (2 * p + 2) * padded)
            to = slice(p * padded, (p + 1) * padded)
            q_keep_ref[to, :] = jnp.where(low_core, q_term[even, :], q_term[odd, :])
            q_send_ref[to, :] = jnp.where(low_core, q_term[odd, :], q_term[even, :])
            o_keep_ref[to, :] = jnp.where(low_core, o_term[even, :], o_term[odd, :])
            o_send_ref[to, :] = jnp.where(low_core, o_term[odd, :], o_term[even, :])

    return kernel


VMEM = pl.BlockSpec(memory_space=pltpu.VMEM)
SMEM = pl.BlockSpec(memory_space=pltpu.SMEM)


def run_kernel(kernel, outs, args, scratch=(), name=None):
    return pl.pallas_call(
        kernel,
        out_shape=[jax.ShapeDtypeStruct(shape, kind) for shape, kind in outs],
        in_specs=[SMEM] + [VMEM] * (len(args) - 1),
        out_specs=[VMEM] * len(outs),
        scratch_shapes=scratch,
        compiler_params=pltpu.CompilerParams(vmem_limit_bytes=56 << 20),
        cost_estimate=pl.CostEstimate(flops=1000, transcendentals=0, bytes_accessed=1000),
        name=name,
    )(*args)


def body(rows, cotangent, lengths, gains, attn_weight, gate_weight, up_weight, down_weight):
    count = rows.shape[0]
    n_fsdp = lax.axis_size("fsdp")
    n_sub = lax.axis_size("sub")
    n_all = n_fsdp * n_sub
    n_far = n_fsdp // 2
    own = D // n_all
    padded = -(-(own + 1) // 16) * 16
    wide = n_all * padded
    half_ff = FF // 2
    quarter = FF // 4
    share = gains.shape[0]
    kv_width = KV * HD
    my_fsdp = lax.axis_index("fsdp")
    my_sub = lax.axis_index("sub")
    my_y = my_sub // 2
    my_c = my_sub % 2

    column = jnp.arange(wide, dtype=jnp.int32)
    place = column // padded
    inner = column % padded
    rel = (place // n_sub) % n_far * 2 + place // (n_sub * n_far)
    real = inner < own
    source = jnp.where(real, ((rel ^ my_fsdp) * n_sub + place % n_sub) * own + inner, -1)
    spread_mat = (jnp.arange(D, dtype=jnp.int32)[:, None] == source[None, :]).astype(BF)

    def padded_block(flat):
        return jnp.pad(flat.reshape(own, FF), ((0, padded - own), (0, 0)))

    def columns(value, index, width):
        return lax.dynamic_slice_in_dim(value, index * width, width, axis=value.ndim - 1)

    position, live, allowed = layout(lengths, count)
    cosine, sine = rope_tables(position, HD)
    cosine = jnp.concatenate([cosine, cosine], axis=1)
    sine = jnp.concatenate([sine, sine], axis=1)
    seg = allowed.astype(F32)
    rows32 = mm(rows, spread_mat)
    grad_outb = (live * mm(cotangent, spread_mat)).astype(BF)

    of_place = [(p // n_sub) % n_far * 2 + p // (n_sub * n_far) for p in range(n_all)]
    at_spot = jnp.where(inner == own, jnp.array(of_place)[place], -1)
    spots = (at_spot[:, None] == jnp.arange(n_fsdp)[None, :]).astype(BF)
    owner = ((rel ^ my_fsdp) * n_sub + place % n_sub)[None, :]

    attn_block = padded_block(attn_weight)
    attn_block = attn_block.at[own, :share].set(gains)
    far = [swap(attn_block, "fsdp", 2 * k) for k in range(1, n_far)]
    mlp_block = jnp.stack([padded_block(w) for w in (gate_weight, up_weight, down_weight)])
    came = swap(columns(mlp_block, 1 - my_y, half_ff), "sub", 2)
    mlp_block = put2(columns(mlp_block, my_y, half_ff), came, my_y, 1)
    came = swap(columns(mlp_block, 1 - my_c, quarter), "sub", 1)
    mlp_block = put2(columns(mlp_block, my_c, quarter), came, my_c, 2)
    mlp_block = mlp_block.reshape(3, n_sub * padded, quarter)
    far, mlp_block = meet(far, mlp_block)

    attn_far = jnp.stack([attn_block] + list(far))
    half0 = attn_far[:, :, :half_ff]
    half1 = attn_far[:, :, half_ff:]
    gate_up = mlp_block[:2]
    down = mlp_block[2]
    x0, y1, near = swap(half0, "fsdp", 1), swap(half1, "sub", 2), swap(gate_up, "fsdp", 2)
    tables = (owner, inner[None, :])
    angles = (cosine, sine, seg)
    half0, half1, gate_up, down, x0, y1, near, rows32, grad_outb, spots, tables, angles = meet(
        half0, half1, gate_up, down, x0, y1, near, rows32, grad_outb, spots, tables, angles
    )

    half0 = jnp.stack([half0, x0])
    half1 = put2(half1, y1, my_y, 1)
    y0, x1, third = swap(half0, "sub", 2), swap(half1, "fsdp", 1), swap(gate_up, "fsdp", 4)
    down_x = swap(down, "fsdp", 1)
    half0, half1, gate_up, down, down_x, near, y0, x1, third, grad_outb = meet(
        half0, half1, gate_up, down, down_x, near, y0, x1, third, grad_outb
    )

    half0 = put2(half0, y0, my_y, 2).reshape(wide // 2, half_ff)
    half1 = jnp.stack([half1, x1]).reshape(wide // 2, half_ff)
    c0, c1, last = swap(half0, "sub", 1), swap(half1, "sub", 1), swap(third, "fsdp", 2)
    cot_y = swap(grad_outb, "sub", 2)
    down = jnp.stack([down, down_x])
    half0, half1, c0, c1, gate_up, near, third, last, down, cot_y = meet(
        half0, half1, c0, c1, gate_up, near, third, last, down, cot_y
    )

    gate_up = jnp.stack([gate_up, near, third, last])
    gate_up_x = swap(gate_up, "fsdp", 1)
    down_near, down_third = swap(down, "fsdp", 2), swap(down, "fsdp", 4)
    by_fsdp = [(f % 2) * n_far * n_sub + (f // 2) * n_sub for f in range(n_fsdp)]
    my_place = jnp.stack([my_fsdp, my_c])
    tall = (count, wide)
    forward = run_kernel(
        make_forward(n_fsdp, own, padded, share, by_fsdp),
        [
            (tall, BF),
            ((count, half_ff), BF),
            ((count, 384), BF),
            ((count, KV * GROUP), F32),
            ((count, half_ff), BF),
            (tall, F32),
            (tall, BF),
            ((2, wide), F32),
            ((wide, half_ff), BF),
            ((wide, half_ff), BF),
        ],
        (my_place, rows32, *tables, *angles, half0, c0, half1, c1),
        name="attn_forward",
    )
    input1, qk, values, logsum, attended, hidden1, input2, gains_p, attn_q, attn_o = forward

    in2_y = swap(input2, "sub", 2)
    input2, in2_y, cot_y, down_near, down_third = meet(input2, in2_y, cot_y, down_near, down_third)
    down_last = swap(down_third, "fsdp", 2)
    in2_all = jnp.stack([input2, in2_y])
    cot_all = jnp.stack([grad_outb, cot_y])
    in2_c, cot_c = swap(in2_all, "sub", 1), swap(cot_all, "sub", 1)
    in2_c, cot_c, gate_up_x, down_last = meet(in2_c, cot_c, gate_up_x, down_last)
    in2_all = jnp.stack([in2_all, in2_c]).reshape(4 * count, wide)
    cot_all = jnp.stack([cot_all, cot_c]).reshape(4 * count, wide)
    gate_w = jnp.stack([gate_up[:, 0], gate_up_x[:, 0]]).reshape(wide, quarter)
    up_w = jnp.stack([gate_up[:, 1], gate_up_x[:, 1]]).reshape(wide, quarter)
    gate = mm(in2_all, gate_w)
    up = mm(in2_all, up_w)
    sigma = jax.nn.sigmoid(gate)
    active = gate * sigma
    hidden = (active * up).astype(BF)
    down_term = term(cot_all, hidden).reshape(2, n_far, n_sub * padded, quarter)
    down_w = jnp.stack([down, down_near, down_third, down_last])
    down_w = down_w.transpose(1, 0, 2, 3).reshape(wide, quarter)
    down_near_came = swap(far_pair(down_term, 1, 1), "fsdp", 2)
    grad_hidden = mm(cot_all, down_w)
    grad_gate = (grad_hidden * up * sigma * (1.0 + gate * (1.0 - sigma))).astype(BF)
    grad_up = (grad_hidden * active).astype(BF)
    grad_in2 = (mm_t(grad_gate, gate_w) + mm_t(grad_up, up_w)).astype(BF).reshape(2, 2 * count, wide)
    gate_up_term = jnp.stack([term(in2_all, grad_gate), term(in2_all, grad_up)])
    gate_up_term = gate_up_term.reshape(2, 2, n_far, n_sub * padded, quarter)
    result = mm_t(hidden, down_w).astype(BF).reshape(2, 2 * count, wide)

    came = swap(grad_in2[1], "sub", 1)
    grad_in2 = add2(grad_in2[0], came).reshape(2, count, wide)
    grad_in2_y = swap(grad_in2[1], "sub", 2)
    gate_up_x_came = swap(gate_up_term[:, 1], "fsdp", 1)
    grad_in2, grad_in2_y, down_near_came = meet(grad_in2, grad_in2_y, down_near_came)
    down_held = add2(far_pair(down_term, 1, 0), down_near_came)
    down_far_came = swap(down_held[:, 1], "fsdp", 4)
    q_keep, q_send, o_keep, o_send, input_grad = run_kernel(
        make_backward(n_fsdp, own, padded, share),
        [((wide // 2, half_ff), BF)] * 4 + [(tall, F32)],
        (
            my_place, grad_in2[0], grad_in2_y, grad_outb, hidden1, rows32, gains_p, *tables, spots, *angles,
            input1, qk, values, logsum, attended, attn_q, attn_o,
        ),
        scratch=[
            pltpu.VMEM((2 * count, wide), BF),
            pltpu.VMEM((2 * count, half_ff), BF),
            pltpu.VMEM((count, half_ff), F32),
        ],
        name="attn_backward",
    )

    q_keep, q_send, o_keep, o_send, down_far_came, gate_up_x_came = meet(
        q_keep, q_send, o_keep, o_send, down_far_came, gate_up_x_came
    )

    q_c, o_c = swap(q_send, "sub", 1), swap(o_send, "sub", 1)
    gate_up_held = add2(gate_up_term[:, 0], gate_up_x_came)
    gate_up_near = swap(far_pair(gate_up_held, 1, 1), "fsdp", 2)
    down_held = add2(down_held[:, 0], down_far_came)
    down_x_came = swap(down_held[1], "fsdp", 1)
    q_c, o_c, gate_up_near, down_x_came = meet(q_c, o_c, gate_up_near, down_x_came)

    full = (2, n_far, 2, padded, half_ff)
    q_held = add2(q_keep, q_c).reshape(full)
    o_held = add2(o_keep, o_c).reshape(full)
    q_y = swap(pick(q_held, 1 - my_y, 2), "sub", 2)
    o_x = swap(o_held[1], "fsdp", 1)
    gate_up_held = add2(far_pair(gate_up_held, 1, 0), gate_up_near)
    gate_up_far = swap(gate_up_held[:, 1], "fsdp", 4)
    input_grad = after(input_grad, q_c)
    input_grad = lax.dot_general(
        input_grad,
        spread_mat.astype(F32),
        (((1,), (1,)), ((), ())),
        precision=lax.Precision.HIGHEST,
    )
    res_c = swap(after(result[1], q_c), "sub", 1)
    q_y, o_x, gate_up_far, input_grad, res_c = meet(q_y, o_x, gate_up_far, input_grad, res_c)

    q_held = add2(pick(q_held, my_y, 2), q_y)
    o_held = add2(o_held[0], o_x)
    q_x = swap(q_held[1], "fsdp", 1)
    o_y = swap(pick(o_held, 1 - my_y, 1), "sub", 2)
    down_own = add2(down_held[0], down_x_came)[None]
    mlp_own = jnp.concatenate([add2(gate_up_held[:, 0], gate_up_far), down_own])
    mlp_own = mlp_own.reshape(3, 2, 2, padded, quarter)
    mlp_c = swap(pick(mlp_own, 1 - my_c, 2), "sub", 1)
    q_x, o_y, mlp_c = meet(q_x, o_y, mlp_c)

    def side_by_side(mine, came, bit):
        first = bit == 0
        return jnp.concatenate([jnp.where(first, mine, came), jnp.where(first, came, mine)], axis=-1)

    q_held = add2(q_held[0], q_x)
    o_held = add2(pick(o_held, my_y, 1), o_y)
    attn_held = jnp.concatenate([q_held, o_held], axis=-1)
    attn_near = swap(far_pair(attn_held, 0, 1), "fsdp", 2)
    result = add2(result[0], res_c).reshape(2, count, wide)
    res_y = swap(result[1], "sub", 2)
    mlp_own = side_by_side(pick(mlp_own, my_c, 2), mlp_c, my_c)
    mlp_y = swap(pick(mlp_own, 1 - my_y, 1), "sub", 2)
    attn_near, res_y, mlp_y = meet(attn_near, res_y, mlp_y)
    attn_held = add2(far_pair(attn_held, 0, 0), attn_near)
    attn_far = swap(attn_held[1], "fsdp", 4)
    result = hidden1 + result[0].astype(F32) + res_y.astype(F32)
    output = mm_t((live * result).astype(BF), spread_mat).astype(BF)
    mlp_own = side_by_side(pick(mlp_own, my_y, 1), mlp_y, my_y)
    attn_own = add2(attn_held[0], attn_far)
    gain_grad = attn_own[own, :share].astype(F32)

    def flat(mine):
        return mine[:own].astype(F32).reshape(-1)

    return (
        output,
        input_grad,
        flat(attn_own),
        flat(mlp_own[0]),
        flat(mlp_own[1]),
        flat(mlp_own[2]),
        gain_grad,
    )


def solution(mesh):
    n_fsdp, n_sub = mesh.shape["fsdp"], mesh.shape["sub"]
    n_all = n_fsdp * n_sub
    by_rows = (
        n_fsdp == 8 and D % n_all == 0 and n_fsdp & (n_fsdp - 1) == 0 and n_fsdp > 1 and n_sub == 4 and D // n_fsdp % (D // n_all) == 0
    )
    in_specs = (
        P(("fsdp", "sub"), None),
        P(("fsdp", "sub"), None),
        P(("fsdp", "sub")),
        P("fsdp"),
        P(("fsdp", "sub")),
        P(("fsdp", "sub")),
        P(("fsdp", "sub")),
        P(("fsdp", "sub")),
    )
    out_specs = (
        P(("fsdp", "sub"), None),
        P(("fsdp", "sub"), None),
        P(("fsdp", "sub")),
        P(("fsdp", "sub")),
        P(("fsdp", "sub")),
        P(("fsdp", "sub")),
        P("fsdp"),
    )
    return jax.shard_map(body if by_rows else plain_body, mesh=mesh, in_specs=in_specs, out_specs=out_specs, check_vma=False)
```

```python
import jax
import jax.numpy as jnp
from jax import lax
from jax.experimental import pallas as pl
from jax.experimental.pallas import tpu as pltpu
from jax.sharding import PartitionSpec as P

D = 960
KV = 5
HD = 64
FF = 2560
GROUP = 3


EPS = 1e-05
THETA = 100000.0
NEG = -1e30
piece_width = 64


def rope_tables(position, width):
    half = jnp.arange(width // 2, dtype=jnp.float32)
    inverse = jnp.exp(-(2.0 * half / width) * jnp.log(jnp.float32(THETA)))
    angle = position.astype(jnp.float32)[:, None] * inverse[None, :]
    cosine = jnp.concatenate([jnp.cos(angle), jnp.cos(angle)], axis=1)
    sine = jnp.concatenate([jnp.sin(angle), jnp.sin(angle)], axis=1)
    return (cosine, sine)


def rotate(values, cosine, sine):
    half = values.shape[-1] // 2
    turned = jnp.concatenate([-values[..., half:], values[..., :half]], axis=-1)
    return values * cosine + turned * sine


def unrotate(grads, cosine, sine):
    half = grads.shape[-1] // 2
    scaled = grads * sine
    return grads * cosine + jnp.concatenate([scaled[..., half:], -scaled[..., :half]], axis=-1)


def norm_forward(values):
    scale = lax.rsqrt(jnp.mean(values * values, axis=1, keepdims=True) + EPS)
    return (values * scale, scale)


def norm_backward(grad_in, normed, scale, gain):
    gain_term = jnp.sum(grad_in * normed, axis=0)
    inner = grad_in * gain[None, :]
    back = scale * (inner - normed * jnp.mean(inner * normed, axis=1, keepdims=True))
    return (back, gain_term)


def layout(block_lengths, count):
    slots = jnp.arange(count, dtype=jnp.int32)
    first = block_lengths[0]
    second = block_lengths[1]
    segment = (slots >= first).astype(jnp.int32) + (slots >= first + second).astype(jnp.int32)
    position = (
        slots - first * (segment >= 1).astype(jnp.int32) - second * (segment >= 2).astype(jnp.int32)
    )
    live = (segment < 2).astype(jnp.float32)[:, None]
    allowed = (segment[:, None] == segment[None, :]) & (slots[None, :] <= slots[:, None])
    return (position, live, allowed)


def masked_scores(queries, keys, allowed):
    scores = jnp.einsum(
        "qkgd,jkd->kgqj", queries, keys, preferred_element_type=jnp.float32
    ) * HD ** (-0.5)
    return jnp.where(allowed[None, None], scores, NEG)


def attend(projected, cosine, sine, allowed, count):
    kv_width = KV * HD
    queries = rotate(
        projected[:, :D].reshape(count, KV, GROUP, HD),
        cosine[:, None, None, :],
        sine[:, None, None, :],
    ).astype(jnp.bfloat16)
    keys = rotate(
        projected[:, D : D + kv_width].reshape(count, KV, HD), cosine[:, None, :], sine[:, None, :]
    ).astype(jnp.bfloat16)
    values = projected[:, D + kv_width :].reshape(count, KV, HD).astype(jnp.bfloat16)
    scores = masked_scores(queries, keys, allowed)
    top = jnp.max(scores, axis=-1, keepdims=True)
    expo = jnp.exp(scores - top)
    total = jnp.sum(expo, axis=-1, keepdims=True)
    logsum = top + jnp.log(total)
    weights = (expo / total).astype(jnp.bfloat16)
    attended = (
        jnp.einsum("kgqj,jkd->qkgd", weights, values, preferred_element_type=jnp.float32)
        .reshape(count, D)
        .astype(jnp.bfloat16)
    )
    return (queries, keys, values, logsum, attended)


def attend_back(grad_att, queries, keys, values, logsum, allowed, cosine, sine, count):
    kv_width = KV * HD
    probs = jnp.exp(masked_scores(queries, keys, allowed) - logsum)
    probs_b = probs.astype(jnp.bfloat16)
    value_grad = jnp.einsum("kgqj,qkgd->jkd", probs_b, grad_att, preferred_element_type=jnp.float32)
    prob_grad = jnp.einsum("qkgd,jkd->kgqj", grad_att, values, preferred_element_type=jnp.float32)
    delta = jnp.sum(probs * prob_grad, axis=-1, keepdims=True)
    score_grad = (probs * (prob_grad - delta) * HD ** (-0.5)).astype(jnp.bfloat16)
    query_grad = jnp.einsum("kgqj,jkd->qkgd", score_grad, keys, preferred_element_type=jnp.float32)
    key_grad = jnp.einsum("kgqj,qkgd->jkd", score_grad, queries, preferred_element_type=jnp.float32)
    query_grad = unrotate(query_grad, cosine[:, None, None, :], sine[:, None, None, :])
    key_grad = unrotate(key_grad, cosine[:, None, :], sine[:, None, :])
    return jnp.concatenate(
        [
            query_grad.reshape(count, D),
            key_grad.reshape(count, kv_width),
            value_grad.reshape(count, kv_width),
        ],
        axis=1,
    ).astype(jnp.bfloat16)


def collect(attn_flat, gate_flat, up_flat, down_flat):
    whole = (
        lax.all_gather(attn_flat, ("fsdp", "sub"), axis=0, tiled=True),
        lax.all_gather(gate_flat, ("fsdp", "sub"), axis=0, tiled=True),
        lax.all_gather(up_flat, ("fsdp", "sub"), axis=0, tiled=True),
        lax.all_gather(down_flat, ("fsdp", "sub"), axis=0, tiled=True),
    )
    return tuple((piece.reshape(D, FF) for piece in whole))


def flat_terms(pair_lists, count):
    results = []
    for pairs in pair_lists:
        blocks = [
            jnp.dot(left.T, right, preferred_element_type=jnp.float32) for left, right in pairs
        ]
        joined = blocks[0] if len(blocks) == 1 else jnp.concatenate(blocks, axis=1)
        results.append(joined.reshape(-1).reshape(count, piece_width))
    return jnp.concatenate(results, axis=1)


def split_owned(owned):
    return tuple(
        (
            owned[:, index * piece_width : (index + 1) * piece_width].reshape(-1)
            for index in range(4)
        )
    )


def spread(pair_lists):
    share = D * FF // (piece_width * lax.axis_size("fsdp") * lax.axis_size("sub"))
    owned = lax.psum_scatter(
        flat_terms(pair_lists, share * lax.axis_size(("fsdp", "sub"))),
        ("fsdp", "sub"),
        scatter_dimension=0,
        tiled=True,
    )
    return split_owned(owned)


def flat_path(
    rows32,
    cotangent,
    live,
    allowed,
    cosine,
    sine,
    gain_attn,
    gain_mlp,
    normed1,
    scale1,
    input1,
    flats,
):
    count = rows32.shape[0]
    q_width = D + 2 * KV * HD
    attn_mat, gate_mat, up_mat, down_mat = collect(flats[0], flats[1], flats[2], flats[3])
    projected = jnp.dot(input1, attn_mat[:, :q_width], preferred_element_type=jnp.float32)
    queries, keys, values, logsum, attended = attend(projected, cosine, sine, allowed, count)
    hidden1 = rows32 + jnp.dot(
        attended, attn_mat[:, q_width:].T, preferred_element_type=jnp.float32
    )
    normed2, scale2 = norm_forward(hidden1)
    input2 = (normed2 * gain_mlp[None, :]).astype(jnp.bfloat16)
    gate = jnp.dot(input2, gate_mat, preferred_element_type=jnp.float32)
    up = jnp.dot(input2, up_mat, preferred_element_type=jnp.float32)
    sigma = jax.nn.sigmoid(gate)
    active = gate * sigma
    hidden = (active * up).astype(jnp.bfloat16)
    result = hidden1 + jnp.dot(hidden, down_mat.T, preferred_element_type=jnp.float32)
    output = (live * result).astype(jnp.bfloat16)
    attn_back, gate_back, up_back, down_back = collect(flats[0], flats[1], flats[2], flats[3])
    grad_out = live * cotangent.astype(jnp.float32)
    grad_outb = grad_out.astype(jnp.bfloat16)
    grad_hidden = jnp.dot(grad_outb, down_back, preferred_element_type=jnp.float32)
    grad_gate = (grad_hidden * up * sigma * (1.0 + gate * (1.0 - sigma))).astype(jnp.bfloat16)
    grad_up = (grad_hidden * active).astype(jnp.bfloat16)
    grad_in2 = jnp.dot(grad_gate, gate_back.T, preferred_element_type=jnp.float32) + jnp.dot(
        grad_up, up_back.T, preferred_element_type=jnp.float32
    )
    back2, gain2_term = norm_backward(grad_in2, normed2, scale2, gain_mlp)
    grad_h1 = grad_out + back2
    grad_h1b = grad_h1.astype(jnp.bfloat16)
    grad_att = (
        jnp.dot(grad_h1b, attn_back[:, q_width:], preferred_element_type=jnp.float32)
        .astype(jnp.bfloat16)
        .reshape(count, KV, GROUP, HD)
    )
    proj_grad = attend_back(grad_att, queries, keys, values, logsum, allowed, cosine, sine, count)
    grad_in1 = jnp.dot(proj_grad, attn_back[:, :q_width].T, preferred_element_type=jnp.float32)
    back1, gain1_term = norm_backward(grad_in1, normed1, scale1, gain_attn)
    input_grad = grad_h1 + back1
    pair_lists = (
        ((input1, proj_grad), (grad_h1b, attended)),
        ((input2, grad_gate),),
        ((input2, grad_up),),
        ((grad_outb, hidden),),
    )
    owned = spread(pair_lists)
    return (output, input_grad, owned, gain1_term, gain2_term)


def plain_body(rows, cotangent, lengths, gains, attn_weight, gate_weight, up_weight, down_weight):
    count = rows.shape[0]
    position, live, allowed = layout(lengths, count)
    cosine, sine = rope_tables(position, HD)
    full_gains = lax.all_gather(gains, "fsdp", axis=0, tiled=True).astype(jnp.float32)
    gain_attn = full_gains[:D]
    gain_mlp = full_gains[D:]
    rows32 = rows.astype(jnp.float32)
    normed1, scale1 = norm_forward(rows32)
    input1 = (normed1 * gain_attn[None, :]).astype(jnp.bfloat16)
    flats = (attn_weight, gate_weight, up_weight, down_weight)
    output, input_grad, owned, gain1_term, gain2_term = flat_path(
        rows32,
        cotangent,
        live,
        allowed,
        cosine,
        sine,
        gain_attn,
        gain_mlp,
        normed1,
        scale1,
        input1,
        flats,
    )
    gain_total = lax.psum(jnp.concatenate([gain1_term, gain2_term]), ("fsdp", "sub"))
    share = gains.shape[0]
    gain_grad = lax.dynamic_slice_in_dim(gain_total, lax.axis_index("fsdp") * share, share)
    return (output, input_grad, owned[0], owned[1], owned[2], owned[3], gain_grad)


BF = jnp.bfloat16
F32 = jnp.float32


def swap(value, axis, bit):
    return lax.ppermute(value, axis, [(i, i ^ bit) for i in range(lax.axis_size(axis))])


def meet(*values):
    return lax.optimization_barrier(values)


def after(value, *done):
    return lax.optimization_barrier((value, *done))[0]


def add2(kept, came):
    return (kept.astype(F32) + came.astype(F32)).astype(BF)


def far_pair(value, axis, odd):
    shape = value.shape
    value = value.reshape(shape[:axis] + (shape[axis] // 2, 2) + shape[axis + 1 :])
    return lax.index_in_dim(value, odd, axis + 1, keepdims=False)


def pick(value, index, axis):
    return lax.dynamic_index_in_dim(value, index, axis, keepdims=False)


def put2(own, came, bit, axis):
    first = bit == 0
    return jnp.stack([jnp.where(first, own, came), jnp.where(first, came, own)], axis=axis)


def mm(a, b):
    return jnp.dot(a, b, preferred_element_type=F32)


def mm_t(a, b):
    return lax.dot_general(a, b, (((1,), (1,)), ((), ())), preferred_element_type=F32)


def term(a, b):
    return lax.dot_general(a, b, (((0,), (0,)), ((), ())), preferred_element_type=F32).astype(BF)


def dot_f(a, b):
    return lax.dot_general(a, b, (((1,), (0,)), ((), ())), preferred_element_type=F32)


def dot_t(a, b):
    return lax.dot_general(a, b, (((1,), (1,)), ((), ())), preferred_element_type=F32)


def dot_0(a, b):
    return lax.dot_general(a, b, (((0,), (0,)), ((), ())), preferred_element_type=F32)


def norm_rows(values):
    mean = jnp.sum(values * values, axis=1, keepdims=True) * (1.0 / D)
    scale = lax.rsqrt(mean + EPS)
    return values * scale, scale


def norm_rows_back(grad_in, normed, scale, gain):
    gain_term = jnp.sum(grad_in * normed, axis=0, keepdims=True)
    inner = grad_in * gain
    mean = jnp.sum(inner * normed, axis=1, keepdims=True) * (1.0 / D)
    return scale * (inner - normed * mean), gain_term


def first_half(shape):
    return lax.broadcasted_iota(jnp.int32, shape, 1) % HD < HD // 2


def gain_masks(owner, my_fsdp, n_fsdp, own, share):
    wide = owner.shape[1]
    per = share // own
    place = lax.broadcasted_iota(jnp.int32, (n_fsdp, wide), 0) ^ my_fsdp
    group = owner // per
    return place == group, place == group + n_fsdp // 2


def slot_matrix(owner, inner, own, height):
    per = D * 2 // 8 // own
    slot = jnp.where(inner < own, owner % per * own + inner, -1)
    return (lax.broadcasted_iota(jnp.int32, (height, owner.shape[1]), 0) == slot).astype(F32).astype(BF)


def make_forward(n_fsdp, own, padded, share, by_fsdp):
    kv_width = KV * HD

    def kernel(
        place_ref, rows_ref, owner_ref, inner_ref, cos_ref, sin_ref, seg_ref,
        own_q_ref, came_q_ref, own_o_ref, came_o_ref,
        att_ref, qk_ref, v_ref, logsum_ref, hidden1_ref, input2_ref, gains_ref, attn_q_ref, attn_o_ref,
    ):
        core = place_ref[1]
        for p in range(own_q_ref.shape[0] // padded):
            here = pl.ds(pl.multiple_of((2 * p + core) * padded, padded), padded)
            there = pl.ds(pl.multiple_of((2 * p + 1 - core) * padded, padded), padded)
            block = slice(p * padded, (p + 1) * padded)
            attn_q_ref[here, :] = own_q_ref[block, :]
            attn_q_ref[there, :] = came_q_ref[block, :]
            attn_o_ref[here, :] = own_o_ref[block, :]
            attn_o_ref[there, :] = came_o_ref[block, :]
        pieces = jnp.concatenate(
            [attn_q_ref[p * padded + own : p * padded + own + 1, :share].astype(F32) for p in by_fsdp], axis=0
        ).astype(BF)
        owner = owner_ref[...]
        first, second = gain_masks(owner, place_ref[0], n_fsdp, own, share)
        spots = dot_f(pieces, slot_matrix(owner, inner_ref[...], own, share))
        gain1 = jnp.sum(jnp.where(first, spots, 0.0), axis=0, keepdims=True)
        gain2 = jnp.sum(jnp.where(second, spots, 0.0), axis=0, keepdims=True)
        gains_ref[0:1, :] = gain1
        gains_ref[1:2, :] = gain2
        rows = rows_ref[...]
        normed, _ = norm_rows(rows)
        input1 = (normed * gain1).astype(BF)
        projected = dot_f(input1, attn_q_ref[...])
        cosine = cos_ref[...]
        sine = sin_ref[...]
        low = first_half(cosine.shape)
        for i in range(projected.shape[1] // 128):
            part = projected[:, 128 * i : 128 * (i + 1)]
            turned = jnp.where(low, -pltpu.roll(part, 96, 1), pltpu.roll(part, 32, 1))
            qk_ref[:, 128 * i : 128 * (i + 1)] = (part * cosine + turned * sine).astype(BF)
        values = dot_f(input1, attn_o_ref[:, :384]).astype(BF)
        v_ref[...] = values
        allowed = seg_ref[...] > 0.0
        att_ref[:, :128] = jnp.zeros((rows.shape[0], 128), BF)
        shift = kv_width - 256
        for k in range(KV):
            keys = qk_ref[:, D + HD * k : D + HD * (k + 1)]
            value = values[:, HD * k : HD * (k + 1)]
            for g in range(GROUP):
                h = GROUP * k + g
                queries = qk_ref[:, HD * h : HD * (h + 1)]
                scores = jnp.where(allowed, dot_t(queries, keys) * HD ** (-0.5), NEG)
                top = jnp.max(scores, axis=1, keepdims=True)
                expo = jnp.exp(scores - top)
                total = jnp.sum(expo, axis=1, keepdims=True)
                logsum_ref[:, h : h + 1] = top + jnp.log(total)
                weights = (expo / total).astype(BF)
                att_ref[:, shift + HD * h : shift + HD * (h + 1)] = dot_f(weights, value).astype(BF)
        hidden1 = rows + dot_t(att_ref[...], attn_o_ref[:, 256:])
        hidden1_ref[...] = hidden1
        normed2, _ = norm_rows(hidden1)
        input2_ref[...] = (normed2 * gain2).astype(BF)

    return kernel


def norm_kernel(
    place_ref, grad_a_ref, grad_b_ref, grad_out_ref, hidden1_ref, gains_ref,
    grad_h1_ref, grad_h1b_ref, gain2_ref,
):
    grad_in2 = grad_a_ref[...].astype(F32) + grad_b_ref[...].astype(F32)
    normed2, scale2 = norm_rows(hidden1_ref[...])
    back2, gain2_term = norm_rows_back(grad_in2, normed2, scale2, gains_ref[1:2, :])
    grad_h1 = grad_out_ref[...].astype(F32) + back2
    grad_h1_ref[...] = grad_h1
    grad_h1b_ref[...] = grad_h1.astype(BF)
    gain2_ref[...] = gain2_term


def make_backward(n_fsdp, own):
    kv_width = KV * HD

    def kernel(
        place_ref, grad_h1_ref, grad_h1b_ref, gain2_ref, rows_ref, gains_ref, owner_ref, inner_ref,
        cos_ref, sin_ref, seg_ref, qk_ref, v_ref, logsum_ref, attn_q_ref, attn_o_ref,
        grads_ref, input_grad_ref,
        turn_ref,
    ):
        count = rows_ref.shape[0]
        qk_width = turn_ref.shape[1]
        grad_att = dot_f(grad_h1b_ref[...], attn_o_ref[...]).astype(BF)
        allowed = seg_ref[...] > 0.0
        grads_ref[:count, qk_width:] = jnp.zeros((count, 384), BF)
        for k in range(KV):
            keys = qk_ref[:, D + HD * k : D + HD * (k + 1)]
            value = v_ref[:, HD * k : HD * (k + 1)]
            value_grad = jnp.zeros((count, HD), F32)
            key_grad = jnp.zeros((count, HD), F32)
            for g in range(GROUP):
                h = GROUP * k + g
                queries = qk_ref[:, HD * h : HD * (h + 1)]
                grad = grad_att[:, kv_width + HD * h : kv_width + HD * (h + 1)]
                scores = jnp.where(allowed, dot_t(queries, keys) * HD ** (-0.5), NEG)
                probs = jnp.exp(scores - logsum_ref[:, h : h + 1])
                value_grad = value_grad + dot_0(probs.astype(BF), grad)
                prob_grad = dot_t(grad, value)
                delta = jnp.sum(probs * prob_grad, axis=1, keepdims=True)
                score_grad = (probs * (prob_grad - delta) * HD ** (-0.5)).astype(BF)
                turn_ref[:, HD * h : HD * (h + 1)] = dot_f(score_grad, keys)
                key_grad = key_grad + dot_0(score_grad, queries)
            turn_ref[:, D + HD * k : D + HD * (k + 1)] = key_grad
            grads_ref[:count, qk_width + HD * k : qk_width + HD * (k + 1)] = value_grad.astype(BF)
        cosine = cos_ref[...]
        sine = sin_ref[...]
        low = first_half(cosine.shape)
        for i in range(qk_width // 128):
            part = turn_ref[:, 128 * i : 128 * (i + 1)]
            scaled = part * sine
            turned = jnp.where(low, pltpu.roll(scaled, 96, 1), -pltpu.roll(scaled, 32, 1))
            grads_ref[:count, 128 * i : 128 * (i + 1)] = (part * cosine + turned).astype(BF)
        owner = owner_ref[...]
        inner = inner_ref[...]
        grad_in1 = dot_t(grads_ref[:count, :qk_width], attn_q_ref[...]) * jnp.where(inner < own, 1.0, 0.0)
        grad_in1 = grad_in1 + dot_t(grads_ref[:count, qk_width:], attn_o_ref[:, :384])
        normed1, scale1 = norm_rows(rows_ref[...])
        back1, gain1_term = norm_rows_back(grad_in1, normed1, scale1, gains_ref[0:1, :])
        input_grad_ref[...] = grad_h1_ref[...] + back1
        first, second = gain_masks(owner, place_ref[0], n_fsdp, own, D * 2 // n_fsdp)
        both = jnp.where(first, gain1_term, 0.0) + jnp.where(second, gain2_ref[...], 0.0)
        gain_rows = dot_t(both.astype(BF), slot_matrix(owner, inner, own, 256))
        extra = grads_ref.shape[0] - count
        grads_ref[count:, :] = jnp.zeros((extra, grads_ref.shape[1]), BF)
        gain_rows = jnp.concatenate([gain_rows, jnp.zeros((extra - n_fsdp, 256), F32)], axis=0)
        grads_ref[count:, :256] = gain_rows.astype(BF)

    return kernel


def make_terms(n_far, n_sub, own, padded, count):
    def kernel(place_ref, rows_ref, gains_ref, *refs):
        att_refs = refs[:n_sub]
        grad_h1_refs = refs[n_sub : 2 * n_sub]
        grads_refs = refs[2 * n_sub : 3 * n_sub]
        keep_ref, send_ref = refs[3 * n_sub :]
        half_ff = FF // 2
        rows = keep_ref.shape[0] * 2
        wide = grad_h1_refs[0].shape[1]

        def tokens(pieces):
            return jnp.concatenate(pieces, axis=0)

        spot = lax.broadcasted_iota(jnp.int32, (wide, rows), 1)
        source = (spot // padded * n_sub + place_ref[2]) * padded + spot % padded
        select = (lax.broadcasted_iota(jnp.int32, (wide, rows), 0) == source).astype(F32).astype(BF)
        spot = lax.broadcasted_iota(jnp.int32, (D, rows), 1)
        block = spot // padded
        owner = ((block % n_far * 2 + block // n_far) ^ place_ref[0]) * n_sub + place_ref[2]
        source = jnp.where(spot % padded < own, owner * own + spot % padded, -1)
        select_d = (lax.broadcasted_iota(jnp.int32, (D, rows), 0) == source).astype(F32).astype(BF)
        group = rows_ref[...].astype(F32)
        scale = lax.rsqrt(jnp.sum(group * group, axis=1, keepdims=True) * (1.0 / D) + EPS)
        gain = dot_f(gains_ref[...].astype(BF), select)[0:1, :]
        left1 = (dot_f(rows_ref[...], select_d) * scale * gain).astype(BF)
        left2 = dot_f(tokens([ref[...] for ref in grad_h1_refs]), select).astype(BF)
        right = tokens([ref[:count, :] for ref in grads_refs])
        extra = tokens([ref[count:, :256] for ref in grads_refs])
        spot = lax.broadcasted_iota(jnp.int32, (extra.shape[0], rows), 1)
        block = spot // padded
        here = lax.broadcasted_iota(jnp.int32, spot.shape, 0) % (extra.shape[0] // n_sub)
        wanted = jnp.where(spot % padded == own, block % n_far * 2 + block // n_far, -1)
        spots = (here == wanted).astype(F32).astype(BF)
        q_term = dot_0(left1, right)
        start = q_term[:, :256] + dot_0(spots, extra)
        o_term = dot_0(left2, tokens([ref[...] for ref in att_refs]))
        mixed = o_term[:, :128] + q_term[:, half_ff + 256 :]
        for ref, at in ((keep_ref, 0), (send_ref, rows // 2)):
            to = slice(at, at + rows // 2)
            ref[:, :256] = start[to, :].astype(BF)
            ref[:, 256:half_ff] = q_term[to, 256:half_ff].astype(BF)
            ref[:, half_ff : half_ff + 256] = q_term[to, half_ff : half_ff + 256].astype(BF)
            ref[:, half_ff + 256 : half_ff + 384] = mixed[to, :].astype(BF)
            ref[:, half_ff + 384 :] = o_term[to, 128:].astype(BF)

    return kernel


VMEM = pl.BlockSpec(memory_space=pltpu.VMEM)
SMEM = pl.BlockSpec(memory_space=pltpu.SMEM)


def run_kernel(kernel, outs, args, scratch=(), name=None):
    return pl.pallas_call(
        kernel,
        out_shape=[jax.ShapeDtypeStruct(shape, kind) for shape, kind in outs],
        in_specs=[SMEM] + [VMEM] * (len(args) - 1),
        out_specs=[VMEM] * len(outs),
        scratch_shapes=scratch,
        compiler_params=pltpu.CompilerParams(vmem_limit_bytes=56 << 20),
        cost_estimate=pl.CostEstimate(flops=1000, transcendentals=0, bytes_accessed=1000),
        name=name,
    )(*args)


def body(rows, cotangent, lengths, gains, attn_weight, gate_weight, up_weight, down_weight):
    count = rows.shape[0]
    n_fsdp = lax.axis_size("fsdp")
    n_sub = lax.axis_size("sub")
    n_all = n_fsdp * n_sub
    n_far = n_fsdp // 2
    own = D // n_all
    padded = -(-(own + 1) // 16) * 16
    wide = n_all * padded
    half_ff = FF // 2
    quarter = FF // 4
    share = gains.shape[0]
    kv_width = KV * HD
    my_fsdp = lax.axis_index("fsdp")
    my_sub = lax.axis_index("sub")
    my_y = my_sub // 2
    my_c = my_sub % 2

    column = jnp.arange(wide, dtype=jnp.int32)
    place = column // padded
    inner = column % padded
    rel = (place // n_sub) % n_far * 2 + place // (n_sub * n_far)
    real = inner < own
    source = jnp.where(real, ((rel ^ my_fsdp) * n_sub + place % n_sub) * own + inner, -1)
    spread_mat = (jnp.arange(D, dtype=jnp.int32)[:, None] == source[None, :]).astype(BF)

    def padded_block(flat):
        return jnp.pad(flat.reshape(own, FF), ((0, padded - own), (0, 0)))

    def columns(value, index, width):
        return lax.dynamic_slice_in_dim(value, index * width, width, axis=value.ndim - 1)

    position, live, allowed = layout(lengths, count)
    cosine, sine = rope_tables(position, HD)
    cosine = jnp.concatenate([cosine, cosine], axis=1)
    sine = jnp.concatenate([sine, sine], axis=1)
    seg = allowed.astype(F32)
    rows32 = mm(rows, spread_mat)
    cot = (live * cotangent.astype(F32)).astype(BF)
    cot_y = swap(cot, "sub", 2)

    owner = ((rel ^ my_fsdp) * n_sub + place % n_sub)[None, :]

    attn_block = padded_block(attn_weight)
    attn_block = attn_block.at[own, :share].set(gains)
    far = [swap(attn_block, "fsdp", 2 * k) for k in range(1, n_far)]
    mlp_block = jnp.stack([padded_block(w) for w in (gate_weight, up_weight, down_weight)])
    came = swap(columns(mlp_block, 1 - my_y, half_ff), "sub", 2)
    mlp_block = put2(columns(mlp_block, my_y, half_ff), came, my_y, 1)
    came = swap(columns(mlp_block, 1 - my_c, quarter), "sub", 1)
    mlp_block = put2(columns(mlp_block, my_c, quarter), came, my_c, 2)
    mlp_block = mlp_block.reshape(3, n_sub * padded, quarter)
    far, mlp_block, cot, cot_y = meet(far, mlp_block, cot, cot_y)

    attn_far = jnp.stack([attn_block] + list(far))
    half0 = attn_far[:, :, :half_ff]
    half1 = attn_far[:, :, half_ff:]
    gate_up = mlp_block[:2]
    down = mlp_block[2]
    x0, y1, near = swap(half0, "fsdp", 1), swap(half1, "sub", 2), swap(gate_up, "fsdp", 2)
    cot = jnp.concatenate([cot, cot_y])
    cot_c = swap(cot, "sub", 1)
    tables = (owner, inner[None, :])
    angles = (cosine, sine, seg)
    half0, half1, gate_up, down, x0, y1, near, rows32, cot, cot_c, tables, angles = meet(
        half0, half1, gate_up, down, x0, y1, near, rows32, cot, cot_c, tables, angles
    )

    half0 = jnp.stack([half0, x0])
    half1 = put2(half1, y1, my_y, 1)
    y0, x1, third = swap(half0, "sub", 2), swap(half1, "fsdp", 1), swap(gate_up, "fsdp", 4)
    down_x = swap(down, "fsdp", 1)
    cot_all = mm(jnp.concatenate([cot, cot_c]), spread_mat).astype(BF)
    half0, half1, gate_up, down, down_x, near, y0, x1, third, cot_all, rows = meet(
        half0, half1, gate_up, down, down_x, near, y0, x1, third, cot_all, rows
    )
    grad_outb = cot_all[:count]

    half0 = put2(half0, y0, my_y, 2).reshape(wide // 2, half_ff)
    half1 = jnp.stack([half1, x1]).reshape(wide // 2, half_ff)
    c0, c1, last = swap(half0, "sub", 1), swap(half1, "sub", 1), swap(third, "fsdp", 2)
    down = jnp.stack([down, down_x])
    rows_y = swap(rows, "sub", 2)
    half0, half1, c0, c1, gate_up, near, third, last, down, rows_y = meet(
        half0, half1, c0, c1, gate_up, near, third, last, down, rows_y
    )
    rows_all = jnp.concatenate([rows, rows_y])

    gate_up = jnp.stack([gate_up, near, third, last])
    gate_up_x = swap(gate_up, "fsdp", 1)
    down_near, down_third = swap(down, "fsdp", 2), swap(down, "fsdp", 4)
    by_fsdp = [(f % 2) * n_far * n_sub + (f // 2) * n_sub for f in range(n_fsdp)]
    my_place = jnp.stack([my_fsdp, my_c, my_sub])
    tall = (count, wide)
    forward = run_kernel(
        make_forward(n_fsdp, own, padded, share, by_fsdp),
        [
            ((count, half_ff - 256), BF),
            ((count, half_ff), BF),
            ((count, 384), BF),
            ((count, KV * GROUP), F32),
            (tall, F32),
            (tall, BF),
            ((2, wide), F32),
            ((wide, half_ff), BF),
            ((wide, half_ff), BF),
        ],
        (my_place, rows32, *tables, *angles, half0, c0, half1, c1),
        name="attn_forward",
    )
    att, qk, values, logsum, hidden1, input2, gains_p, attn_q, attn_o = forward

    in2_y = swap(input2, "sub", 2)
    input2, in2_y, down_near, down_third = meet(input2, in2_y, down_near, down_third)
    down_last = swap(down_third, "fsdp", 2)
    in2_all = jnp.stack([input2, in2_y])
    in2_c = swap(in2_all, "sub", 1)
    rows_c = swap(rows_all, "sub", 1)
    in2_c, gate_up_x, rows_c = meet(in2_c, gate_up_x, rows_c)
    rows_all = jnp.concatenate([rows_all, rows_c])
    att_y = swap(att, "sub", 2)
    in2_all = jnp.stack([in2_all, in2_c]).reshape(4 * count, wide)
    gate_w = jnp.stack([gate_up[:, 0], gate_up_x[:, 0]]).reshape(wide, quarter)
    up_w = jnp.stack([gate_up[:, 1], gate_up_x[:, 1]]).reshape(wide, quarter)
    gate = mm(in2_all, gate_w)
    up = mm(in2_all, up_w)
    sigma = jax.nn.sigmoid(gate)
    active = gate * sigma
    hidden = (active * up).astype(BF)
    hidden, att_y, down_last = meet(hidden, att_y, down_last)
    down_term = term(cot_all, hidden).reshape(2, n_far, n_sub * padded, quarter)
    down_w = jnp.stack([down, down_near, down_third, down_last])
    down_w = down_w.transpose(1, 0, 2, 3).reshape(wide, quarter)
    down_near_came = swap(far_pair(down_term, 1, 1), "fsdp", 2)
    grad_hidden = mm(after(cot_all, down_term), down_w)
    grad_gate = (grad_hidden * up * sigma * (1.0 + gate * (1.0 - sigma))).astype(BF)
    grad_up = (grad_hidden * active).astype(BF)
    grad_in2 = (mm_t(grad_gate, gate_w) + mm_t(grad_up, up_w)).astype(BF).reshape(2, 2 * count, wide)
    gate_up_term = [
        term(in2_all, grad).reshape(2, n_far, n_sub * padded, quarter) for grad in (grad_gate, grad_up)
    ]
    gate_up_x_came = [swap(part[1], "fsdp", 1) for part in gate_up_term]
    result = mm_t(hidden, down_w).astype(BF).reshape(2, 2 * count, wide)

    came = swap(grad_in2[1], "sub", 1)
    atts = [att, att_y, swap(att, "sub", 1), swap(att_y, "sub", 1)]
    came, atts = meet(came, atts)
    grad_in2 = add2(grad_in2[0], came).reshape(2, count, wide)
    grad_in2_y = swap(grad_in2[1], "sub", 2)
    grad_h1, grad_h1b, gain2_term = run_kernel(
        norm_kernel,
        [(tall, F32), (tall, BF), ((1, wide), F32)],
        (my_place, grad_in2[0], grad_in2_y, grad_outb, hidden1, gains_p),
        name="norm_backward",
    )
    grad_h1_y = swap(grad_h1b, "sub", 2)
    grad_h1, down_near_came = meet(grad_h1, down_near_came)
    down_held = add2(far_pair(down_term, 1, 0), down_near_came)
    down_far_came = swap(down_held[:, 1], "fsdp", 4)
    grads, input_grad = run_kernel(
        make_backward(n_fsdp, own),
        [((count + 16, half_ff + 384), BF), (tall, F32)],
        (
            my_place, grad_h1, grad_h1b, gain2_term, rows32, gains_p, *tables, *angles,
            qk, values, logsum, attn_q, attn_o,
        ),
        scratch=[pltpu.VMEM((count, half_ff), F32)],
        name="attn_backward",
    )

    grads_y = swap(grads, "sub", 2)
    grads_c = swap(grads, "sub", 1)
    grads, grad_h1_y, gate_up_x_came, down_far_came = meet(
        grads, grad_h1_y, gate_up_x_came, down_far_came
    )
    grad_h1_c, grad_h1_yc = swap(grad_h1b, "sub", 1), swap(grad_h1_y, "sub", 1)
    gate_up_held = jnp.stack([add2(part[0], came) for part, came in zip(gate_up_term, gate_up_x_came)])
    gate_up_near = swap(far_pair(gate_up_held, 1, 1), "fsdp", 2)
    down_held = add2(down_held[:, 0], down_far_came)
    down_x_came = swap(down_held[1], "fsdp", 1)
    grads_y, grads_c, grad_h1_c, grad_h1_yc, down_x_came = meet(
        grads_y, grads_c, grad_h1_c, grad_h1_yc, down_x_came
    )

    grads_yc = swap(grads_y, "sub", 1)
    res_c = swap(after(result[1], grads_y), "sub", 1)
    attn_keep, attn_send = run_kernel(
        make_terms(n_far, n_sub, own, padded, count),
        [((n_far * padded, FF), BF)] * 2,
        (
            my_place, rows_all, gains_p, *atts, grad_h1b, grad_h1_y, grad_h1_c, grad_h1_yc, grads, grads_y, grads_c, grads_yc,
        ),
        name="attn_terms",
    )

    attn_x = swap(attn_send, "fsdp", 1)
    gate_up_held = add2(far_pair(gate_up_held, 1, 0), after(gate_up_near, attn_send))
    gate_up_far = swap(gate_up_held[:, 1], "fsdp", 4)
    result = add2(result[0], res_c).reshape(2, count, wide)
    res_y = swap(result[1], "sub", 2)
    input_grad = after(input_grad, attn_send)
    input_grad = lax.dot_general(
        input_grad,
        spread_mat.astype(F32),
        (((1,), (1,)), ((), ())),
        precision=lax.Precision.HIGHEST,
    )
    attn_x, gate_up_far, input_grad, res_y = meet(attn_x, gate_up_far, input_grad, res_y)

    def side_by_side(mine, came, bit):
        first = bit == 0
        return jnp.concatenate([jnp.where(first, mine, came), jnp.where(first, came, mine)], axis=-1)

    attn_held = add2(attn_keep, attn_x).reshape(n_far, padded, FF)
    attn_near = swap(far_pair(attn_held, 0, 1), "fsdp", 2)
    down_own = add2(down_held[0], down_x_came)[None]
    mlp_own = jnp.concatenate([add2(gate_up_held[:, 0], gate_up_far), down_own])
    mlp_own = mlp_own.reshape(3, 2, 2, padded, quarter)
    mlp_c = swap(pick(mlp_own, 1 - my_c, 2), "sub", 1)
    attn_near, mlp_c = meet(attn_near, mlp_c)
    mlp_own = side_by_side(pick(mlp_own, my_c, 2), mlp_c, my_c)
    mlp_y = swap(pick(mlp_own, 1 - my_y, 1), "sub", 2)
    attn_held = add2(far_pair(attn_held, 0, 0), attn_near)
    attn_far = swap(attn_held[1], "fsdp", 4)
    result = hidden1 + result[0].astype(F32) + res_y.astype(F32)
    output = mm_t((live * result).astype(BF), spread_mat).astype(BF)
    mlp_own = side_by_side(pick(mlp_own, my_y, 1), mlp_y, my_y)

    def flat(part):
        return part[:own].astype(F32).reshape(-1)

    mlp_flat = [flat(mlp_own[i]) for i in range(3)]
    attn_far, mlp_flat, output = meet(attn_far, mlp_flat, output)
    attn_own = add2(attn_held[0], attn_far)
    gain_grad = attn_own[own, :share].astype(F32)
    return (
        output,
        input_grad,
        flat(attn_own),
        *mlp_flat,
        gain_grad,
    )


def solution(mesh):
    n_fsdp, n_sub = mesh.shape["fsdp"], mesh.shape["sub"]
    n_all = n_fsdp * n_sub
    by_rows = (
        n_fsdp == 8 and D % n_all == 0 and n_fsdp & (n_fsdp - 1) == 0 and n_fsdp > 1 and n_sub == 4 and D // n_fsdp % (D // n_all) == 0
    )
    in_specs = (
        P(("fsdp", "sub"), None),
        P(("fsdp", "sub"), None),
        P(("fsdp", "sub")),
        P("fsdp"),
        P(("fsdp", "sub")),
        P(("fsdp", "sub")),
        P(("fsdp", "sub")),
        P(("fsdp", "sub")),
    )
    out_specs = (
        P(("fsdp", "sub"), None),
        P(("fsdp", "sub"), None),
        P(("fsdp", "sub")),
        P(("fsdp", "sub")),
        P(("fsdp", "sub")),
        P(("fsdp", "sub")),
        P("fsdp"),
    )
    return jax.shard_map(body if by_rows else plain_body, mesh=mesh, in_specs=in_specs, out_specs=out_specs, check_vma=False)
```

```python
import jax
import jax.numpy as jnp
from jax import lax
from jax.experimental import pallas as pl
from jax.experimental.pallas import tpu as pltpu
from jax.sharding import PartitionSpec as P

D = 960
KV = 5
HD = 64
FF = 2560
GROUP = 3


EPS = 1e-05
THETA = 100000.0
NEG = -1e30
piece_width = 64


def rope_tables(position, width):
    half = jnp.arange(width // 2, dtype=jnp.float32)
    inverse = jnp.exp(-(2.0 * half / width) * jnp.log(jnp.float32(THETA)))
    angle = position.astype(jnp.float32)[:, None] * inverse[None, :]
    cosine = jnp.concatenate([jnp.cos(angle), jnp.cos(angle)], axis=1)
    sine = jnp.concatenate([jnp.sin(angle), jnp.sin(angle)], axis=1)
    return (cosine, sine)


def rotate(values, cosine, sine):
    half = values.shape[-1] // 2
    turned = jnp.concatenate([-values[..., half:], values[..., :half]], axis=-1)
    return values * cosine + turned * sine


def unrotate(grads, cosine, sine):
    half = grads.shape[-1] // 2
    scaled = grads * sine
    return grads * cosine + jnp.concatenate([scaled[..., half:], -scaled[..., :half]], axis=-1)


def norm_forward(values):
    scale = lax.rsqrt(jnp.mean(values * values, axis=1, keepdims=True) + EPS)
    return (values * scale, scale)


def norm_backward(grad_in, normed, scale, gain):
    gain_term = jnp.sum(grad_in * normed, axis=0)
    inner = grad_in * gain[None, :]
    back = scale * (inner - normed * jnp.mean(inner * normed, axis=1, keepdims=True))
    return (back, gain_term)


def layout(block_lengths, count):
    slots = jnp.arange(count, dtype=jnp.int32)
    first = block_lengths[0]
    second = block_lengths[1]
    segment = (slots >= first).astype(jnp.int32) + (slots >= first + second).astype(jnp.int32)
    position = (
        slots - first * (segment >= 1).astype(jnp.int32) - second * (segment >= 2).astype(jnp.int32)
    )
    live = (segment < 2).astype(jnp.float32)[:, None]
    allowed = (segment[:, None] == segment[None, :]) & (slots[None, :] <= slots[:, None])
    return (position, live, allowed)


def masked_scores(queries, keys, allowed):
    scores = jnp.einsum(
        "qkgd,jkd->kgqj", queries, keys, preferred_element_type=jnp.float32
    ) * HD ** (-0.5)
    return jnp.where(allowed[None, None], scores, NEG)


def attend(projected, cosine, sine, allowed, count):
    kv_width = KV * HD
    queries = rotate(
        projected[:, :D].reshape(count, KV, GROUP, HD),
        cosine[:, None, None, :],
        sine[:, None, None, :],
    ).astype(jnp.bfloat16)
    keys = rotate(
        projected[:, D : D + kv_width].reshape(count, KV, HD), cosine[:, None, :], sine[:, None, :]
    ).astype(jnp.bfloat16)
    values = projected[:, D + kv_width :].reshape(count, KV, HD).astype(jnp.bfloat16)
    scores = masked_scores(queries, keys, allowed)
    top = jnp.max(scores, axis=-1, keepdims=True)
    expo = jnp.exp(scores - top)
    total = jnp.sum(expo, axis=-1, keepdims=True)
    logsum = top + jnp.log(total)
    weights = (expo / total).astype(jnp.bfloat16)
    attended = (
        jnp.einsum("kgqj,jkd->qkgd", weights, values, preferred_element_type=jnp.float32)
        .reshape(count, D)
        .astype(jnp.bfloat16)
    )
    return (queries, keys, values, logsum, attended)


def attend_back(grad_att, queries, keys, values, logsum, allowed, cosine, sine, count):
    kv_width = KV * HD
    probs = jnp.exp(masked_scores(queries, keys, allowed) - logsum)
    probs_b = probs.astype(jnp.bfloat16)
    value_grad = jnp.einsum("kgqj,qkgd->jkd", probs_b, grad_att, preferred_element_type=jnp.float32)
    prob_grad = jnp.einsum("qkgd,jkd->kgqj", grad_att, values, preferred_element_type=jnp.float32)
    delta = jnp.sum(probs * prob_grad, axis=-1, keepdims=True)
    score_grad = (probs * (prob_grad - delta) * HD ** (-0.5)).astype(jnp.bfloat16)
    query_grad = jnp.einsum("kgqj,jkd->qkgd", score_grad, keys, preferred_element_type=jnp.float32)
    key_grad = jnp.einsum("kgqj,qkgd->jkd", score_grad, queries, preferred_element_type=jnp.float32)
    query_grad = unrotate(query_grad, cosine[:, None, None, :], sine[:, None, None, :])
    key_grad = unrotate(key_grad, cosine[:, None, :], sine[:, None, :])
    return jnp.concatenate(
        [
            query_grad.reshape(count, D),
            key_grad.reshape(count, kv_width),
            value_grad.reshape(count, kv_width),
        ],
        axis=1,
    ).astype(jnp.bfloat16)


def collect(attn_flat, gate_flat, up_flat, down_flat):
    whole = (
        lax.all_gather(attn_flat, ("fsdp", "sub"), axis=0, tiled=True),
        lax.all_gather(gate_flat, ("fsdp", "sub"), axis=0, tiled=True),
        lax.all_gather(up_flat, ("fsdp", "sub"), axis=0, tiled=True),
        lax.all_gather(down_flat, ("fsdp", "sub"), axis=0, tiled=True),
    )
    return tuple((piece.reshape(D, FF) for piece in whole))


def flat_terms(pair_lists, count):
    results = []
    for pairs in pair_lists:
        blocks = [
            jnp.dot(left.T, right, preferred_element_type=jnp.float32) for left, right in pairs
        ]
        joined = blocks[0] if len(blocks) == 1 else jnp.concatenate(blocks, axis=1)
        results.append(joined.reshape(-1).reshape(count, piece_width))
    return jnp.concatenate(results, axis=1)


def split_owned(owned):
    return tuple(
        (
            owned[:, index * piece_width : (index + 1) * piece_width].reshape(-1)
            for index in range(4)
        )
    )


def spread(pair_lists):
    share = D * FF // (piece_width * lax.axis_size("fsdp") * lax.axis_size("sub"))
    owned = lax.psum_scatter(
        flat_terms(pair_lists, share * lax.axis_size(("fsdp", "sub"))),
        ("fsdp", "sub"),
        scatter_dimension=0,
        tiled=True,
    )
    return split_owned(owned)


def flat_path(
    rows32,
    cotangent,
    live,
    allowed,
    cosine,
    sine,
    gain_attn,
    gain_mlp,
    normed1,
    scale1,
    input1,
    flats,
):
    count = rows32.shape[0]
    q_width = D + 2 * KV * HD
    attn_mat, gate_mat, up_mat, down_mat = collect(flats[0], flats[1], flats[2], flats[3])
    projected = jnp.dot(input1, attn_mat[:, :q_width], preferred_element_type=jnp.float32)
    queries, keys, values, logsum, attended = attend(projected, cosine, sine, allowed, count)
    hidden1 = rows32 + jnp.dot(
        attended, attn_mat[:, q_width:].T, preferred_element_type=jnp.float32
    )
    normed2, scale2 = norm_forward(hidden1)
    input2 = (normed2 * gain_mlp[None, :]).astype(jnp.bfloat16)
    gate = jnp.dot(input2, gate_mat, preferred_element_type=jnp.float32)
    up = jnp.dot(input2, up_mat, preferred_element_type=jnp.float32)
    sigma = jax.nn.sigmoid(gate)
    active = gate * sigma
    hidden = (active * up).astype(jnp.bfloat16)
    result = hidden1 + jnp.dot(hidden, down_mat.T, preferred_element_type=jnp.float32)
    output = (live * result).astype(jnp.bfloat16)
    attn_back, gate_back, up_back, down_back = collect(flats[0], flats[1], flats[2], flats[3])
    grad_out = live * cotangent.astype(jnp.float32)
    grad_outb = grad_out.astype(jnp.bfloat16)
    grad_hidden = jnp.dot(grad_outb, down_back, preferred_element_type=jnp.float32)
    grad_gate = (grad_hidden * up * sigma * (1.0 + gate * (1.0 - sigma))).astype(jnp.bfloat16)
    grad_up = (grad_hidden * active).astype(jnp.bfloat16)
    grad_in2 = jnp.dot(grad_gate, gate_back.T, preferred_element_type=jnp.float32) + jnp.dot(
        grad_up, up_back.T, preferred_element_type=jnp.float32
    )
    back2, gain2_term = norm_backward(grad_in2, normed2, scale2, gain_mlp)
    grad_h1 = grad_out + back2
    grad_h1b = grad_h1.astype(jnp.bfloat16)
    grad_att = (
        jnp.dot(grad_h1b, attn_back[:, q_width:], preferred_element_type=jnp.float32)
        .astype(jnp.bfloat16)
        .reshape(count, KV, GROUP, HD)
    )
    proj_grad = attend_back(grad_att, queries, keys, values, logsum, allowed, cosine, sine, count)
    grad_in1 = jnp.dot(proj_grad, attn_back[:, :q_width].T, preferred_element_type=jnp.float32)
    back1, gain1_term = norm_backward(grad_in1, normed1, scale1, gain_attn)
    input_grad = grad_h1 + back1
    pair_lists = (
        ((input1, proj_grad), (grad_h1b, attended)),
        ((input2, grad_gate),),
        ((input2, grad_up),),
        ((grad_outb, hidden),),
    )
    owned = spread(pair_lists)
    return (output, input_grad, owned, gain1_term, gain2_term)


def plain_body(rows, cotangent, lengths, gains, attn_weight, gate_weight, up_weight, down_weight):
    count = rows.shape[0]
    position, live, allowed = layout(lengths, count)
    cosine, sine = rope_tables(position, HD)
    full_gains = lax.all_gather(gains, "fsdp", axis=0, tiled=True).astype(jnp.float32)
    gain_attn = full_gains[:D]
    gain_mlp = full_gains[D:]
    rows32 = rows.astype(jnp.float32)
    normed1, scale1 = norm_forward(rows32)
    input1 = (normed1 * gain_attn[None, :]).astype(jnp.bfloat16)
    flats = (attn_weight, gate_weight, up_weight, down_weight)
    output, input_grad, owned, gain1_term, gain2_term = flat_path(
        rows32,
        cotangent,
        live,
        allowed,
        cosine,
        sine,
        gain_attn,
        gain_mlp,
        normed1,
        scale1,
        input1,
        flats,
    )
    gain_total = lax.psum(jnp.concatenate([gain1_term, gain2_term]), ("fsdp", "sub"))
    share = gains.shape[0]
    gain_grad = lax.dynamic_slice_in_dim(gain_total, lax.axis_index("fsdp") * share, share)
    return (output, input_grad, owned[0], owned[1], owned[2], owned[3], gain_grad)


BF = jnp.bfloat16
F32 = jnp.float32


def swap(value, axis, bit):
    return lax.ppermute(value, axis, [(i, i ^ bit) for i in range(lax.axis_size(axis))])


def meet(*values):
    return lax.optimization_barrier(values)


def after(value, *done):
    return lax.optimization_barrier((value, *done))[0]


def add2(kept, came):
    return (kept.astype(F32) + came.astype(F32)).astype(BF)


def far_pair(value, axis, odd):
    shape = value.shape
    value = value.reshape(shape[:axis] + (shape[axis] // 2, 2) + shape[axis + 1 :])
    return lax.index_in_dim(value, odd, axis + 1, keepdims=False)


def pick(value, index, axis):
    return lax.dynamic_index_in_dim(value, index, axis, keepdims=False)


def put2(own, came, bit, axis):
    first = bit == 0
    return jnp.stack([jnp.where(first, own, came), jnp.where(first, came, own)], axis=axis)


def mm(a, b):
    return jnp.dot(a, b, preferred_element_type=F32)


def mm_t(a, b):
    return lax.dot_general(a, b, (((1,), (1,)), ((), ())), preferred_element_type=F32)


def term(a, b):
    return lax.dot_general(a, b, (((0,), (0,)), ((), ())), preferred_element_type=F32).astype(BF)


def dot_f(a, b):
    return lax.dot_general(a, b, (((1,), (0,)), ((), ())), preferred_element_type=F32)


def dot_t(a, b):
    return lax.dot_general(a, b, (((1,), (1,)), ((), ())), preferred_element_type=F32)


def dot_0(a, b):
    return lax.dot_general(a, b, (((0,), (0,)), ((), ())), preferred_element_type=F32)


def norm_rows(values):
    mean = jnp.sum(values * values, axis=1, keepdims=True) * (1.0 / D)
    scale = lax.rsqrt(mean + EPS)
    return values * scale, scale


def norm_rows_back(grad_in, normed, scale, gain):
    gain_term = jnp.sum(grad_in * normed, axis=0, keepdims=True)
    inner = grad_in * gain
    mean = jnp.sum(inner * normed, axis=1, keepdims=True) * (1.0 / D)
    return scale * (inner - normed * mean), gain_term


def first_half(shape):
    return lax.broadcasted_iota(jnp.int32, shape, 1) % HD < HD // 2


def gain_masks(owner, my_fsdp, n_fsdp, own, share):
    wide = owner.shape[1]
    per = share // own
    place = lax.broadcasted_iota(jnp.int32, (n_fsdp, wide), 0) ^ my_fsdp
    group = owner // per
    return place == group, place == group + n_fsdp // 2


def slot_matrix(owner, inner, own, height):
    per = D * 2 // 8 // own
    slot = jnp.where(inner < own, owner % per * own + inner, -1)
    return (lax.broadcasted_iota(jnp.int32, (height, owner.shape[1]), 0) == slot).astype(F32).astype(BF)


def make_forward(n_fsdp, own, padded, share, by_fsdp):
    kv_width = KV * HD

    def kernel(
        place_ref, rows_ref, owner_ref, inner_ref, cos_ref, sin_ref, seg_ref,
        own_q_ref, came_q_ref, own_o_ref, came_o_ref,
        att_ref, qk_ref, v_ref, logsum_ref, hidden1_ref, input2_ref, gains_ref, attn_q_ref, attn_o_ref,
    ):
        core = place_ref[1]
        for p in range(own_q_ref.shape[0] // padded):
            here = pl.ds(pl.multiple_of((2 * p + core) * padded, padded), padded)
            there = pl.ds(pl.multiple_of((2 * p + 1 - core) * padded, padded), padded)
            block = slice(p * padded, (p + 1) * padded)
            attn_q_ref[here, :] = own_q_ref[block, :]
            attn_q_ref[there, :] = came_q_ref[block, :]
            attn_o_ref[here, :] = own_o_ref[block, :]
            attn_o_ref[there, :] = came_o_ref[block, :]
        pieces = jnp.concatenate(
            [attn_q_ref[p * padded + own : p * padded + own + 1, :share].astype(F32) for p in by_fsdp], axis=0
        ).astype(BF)
        owner = owner_ref[...]
        first, second = gain_masks(owner, place_ref[0], n_fsdp, own, share)
        spots = dot_f(pieces, slot_matrix(owner, inner_ref[...], own, share))
        gain1 = jnp.sum(jnp.where(first, spots, 0.0), axis=0, keepdims=True)
        gain2 = jnp.sum(jnp.where(second, spots, 0.0), axis=0, keepdims=True)
        gains_ref[0:1, :] = gain1
        gains_ref[1:2, :] = gain2
        rows = rows_ref[...]
        normed, _ = norm_rows(rows)
        input1 = (normed * gain1).astype(BF)
        projected = dot_f(input1, attn_q_ref[...])
        cosine = cos_ref[...]
        sine = sin_ref[...]
        low = first_half(cosine.shape)
        for i in range(projected.shape[1] // 128):
            part = projected[:, 128 * i : 128 * (i + 1)]
            turned = jnp.where(low, -pltpu.roll(part, 96, 1), pltpu.roll(part, 32, 1))
            qk_ref[:, 128 * i : 128 * (i + 1)] = (part * cosine + turned * sine).astype(BF)
        values = dot_f(input1, attn_o_ref[:, :384]).astype(BF)
        v_ref[...] = values
        allowed = seg_ref[...] > 0.0
        att_ref[:, :128] = jnp.zeros((rows.shape[0], 128), BF)
        shift = kv_width - 256
        for k in range(KV):
            keys = qk_ref[:, D + HD * k : D + HD * (k + 1)]
            value = values[:, HD * k : HD * (k + 1)]
            for g in range(GROUP):
                h = GROUP * k + g
                queries = qk_ref[:, HD * h : HD * (h + 1)]
                scores = jnp.where(allowed, dot_t(queries, keys) * HD ** (-0.5), NEG)
                top = jnp.max(scores, axis=1, keepdims=True)
                expo = jnp.exp(scores - top)
                total = jnp.sum(expo, axis=1, keepdims=True)
                logsum_ref[:, h : h + 1] = top + jnp.log(total)
                weights = (expo / total).astype(BF)
                att_ref[:, shift + HD * h : shift + HD * (h + 1)] = dot_f(weights, value).astype(BF)
        hidden1 = rows + dot_t(att_ref[...], attn_o_ref[:, 256:])
        hidden1_ref[...] = hidden1
        normed2, _ = norm_rows(hidden1)
        input2_ref[...] = (normed2 * gain2).astype(BF)

    return kernel


def norm_kernel(
    place_ref, grad_a_ref, grad_b_ref, grad_out_ref, hidden1_ref, gains_ref,
    grad_h1_ref, grad_h1b_ref, gain2_ref,
):
    grad_in2 = grad_a_ref[...].astype(F32) + grad_b_ref[...].astype(F32)
    normed2, scale2 = norm_rows(hidden1_ref[...])
    back2, gain2_term = norm_rows_back(grad_in2, normed2, scale2, gains_ref[1:2, :])
    grad_h1 = grad_out_ref[: hidden1_ref.shape[0], :].astype(F32) + back2
    grad_h1_ref[...] = grad_h1
    grad_h1b_ref[...] = grad_h1.astype(BF)
    gain2_ref[...] = gain2_term


def make_backward(n_fsdp, own):
    kv_width = KV * HD

    def kernel(
        place_ref, grad_h1_ref, grad_h1b_ref, gain2_ref, rows_ref, gains_ref, owner_ref, inner_ref,
        cos_ref, sin_ref, seg_ref, qk_ref, v_ref, logsum_ref, attn_q_ref, attn_o_ref,
        grads_ref, input_grad_ref,
        turn_ref,
    ):
        count = rows_ref.shape[0]
        qk_width = turn_ref.shape[1]
        grad_att = dot_f(grad_h1b_ref[...], attn_o_ref[...]).astype(BF)
        allowed = seg_ref[...] > 0.0
        grads_ref[:count, qk_width:] = jnp.zeros((count, 384), BF)
        for k in range(KV):
            keys = qk_ref[:, D + HD * k : D + HD * (k + 1)]
            value = v_ref[:, HD * k : HD * (k + 1)]
            value_grad = jnp.zeros((count, HD), F32)
            key_grad = jnp.zeros((count, HD), F32)
            for g in range(GROUP):
                h = GROUP * k + g
                queries = qk_ref[:, HD * h : HD * (h + 1)]
                grad = grad_att[:, kv_width + HD * h : kv_width + HD * (h + 1)]
                scores = jnp.where(allowed, dot_t(queries, keys) * HD ** (-0.5), NEG)
                probs = jnp.exp(scores - logsum_ref[:, h : h + 1])
                value_grad = value_grad + dot_0(probs.astype(BF), grad)
                prob_grad = dot_t(grad, value)
                delta = jnp.sum(probs * prob_grad, axis=1, keepdims=True)
                score_grad = (probs * (prob_grad - delta) * HD ** (-0.5)).astype(BF)
                turn_ref[:, HD * h : HD * (h + 1)] = dot_f(score_grad, keys)
                key_grad = key_grad + dot_0(score_grad, queries)
            turn_ref[:, D + HD * k : D + HD * (k + 1)] = key_grad
            grads_ref[:count, qk_width + HD * k : qk_width + HD * (k + 1)] = value_grad.astype(BF)
        cosine = cos_ref[...]
        sine = sin_ref[...]
        low = first_half(cosine.shape)
        for i in range(qk_width // 128):
            part = turn_ref[:, 128 * i : 128 * (i + 1)]
            scaled = part * sine
            turned = jnp.where(low, pltpu.roll(scaled, 96, 1), -pltpu.roll(scaled, 32, 1))
            grads_ref[:count, 128 * i : 128 * (i + 1)] = (part * cosine + turned).astype(BF)
        owner = owner_ref[...]
        inner = inner_ref[...]
        grad_in1 = dot_t(grads_ref[:count, :qk_width], attn_q_ref[...]) * jnp.where(inner < own, 1.0, 0.0)
        grad_in1 = grad_in1 + dot_t(grads_ref[:count, qk_width:], attn_o_ref[:, :384])
        normed1, scale1 = norm_rows(rows_ref[...])
        back1, gain1_term = norm_rows_back(grad_in1, normed1, scale1, gains_ref[0:1, :])
        input_grad_ref[...] = grad_h1_ref[...] + back1
        first, second = gain_masks(owner, place_ref[0], n_fsdp, own, D * 2 // n_fsdp)
        both = jnp.where(first, gain1_term, 0.0) + jnp.where(second, gain2_ref[...], 0.0)
        gain_rows = dot_t(both.astype(BF), slot_matrix(owner, inner, own, 256))
        extra = grads_ref.shape[0] - count
        grads_ref[count:, :] = jnp.zeros((extra, grads_ref.shape[1]), BF)
        gain_rows = jnp.concatenate([gain_rows, jnp.zeros((extra - n_fsdp, 256), F32)], axis=0)
        grads_ref[count:, :256] = gain_rows.astype(BF)

    return kernel


def make_terms(n_far, n_sub, own, padded, count):
    def kernel(place_ref, rows_a_ref, rows_b_ref, gains_ref, *refs):
        att_refs = refs[:n_sub]
        grad_h1_refs = refs[n_sub : 2 * n_sub]
        grads_refs = refs[2 * n_sub : 3 * n_sub]
        keep_ref, send_ref = refs[3 * n_sub :]
        half_ff = FF // 2
        rows = keep_ref.shape[0] * 2
        wide = grad_h1_refs[0].shape[1]

        def tokens(pieces):
            return jnp.concatenate(pieces, axis=0)

        spot = lax.broadcasted_iota(jnp.int32, (wide, rows), 1)
        source = (spot // padded * n_sub + place_ref[2]) * padded + spot % padded
        select = (lax.broadcasted_iota(jnp.int32, (wide, rows), 0) == source).astype(F32).astype(BF)
        spot = lax.broadcasted_iota(jnp.int32, (D, rows), 1)
        block = spot // padded
        owner = ((block % n_far * 2 + block // n_far) ^ place_ref[0]) * n_sub + place_ref[2]
        source = jnp.where(spot % padded < own, owner * own + spot % padded, -1)
        select_d = (lax.broadcasted_iota(jnp.int32, (D, rows), 0) == source).astype(F32).astype(BF)
        rows_b = jnp.concatenate([rows_a_ref[...], rows_b_ref[...]], axis=0)
        group = rows_b.astype(F32)
        scale = lax.rsqrt(jnp.sum(group * group, axis=1, keepdims=True) * (1.0 / D) + EPS)
        gain = dot_f(gains_ref[...].astype(BF), select)[0:1, :]
        left1 = (dot_f(rows_b, select_d) * scale * gain).astype(BF)
        left2 = dot_f(tokens([ref[...] for ref in grad_h1_refs]), select).astype(BF)
        right = tokens([ref[:count, :] for ref in grads_refs])
        extra = tokens([ref[count:, :256] for ref in grads_refs])
        spot = lax.broadcasted_iota(jnp.int32, (extra.shape[0], rows), 1)
        block = spot // padded
        here = lax.broadcasted_iota(jnp.int32, spot.shape, 0) % (extra.shape[0] // n_sub)
        wanted = jnp.where(spot % padded == own, block % n_far * 2 + block // n_far, -1)
        spots = (here == wanted).astype(F32).astype(BF)
        q_term = dot_0(left1, right)
        start = q_term[:, :256] + dot_0(spots, extra)
        o_term = dot_0(left2, tokens([ref[...] for ref in att_refs]))
        mixed = o_term[:, :128] + q_term[:, half_ff + 256 :]
        for ref, at in ((keep_ref, 0), (send_ref, rows // 2)):
            to = slice(at, at + rows // 2)
            ref[:, :256] = start[to, :].astype(BF)
            ref[:, 256:half_ff] = q_term[to, 256:half_ff].astype(BF)
            ref[:, half_ff : half_ff + 256] = q_term[to, half_ff : half_ff + 256].astype(BF)
            ref[:, half_ff + 256 : half_ff + 384] = mixed[to, :].astype(BF)
            ref[:, half_ff + 384 :] = o_term[to, 128:].astype(BF)

    return kernel


VMEM = pl.BlockSpec(memory_space=pltpu.VMEM)
SMEM = pl.BlockSpec(memory_space=pltpu.SMEM)


def run_kernel(kernel, outs, args, scratch=(), name=None):
    return pl.pallas_call(
        kernel,
        out_shape=[jax.ShapeDtypeStruct(shape, kind) for shape, kind in outs],
        in_specs=[SMEM] + [VMEM] * (len(args) - 1),
        out_specs=[VMEM] * len(outs),
        scratch_shapes=scratch,
        compiler_params=pltpu.CompilerParams(vmem_limit_bytes=56 << 20),
        cost_estimate=pl.CostEstimate(flops=1000, transcendentals=0, bytes_accessed=1000),
        name=name,
    )(*args)


def body(rows, cotangent, lengths, gains, attn_weight, gate_weight, up_weight, down_weight):
    count = rows.shape[0]
    n_fsdp = lax.axis_size("fsdp")
    n_sub = lax.axis_size("sub")
    n_all = n_fsdp * n_sub
    n_far = n_fsdp // 2
    own = D // n_all
    padded = -(-(own + 1) // 16) * 16
    wide = n_all * padded
    half_ff = FF // 2
    quarter = FF // 4
    share = gains.shape[0]
    kv_width = KV * HD
    my_fsdp = lax.axis_index("fsdp")
    my_sub = lax.axis_index("sub")
    my_y = my_sub // 2
    my_c = my_sub % 2

    column = jnp.arange(wide, dtype=jnp.int32)
    place = column // padded
    inner = column % padded
    rel = (place // n_sub) % n_far * 2 + place // (n_sub * n_far)
    real = inner < own
    source = jnp.where(real, ((rel ^ my_fsdp) * n_sub + place % n_sub) * own + inner, -1)
    spread_mat = (jnp.arange(D, dtype=jnp.int32)[:, None] == source[None, :]).astype(BF)

    def padded_block(flat):
        return jnp.pad(flat.reshape(own, FF), ((0, padded - own), (0, 0)))

    def columns(value, index, width):
        return lax.dynamic_slice_in_dim(value, index * width, width, axis=value.ndim - 1)

    position, live, allowed = layout(lengths, count)
    cosine, sine = rope_tables(position, HD)
    cosine = jnp.concatenate([cosine, cosine], axis=1)
    sine = jnp.concatenate([sine, sine], axis=1)
    seg = allowed.astype(F32)
    rows32 = mm(rows, spread_mat)

    owner = ((rel ^ my_fsdp) * n_sub + place % n_sub)[None, :]

    attn_block = padded_block(attn_weight)
    attn_block = attn_block.at[own, :share].set(gains)
    far = [swap(attn_block, "fsdp", 2 * k) for k in range(1, n_far)]
    mlp_block = jnp.stack([padded_block(w) for w in (gate_weight, up_weight, down_weight)])
    sent = columns(mlp_block, 1 - my_y, half_ff)
    came = swap(sent, "sub", 2)
    cot = (live * after(cotangent, sent).astype(F32)).astype(BF)
    cot_y = swap(cot, "sub", 2)
    mlp_block = put2(columns(mlp_block, my_y, half_ff), came, my_y, 1)
    came = swap(columns(mlp_block, 1 - my_c, quarter), "sub", 1)
    mlp_block = put2(columns(mlp_block, my_c, quarter), came, my_c, 2)
    mlp_block = mlp_block.reshape(3, n_sub * padded, quarter)
    far, mlp_block, cot, cot_y = meet(far, mlp_block, cot, cot_y)

    attn_far = jnp.stack([attn_block] + list(far))
    half0 = attn_far[:, :, :half_ff]
    half1 = attn_far[:, :, half_ff:]
    gate_up = mlp_block[:2]
    down = mlp_block[2]
    x0, y1, near = swap(half0, "fsdp", 1), swap(half1, "sub", 2), swap(gate_up, "fsdp", 2)
    cot = jnp.concatenate([cot, cot_y])
    cot_c = swap(cot, "sub", 1)
    tables = (owner, inner[None, :])
    angles = (cosine, sine, seg)
    half0, half1, gate_up, down, x0, y1, near, rows32, cot, cot_c, tables, angles = meet(
        half0, half1, gate_up, down, x0, y1, near, rows32, cot, cot_c, tables, angles
    )

    half0 = jnp.stack([half0, x0])
    half1 = put2(half1, y1, my_y, 1)
    y0, x1, third = swap(half0, "sub", 2), swap(half1, "fsdp", 1), swap(gate_up, "fsdp", 4)
    down_x = swap(down, "fsdp", 1)
    cot_all = mm(jnp.concatenate([cot, cot_c]), spread_mat).astype(BF)
    half0, half1, gate_up, down, down_x, near, y0, x1, third, cot_all = meet(
        half0, half1, gate_up, down, down_x, near, y0, x1, third, cot_all
    )

    half0 = put2(half0, y0, my_y, 2).reshape(wide // 2, half_ff)
    half1 = jnp.stack([half1, x1]).reshape(wide // 2, half_ff)
    c0, c1, last = swap(half0, "sub", 1), swap(half1, "sub", 1), swap(third, "fsdp", 2)
    down = jnp.stack([down, down_x])
    rows_y = swap(rows, "sub", 2)
    half0, half1, c0, c1, gate_up, near, third, last, down, rows_y = meet(
        half0, half1, c0, c1, gate_up, near, third, last, down, rows_y
    )
    rows_all = jnp.concatenate([rows, rows_y])

    gate_up = jnp.stack([gate_up, near, third, last])
    gate_up_x = swap(gate_up, "fsdp", 1)
    down_near, down_third = swap(down, "fsdp", 2), swap(down, "fsdp", 4)
    by_fsdp = [(f % 2) * n_far * n_sub + (f // 2) * n_sub for f in range(n_fsdp)]
    my_place = jnp.stack([my_fsdp, my_c, my_sub])
    tall = (count, wide)
    forward = run_kernel(
        make_forward(n_fsdp, own, padded, share, by_fsdp),
        [
            ((count, half_ff - 256), BF),
            ((count, half_ff), BF),
            ((count, 384), BF),
            ((count, KV * GROUP), F32),
            (tall, F32),
            (tall, BF),
            ((2, wide), F32),
            ((wide, half_ff), BF),
            ((wide, half_ff), BF),
        ],
        (my_place, rows32, *tables, *angles, half0, c0, half1, c1),
        name="attn_forward",
    )
    att, qk, values, logsum, hidden1, input2, gains_p, attn_q, attn_o = forward

    in2_y = swap(input2, "sub", 2)
    input2, in2_y, down_near, down_third = meet(input2, in2_y, down_near, down_third)
    down_last = swap(down_third, "fsdp", 2)
    in2_all = jnp.stack([input2, in2_y])
    in2_c = swap(in2_all, "sub", 1)
    rows_c = swap(rows_all, "sub", 1)
    in2_c, gate_up_x, rows_c = meet(in2_c, gate_up_x, rows_c)
    att_y = swap(after(att, in2_c), "sub", 2)
    in2_all = jnp.stack([in2_all, in2_c]).reshape(4 * count, wide)
    gate_w = jnp.stack([gate_up[:, 0], gate_up_x[:, 0]]).reshape(wide, quarter)
    up_w = jnp.stack([gate_up[:, 1], gate_up_x[:, 1]]).reshape(wide, quarter)
    gate = mm(in2_all, gate_w)
    up = mm(in2_all, up_w)
    sigma = jax.nn.sigmoid(gate)
    active = gate * sigma
    hidden = (active * up).astype(BF)
    down_term = term(cot_all, hidden).reshape(2, n_far, n_sub * padded, quarter)
    hidden, down_term, down_last = meet(hidden, down_term, down_last)
    down_w = jnp.stack([down, down_near, down_third, down_last])
    down_w = down_w.transpose(1, 0, 2, 3).reshape(wide, quarter)
    down_near_came = swap(far_pair(down_term, 1, 1), "fsdp", 2)
    grad_hidden = mm(cot_all, down_w)
    grad_gate = (grad_hidden * up * sigma * (1.0 + gate * (1.0 - sigma))).astype(BF)
    grad_up = (grad_hidden * active).astype(BF)
    grad_in2 = (mm_t(grad_gate, gate_w) + mm_t(grad_up, up_w)).astype(BF).reshape(2, 2 * count, wide)
    in2_terms = after(in2_all, grad_in2)
    gate_up_term = [
        term(in2_terms, grad).reshape(2, n_far, n_sub * padded, quarter) for grad in (grad_gate, grad_up)
    ]
    gate_up_x_came = [swap(part[1], "fsdp", 1) for part in gate_up_term]
    result = mm_t(hidden, down_w).astype(BF).reshape(2, 2 * count, wide)

    came = swap(grad_in2[1], "sub", 1)
    came, att_y = meet(came, att_y)
    atts = [att, att_y, swap(att, "sub", 1), swap(att_y, "sub", 1)]
    grad_in2 = add2(grad_in2[0], came).reshape(2, count, wide)
    grad_in2_y = swap(grad_in2[1], "sub", 2)
    down_held = add2(far_pair(down_term, 1, 0), down_near_came)
    grad_in2_y, result, down_held, atts = meet(grad_in2_y, result, down_held, atts)
    down_far_came = swap(down_held[:, 1], "fsdp", 4)
    grad_h1, grad_h1b, gain2_term = run_kernel(
        norm_kernel,
        [(tall, F32), (tall, BF), ((1, wide), F32)],
        (my_place, grad_in2[0], grad_in2_y, cot_all, hidden1, gains_p),
        name="norm_backward",
    )
    grad_h1_y = swap(grad_h1b, "sub", 2)
    grads, input_grad = run_kernel(
        make_backward(n_fsdp, own),
        [((count + 16, half_ff + 384), BF), (tall, F32)],
        (
            my_place, grad_h1, grad_h1b, gain2_term, rows32, gains_p, *tables, *angles,
            qk, values, logsum, attn_q, attn_o,
        ),
        scratch=[pltpu.VMEM((count, half_ff), F32)],
        name="attn_backward",
    )

    grads_y = swap(grads, "sub", 2)
    grads, grad_h1_y, gate_up_x_came, down_far_came = meet(
        grads, grad_h1_y, gate_up_x_came, down_far_came
    )
    grads_c = swap(grads, "sub", 1)
    grad_h1_c, grad_h1_yc = swap(grad_h1b, "sub", 1), swap(grad_h1_y, "sub", 1)
    down_held = add2(down_held[:, 0], down_far_came)
    down_x_came = swap(down_held[1], "fsdp", 1)
    gate_up_x_came, down_held = meet(gate_up_x_came, down_held)
    gate_up_held = jnp.stack([add2(part[0], came) for part, came in zip(gate_up_term, gate_up_x_came)])
    gate_up_near = swap(far_pair(gate_up_held, 1, 1), "fsdp", 2)
    grads_y, grads_c, grad_h1_c, grad_h1_yc, down_x_came = meet(
        grads_y, grads_c, grad_h1_c, grad_h1_yc, down_x_came
    )

    grads_yc = swap(grads_y, "sub", 1)
    attn_keep, attn_send = run_kernel(
        make_terms(n_far, n_sub, own, padded, count),
        [((n_far * padded, FF), BF)] * 2,
        (
            my_place, rows_all, rows_c, gains_p, *atts, grad_h1b, grad_h1_y, grad_h1_c, grad_h1_yc, grads, grads_y, grads_c, grads_yc,
        ),
        name="attn_terms",
    )

    attn_x = swap(attn_send, "fsdp", 1)
    gate_up_held = add2(far_pair(gate_up_held, 1, 0), after(gate_up_near, attn_send))
    gate_up_far = swap(gate_up_held[:, 1], "fsdp", 4)
    res_c = swap(after(result[1], attn_send), "sub", 1)
    result = add2(result[0], res_c).reshape(2, count, wide)
    res_y = swap(result[1], "sub", 2)
    input_grad = after(input_grad, attn_send)
    input_grad = lax.dot_general(
        input_grad,
        spread_mat.astype(F32),
        (((1,), (1,)), ((), ())),
        precision=lax.Precision.HIGHEST,
    )
    attn_x, gate_up_far, input_grad, res_y = meet(attn_x, gate_up_far, input_grad, res_y)

    def side_by_side(mine, came, bit):
        first = bit == 0
        return jnp.concatenate([jnp.where(first, mine, came), jnp.where(first, came, mine)], axis=-1)

    attn_held = add2(attn_keep, attn_x).reshape(n_far, padded, FF)
    attn_near = swap(far_pair(attn_held, 0, 1), "fsdp", 2)
    down_own = add2(down_held[0], down_x_came)[None]
    mlp_own = jnp.concatenate([add2(gate_up_held[:, 0], gate_up_far), down_own])
    mlp_own = mlp_own.reshape(3, 2, 2, padded, quarter)
    mlp_c = swap(pick(mlp_own, 1 - my_c, 2), "sub", 1)
    attn_near, mlp_c = meet(attn_near, mlp_c)
    attn_held = add2(far_pair(attn_held, 0, 0), attn_near)
    mlp_c = after(mlp_c, attn_held)
    mlp_own = side_by_side(pick(mlp_own, my_c, 2), mlp_c, my_c)
    mlp_y = swap(pick(mlp_own, 1 - my_y, 1), "sub", 2)
    attn_far = swap(attn_held[1], "fsdp", 4)
    result = hidden1 + result[0].astype(F32) + res_y.astype(F32)
    output = mm_t((live * result).astype(BF), spread_mat).astype(BF)
    mlp_own = side_by_side(pick(mlp_own, my_y, 1), mlp_y, my_y)

    def flat(part):
        return part[:own].astype(F32).reshape(-1)

    mlp_flat = [flat(mlp_own[i]) for i in range(3)]
    attn_far, mlp_flat, output = meet(attn_far, mlp_flat, output)
    attn_own = add2(attn_held[0], attn_far)
    gain_grad = attn_own[own, :share].astype(F32)
    return (
        output,
        input_grad,
        flat(attn_own),
        *mlp_flat,
        gain_grad,
    )


def solution(mesh):
    n_fsdp, n_sub = mesh.shape["fsdp"], mesh.shape["sub"]
    n_all = n_fsdp * n_sub
    by_rows = (
        n_fsdp == 8 and D % n_all == 0 and n_fsdp & (n_fsdp - 1) == 0 and n_fsdp > 1 and n_sub == 4 and D // n_fsdp % (D // n_all) == 0
    )
    in_specs = (
        P(("fsdp", "sub"), None),
        P(("fsdp", "sub"), None),
        P(("fsdp", "sub")),
        P("fsdp"),
        P(("fsdp", "sub")),
        P(("fsdp", "sub")),
        P(("fsdp", "sub")),
        P(("fsdp", "sub")),
    )
    out_specs = (
        P(("fsdp", "sub"), None),
        P(("fsdp", "sub"), None),
        P(("fsdp", "sub")),
        P(("fsdp", "sub")),
        P(("fsdp", "sub")),
        P(("fsdp", "sub")),
        P("fsdp"),
    )
    return jax.shard_map(body if by_rows else plain_body, mesh=mesh, in_specs=in_specs, out_specs=out_specs, check_vma=False)
```

```python
import jax
import jax.numpy as jnp
from jax import lax
from jax.experimental import pallas as pl
from jax.experimental.pallas import tpu as pltpu
from jax.sharding import PartitionSpec as P

D = 960
KV = 5
HD = 64
FF = 2560
GROUP = 3


EPS = 1e-05
THETA = 100000.0
NEG = -1e30
piece_width = 64


def rope_tables(position, width):
    half = jnp.arange(width // 2, dtype=jnp.float32)
    inverse = jnp.exp(-(2.0 * half / width) * jnp.log(jnp.float32(THETA)))
    angle = position.astype(jnp.float32)[:, None] * inverse[None, :]
    cosine = jnp.concatenate([jnp.cos(angle), jnp.cos(angle)], axis=1)
    sine = jnp.concatenate([jnp.sin(angle), jnp.sin(angle)], axis=1)
    return (cosine, sine)


def rotate(values, cosine, sine):
    half = values.shape[-1] // 2
    turned = jnp.concatenate([-values[..., half:], values[..., :half]], axis=-1)
    return values * cosine + turned * sine


def unrotate(grads, cosine, sine):
    half = grads.shape[-1] // 2
    scaled = grads * sine
    return grads * cosine + jnp.concatenate([scaled[..., half:], -scaled[..., :half]], axis=-1)


def norm_forward(values):
    scale = lax.rsqrt(jnp.mean(values * values, axis=1, keepdims=True) + EPS)
    return (values * scale, scale)


def norm_backward(grad_in, normed, scale, gain):
    gain_term = jnp.sum(grad_in * normed, axis=0)
    inner = grad_in * gain[None, :]
    back = scale * (inner - normed * jnp.mean(inner * normed, axis=1, keepdims=True))
    return (back, gain_term)


def layout(block_lengths, count):
    slots = jnp.arange(count, dtype=jnp.int32)
    first = block_lengths[0]
    second = block_lengths[1]
    segment = (slots >= first).astype(jnp.int32) + (slots >= first + second).astype(jnp.int32)
    position = (
        slots - first * (segment >= 1).astype(jnp.int32) - second * (segment >= 2).astype(jnp.int32)
    )
    live = (segment < 2).astype(jnp.float32)[:, None]
    allowed = (segment[:, None] == segment[None, :]) & (slots[None, :] <= slots[:, None])
    return (position, live, allowed)


def masked_scores(queries, keys, allowed):
    scores = jnp.einsum(
        "qkgd,jkd->kgqj", queries, keys, preferred_element_type=jnp.float32
    ) * HD ** (-0.5)
    return jnp.where(allowed[None, None], scores, NEG)


def attend(projected, cosine, sine, allowed, count):
    kv_width = KV * HD
    queries = rotate(
        projected[:, :D].reshape(count, KV, GROUP, HD),
        cosine[:, None, None, :],
        sine[:, None, None, :],
    ).astype(jnp.bfloat16)
    keys = rotate(
        projected[:, D : D + kv_width].reshape(count, KV, HD), cosine[:, None, :], sine[:, None, :]
    ).astype(jnp.bfloat16)
    values = projected[:, D + kv_width :].reshape(count, KV, HD).astype(jnp.bfloat16)
    scores = masked_scores(queries, keys, allowed)
    top = jnp.max(scores, axis=-1, keepdims=True)
    expo = jnp.exp(scores - top)
    total = jnp.sum(expo, axis=-1, keepdims=True)
    logsum = top + jnp.log(total)
    weights = (expo / total).astype(jnp.bfloat16)
    attended = (
        jnp.einsum("kgqj,jkd->qkgd", weights, values, preferred_element_type=jnp.float32)
        .reshape(count, D)
        .astype(jnp.bfloat16)
    )
    return (queries, keys, values, logsum, attended)


def attend_back(grad_att, queries, keys, values, logsum, allowed, cosine, sine, count):
    kv_width = KV * HD
    probs = jnp.exp(masked_scores(queries, keys, allowed) - logsum)
    probs_b = probs.astype(jnp.bfloat16)
    value_grad = jnp.einsum("kgqj,qkgd->jkd", probs_b, grad_att, preferred_element_type=jnp.float32)
    prob_grad = jnp.einsum("qkgd,jkd->kgqj", grad_att, values, preferred_element_type=jnp.float32)
    delta = jnp.sum(probs * prob_grad, axis=-1, keepdims=True)
    score_grad = (probs * (prob_grad - delta) * HD ** (-0.5)).astype(jnp.bfloat16)
    query_grad = jnp.einsum("kgqj,jkd->qkgd", score_grad, keys, preferred_element_type=jnp.float32)
    key_grad = jnp.einsum("kgqj,qkgd->jkd", score_grad, queries, preferred_element_type=jnp.float32)
    query_grad = unrotate(query_grad, cosine[:, None, None, :], sine[:, None, None, :])
    key_grad = unrotate(key_grad, cosine[:, None, :], sine[:, None, :])
    return jnp.concatenate(
        [
            query_grad.reshape(count, D),
            key_grad.reshape(count, kv_width),
            value_grad.reshape(count, kv_width),
        ],
        axis=1,
    ).astype(jnp.bfloat16)


def collect(attn_flat, gate_flat, up_flat, down_flat):
    whole = (
        lax.all_gather(attn_flat, ("fsdp", "sub"), axis=0, tiled=True),
        lax.all_gather(gate_flat, ("fsdp", "sub"), axis=0, tiled=True),
        lax.all_gather(up_flat, ("fsdp", "sub"), axis=0, tiled=True),
        lax.all_gather(down_flat, ("fsdp", "sub"), axis=0, tiled=True),
    )
    return tuple((piece.reshape(D, FF) for piece in whole))


def flat_terms(pair_lists, count):
    results = []
    for pairs in pair_lists:
        blocks = [
            jnp.dot(left.T, right, preferred_element_type=jnp.float32) for left, right in pairs
        ]
        joined = blocks[0] if len(blocks) == 1 else jnp.concatenate(blocks, axis=1)
        results.append(joined.reshape(-1).reshape(count, piece_width))
    return jnp.concatenate(results, axis=1)


def split_owned(owned):
    return tuple(
        (
            owned[:, index * piece_width : (index + 1) * piece_width].reshape(-1)
            for index in range(4)
        )
    )


def spread(pair_lists):
    share = D * FF // (piece_width * lax.axis_size("fsdp") * lax.axis_size("sub"))
    owned = lax.psum_scatter(
        flat_terms(pair_lists, share * lax.axis_size(("fsdp", "sub"))),
        ("fsdp", "sub"),
        scatter_dimension=0,
        tiled=True,
    )
    return split_owned(owned)


def flat_path(
    rows32,
    cotangent,
    live,
    allowed,
    cosine,
    sine,
    gain_attn,
    gain_mlp,
    normed1,
    scale1,
    input1,
    flats,
):
    count = rows32.shape[0]
    q_width = D + 2 * KV * HD
    attn_mat, gate_mat, up_mat, down_mat = collect(flats[0], flats[1], flats[2], flats[3])
    projected = jnp.dot(input1, attn_mat[:, :q_width], preferred_element_type=jnp.float32)
    queries, keys, values, logsum, attended = attend(projected, cosine, sine, allowed, count)
    hidden1 = rows32 + jnp.dot(
        attended, attn_mat[:, q_width:].T, preferred_element_type=jnp.float32
    )
    normed2, scale2 = norm_forward(hidden1)
    input2 = (normed2 * gain_mlp[None, :]).astype(jnp.bfloat16)
    gate = jnp.dot(input2, gate_mat, preferred_element_type=jnp.float32)
    up = jnp.dot(input2, up_mat, preferred_element_type=jnp.float32)
    sigma = jax.nn.sigmoid(gate)
    active = gate * sigma
    hidden = (active * up).astype(jnp.bfloat16)
    result = hidden1 + jnp.dot(hidden, down_mat.T, preferred_element_type=jnp.float32)
    output = (live * result).astype(jnp.bfloat16)
    attn_back, gate_back, up_back, down_back = collect(flats[0], flats[1], flats[2], flats[3])
    grad_out = live * cotangent.astype(jnp.float32)
    grad_outb = grad_out.astype(jnp.bfloat16)
    grad_hidden = jnp.dot(grad_outb, down_back, preferred_element_type=jnp.float32)
    grad_gate = (grad_hidden * up * sigma * (1.0 + gate * (1.0 - sigma))).astype(jnp.bfloat16)
    grad_up = (grad_hidden * active).astype(jnp.bfloat16)
    grad_in2 = jnp.dot(grad_gate, gate_back.T, preferred_element_type=jnp.float32) + jnp.dot(
        grad_up, up_back.T, preferred_element_type=jnp.float32
    )
    back2, gain2_term = norm_backward(grad_in2, normed2, scale2, gain_mlp)
    grad_h1 = grad_out + back2
    grad_h1b = grad_h1.astype(jnp.bfloat16)
    grad_att = (
        jnp.dot(grad_h1b, attn_back[:, q_width:], preferred_element_type=jnp.float32)
        .astype(jnp.bfloat16)
        .reshape(count, KV, GROUP, HD)
    )
    proj_grad = attend_back(grad_att, queries, keys, values, logsum, allowed, cosine, sine, count)
    grad_in1 = jnp.dot(proj_grad, attn_back[:, :q_width].T, preferred_element_type=jnp.float32)
    back1, gain1_term = norm_backward(grad_in1, normed1, scale1, gain_attn)
    input_grad = grad_h1 + back1
    pair_lists = (
        ((input1, proj_grad), (grad_h1b, attended)),
        ((input2, grad_gate),),
        ((input2, grad_up),),
        ((grad_outb, hidden),),
    )
    owned = spread(pair_lists)
    return (output, input_grad, owned, gain1_term, gain2_term)


def plain_body(rows, cotangent, lengths, gains, attn_weight, gate_weight, up_weight, down_weight):
    count = rows.shape[0]
    position, live, allowed = layout(lengths, count)
    cosine, sine = rope_tables(position, HD)
    full_gains = lax.all_gather(gains, "fsdp", axis=0, tiled=True).astype(jnp.float32)
    gain_attn = full_gains[:D]
    gain_mlp = full_gains[D:]
    rows32 = rows.astype(jnp.float32)
    normed1, scale1 = norm_forward(rows32)
    input1 = (normed1 * gain_attn[None, :]).astype(jnp.bfloat16)
    flats = (attn_weight, gate_weight, up_weight, down_weight)
    output, input_grad, owned, gain1_term, gain2_term = flat_path(
        rows32,
        cotangent,
        live,
        allowed,
        cosine,
        sine,
        gain_attn,
        gain_mlp,
        normed1,
        scale1,
        input1,
        flats,
    )
    gain_total = lax.psum(jnp.concatenate([gain1_term, gain2_term]), ("fsdp", "sub"))
    share = gains.shape[0]
    gain_grad = lax.dynamic_slice_in_dim(gain_total, lax.axis_index("fsdp") * share, share)
    return (output, input_grad, owned[0], owned[1], owned[2], owned[3], gain_grad)


BF = jnp.bfloat16
F32 = jnp.float32


def swap(value, axis, bit):
    return lax.ppermute(value, axis, [(i, i ^ bit) for i in range(lax.axis_size(axis))])


def meet(*values):
    return lax.optimization_barrier(values)


def after(value, *done):
    return lax.optimization_barrier((value, *done))[0]


def add2(kept, came):
    return (kept.astype(F32) + came.astype(F32)).astype(BF)


def far_pair(value, axis, odd):
    shape = value.shape
    value = value.reshape(shape[:axis] + (shape[axis] // 2, 2) + shape[axis + 1 :])
    return lax.index_in_dim(value, odd, axis + 1, keepdims=False)


def pick(value, index, axis):
    return lax.dynamic_index_in_dim(value, index, axis, keepdims=False)


def put2(own, came, bit, axis):
    first = bit == 0
    return jnp.stack([jnp.where(first, own, came), jnp.where(first, came, own)], axis=axis)


def mm(a, b):
    return jnp.dot(a, b, preferred_element_type=F32)


def mm_t(a, b):
    return lax.dot_general(a, b, (((1,), (1,)), ((), ())), preferred_element_type=F32)


def term(a, b):
    return lax.dot_general(a, b, (((0,), (0,)), ((), ())), preferred_element_type=F32).astype(BF)


def dot_f(a, b):
    return lax.dot_general(a, b, (((1,), (0,)), ((), ())), preferred_element_type=F32)


def dot_t(a, b):
    return lax.dot_general(a, b, (((1,), (1,)), ((), ())), preferred_element_type=F32)


def dot_0(a, b):
    return lax.dot_general(a, b, (((0,), (0,)), ((), ())), preferred_element_type=F32)


def stacked(parts):
    return jnp.concatenate(parts, axis=0)


def norm_rows(values):
    mean = jnp.sum(values * values, axis=1, keepdims=True) * (1.0 / D)
    scale = lax.rsqrt(mean + EPS)
    return values * scale, scale


def norm_rows_back(grad_in, normed, scale, gain):
    gain_term = jnp.sum(grad_in * normed, axis=0, keepdims=True)
    inner = grad_in * gain
    mean = jnp.sum(inner * normed, axis=1, keepdims=True) * (1.0 / D)
    return scale * (inner - normed * mean), gain_term


def first_half(shape):
    return lax.broadcasted_iota(jnp.int32, shape, 1) % HD < HD // 2


def gain_masks(owner, my_fsdp, n_fsdp, own, share):
    wide = owner.shape[1]
    per = share // own
    place = lax.broadcasted_iota(jnp.int32, (n_fsdp, wide), 0) ^ my_fsdp
    group = owner // per
    return place == group, place == group + n_fsdp // 2


def slot_matrix(owner, inner, own, height):
    per = D * 2 // 8 // own
    slot = jnp.where(inner < own, owner % per * own + inner, -1)
    return (lax.broadcasted_iota(jnp.int32, (height, owner.shape[1]), 0) == slot).astype(F32).astype(BF)


def make_forward(n_fsdp, own, padded, share, by_fsdp):
    kv_width = KV * HD

    def kernel(
        place_ref, rows_ref, owner_ref, inner_ref, cos_ref, sin_ref, seg_ref,
        own_q_ref, came_q_ref, own_o_ref, came_o_ref,
        att_ref, qk_ref, v_ref, logsum_ref, hidden1_ref, input2_ref, gains_ref, attn_q_ref, attn_o_ref,
    ):
        core = place_ref[1]
        for p in range(own_q_ref.shape[0] // padded):
            here = pl.ds(pl.multiple_of((2 * p + core) * padded, padded), padded)
            there = pl.ds(pl.multiple_of((2 * p + 1 - core) * padded, padded), padded)
            block = slice(p * padded, (p + 1) * padded)
            attn_q_ref[here, :] = own_q_ref[block, :]
            attn_q_ref[there, :] = came_q_ref[block, :]
            attn_o_ref[here, :] = own_o_ref[block, :]
            attn_o_ref[there, :] = came_o_ref[block, :]
        pieces = jnp.concatenate(
            [attn_q_ref[p * padded + own : p * padded + own + 1, :share].astype(F32) for p in by_fsdp], axis=0
        ).astype(BF)
        owner = owner_ref[...]
        first, second = gain_masks(owner, place_ref[0], n_fsdp, own, share)
        spots = dot_f(pieces, slot_matrix(owner, inner_ref[...], own, share))
        gain1 = jnp.sum(jnp.where(first, spots, 0.0), axis=0, keepdims=True)
        gain2 = jnp.sum(jnp.where(second, spots, 0.0), axis=0, keepdims=True)
        gains_ref[0:1, :] = gain1
        gains_ref[1:2, :] = gain2
        rows = rows_ref[...]
        normed, _ = norm_rows(rows)
        input1 = (normed * gain1).astype(BF)
        projected = dot_f(input1, attn_q_ref[...])
        cosine = cos_ref[...]
        sine = sin_ref[...]
        low = first_half(cosine.shape)
        for i in range(projected.shape[1] // 128):
            part = projected[:, 128 * i : 128 * (i + 1)]
            turned = jnp.where(low, -pltpu.roll(part, 96, 1), pltpu.roll(part, 32, 1))
            qk_ref[:, 128 * i : 128 * (i + 1)] = (part * cosine + turned * sine).astype(BF)
        values = dot_f(input1, attn_o_ref[:, :384]).astype(BF)
        v_ref[...] = values
        count = rows.shape[0]
        allowed = stacked([seg_ref[...]] * GROUP) > 0.0
        att_ref[:, :128] = jnp.zeros((count, 128), BF)
        shift = kv_width - 256
        for k in range(KV):
            keys = qk_ref[:, D + HD * k : D + HD * (k + 1)]
            value = values[:, HD * k : HD * (k + 1)]
            heads = [HD * (GROUP * k + g) for g in range(GROUP)]
            queries = stacked([qk_ref[:, h : h + HD] for h in heads])
            scores = jnp.where(allowed, dot_t(queries, keys) * HD ** (-0.5), NEG)
            top = jnp.max(scores, axis=1, keepdims=True)
            expo = jnp.exp(scores - top)
            total = jnp.sum(expo, axis=1, keepdims=True)
            logsum_ref[:, k : k + 1] = top + jnp.log(total)
            weights = (expo / total).astype(BF)
            attended = dot_f(weights, value).astype(BF)
            for g, h in enumerate(heads):
                att_ref[:, shift + h : shift + h + HD] = attended[count * g : count * (g + 1), :]
        hidden1 = rows + dot_t(att_ref[...], attn_o_ref[:, 256:])
        hidden1_ref[...] = hidden1
        normed2, _ = norm_rows(hidden1)
        input2_ref[...] = (normed2 * gain2).astype(BF)

    return kernel


def norm_kernel(
    place_ref, grad_a_ref, grad_b_ref, grad_out_ref, hidden1_ref, gains_ref,
    grad_h1_ref, grad_h1b_ref, gain2_ref,
):
    grad_in2 = grad_a_ref[...].astype(F32) + grad_b_ref[...].astype(F32)
    normed2, scale2 = norm_rows(hidden1_ref[...])
    back2, gain2_term = norm_rows_back(grad_in2, normed2, scale2, gains_ref[1:2, :])
    grad_h1 = grad_out_ref[: hidden1_ref.shape[0], :].astype(F32) + back2
    grad_h1_ref[...] = grad_h1
    grad_h1b_ref[...] = grad_h1.astype(BF)
    gain2_ref[...] = gain2_term


def make_backward(n_fsdp, own):
    kv_width = KV * HD

    def kernel(
        place_ref, grad_h1_ref, grad_h1b_ref, gain2_ref, rows_ref, gains_ref, owner_ref, inner_ref,
        cos_ref, sin_ref, seg_ref, qk_ref, v_ref, logsum_ref, attn_q_ref, attn_o_ref,
        grads_ref, input_grad_ref,
        turn_ref,
    ):
        count = rows_ref.shape[0]
        qk_width = turn_ref.shape[1]
        grad_att = dot_f(grad_h1b_ref[...], attn_o_ref[...]).astype(BF)
        allowed = stacked([seg_ref[...]] * GROUP) > 0.0
        grads_ref[:count, qk_width:] = jnp.zeros((count, 384), BF)
        for k in range(KV):
            keys = qk_ref[:, D + HD * k : D + HD * (k + 1)]
            value = v_ref[:, HD * k : HD * (k + 1)]
            heads = [HD * (GROUP * k + g) for g in range(GROUP)]
            queries = stacked([qk_ref[:, h : h + HD] for h in heads])
            grad = stacked([grad_att[:, kv_width + h : kv_width + h + HD] for h in heads])
            scores = jnp.where(allowed, dot_t(queries, keys) * HD ** (-0.5), NEG)
            probs = jnp.exp(scores - logsum_ref[:, k : k + 1])
            value_grad = dot_0(probs.astype(BF), grad)
            prob_grad = dot_t(grad, value)
            delta = jnp.sum(probs * prob_grad, axis=1, keepdims=True)
            score_grad = (probs * (prob_grad - delta) * HD ** (-0.5)).astype(BF)
            query_grad = dot_f(score_grad, keys)
            for g, h in enumerate(heads):
                turn_ref[:, h : h + HD] = query_grad[count * g : count * (g + 1), :]
            turn_ref[:, D + HD * k : D + HD * (k + 1)] = dot_0(score_grad, queries)
            grads_ref[:count, qk_width + HD * k : qk_width + HD * (k + 1)] = value_grad.astype(BF)
        cosine = cos_ref[...]
        sine = sin_ref[...]
        low = first_half(cosine.shape)
        for i in range(qk_width // 128):
            part = turn_ref[:, 128 * i : 128 * (i + 1)]
            scaled = part * sine
            turned = jnp.where(low, pltpu.roll(scaled, 96, 1), -pltpu.roll(scaled, 32, 1))
            grads_ref[:count, 128 * i : 128 * (i + 1)] = (part * cosine + turned).astype(BF)
        owner = owner_ref[...]
        inner = inner_ref[...]
        grad_in1 = dot_t(grads_ref[:count, :qk_width], attn_q_ref[...]) * jnp.where(inner < own, 1.0, 0.0)
        grad_in1 = grad_in1 + dot_t(grads_ref[:count, qk_width:], attn_o_ref[:, :384])
        normed1, scale1 = norm_rows(rows_ref[...])
        back1, gain1_term = norm_rows_back(grad_in1, normed1, scale1, gains_ref[0:1, :])
        input_grad_ref[...] = grad_h1_ref[...] + back1
        first, second = gain_masks(owner, place_ref[0], n_fsdp, own, D * 2 // n_fsdp)
        both = jnp.where(first, gain1_term, 0.0) + jnp.where(second, gain2_ref[...], 0.0)
        gain_rows = dot_t(both.astype(BF), slot_matrix(owner, inner, own, 256))
        extra = grads_ref.shape[0] - count
        grads_ref[count:, :] = jnp.zeros((extra, grads_ref.shape[1]), BF)
        gain_rows = jnp.concatenate([gain_rows, jnp.zeros((extra - n_fsdp, 256), F32)], axis=0)
        grads_ref[count:, :256] = gain_rows.astype(BF)

    return kernel


def make_terms(n_far, n_sub, own, padded, count):
    def kernel(place_ref, rows_a_ref, rows_b_ref, gains_ref, *refs):
        att_refs = refs[:n_sub]
        grad_h1_refs = refs[n_sub : 2 * n_sub]
        grads_refs = refs[2 * n_sub : 3 * n_sub]
        keep_ref, send_ref = refs[3 * n_sub :]
        half_ff = FF // 2
        rows = keep_ref.shape[0] * 2
        wide = grad_h1_refs[0].shape[1]

        def tokens(pieces):
            return jnp.concatenate(pieces, axis=0)

        spot = lax.broadcasted_iota(jnp.int32, (wide, rows), 1)
        source = (spot // padded * n_sub + place_ref[2]) * padded + spot % padded
        select = (lax.broadcasted_iota(jnp.int32, (wide, rows), 0) == source).astype(F32).astype(BF)
        spot = lax.broadcasted_iota(jnp.int32, (D, rows), 1)
        block = spot // padded
        owner = ((block % n_far * 2 + block // n_far) ^ place_ref[0]) * n_sub + place_ref[2]
        source = jnp.where(spot % padded < own, owner * own + spot % padded, -1)
        select_d = (lax.broadcasted_iota(jnp.int32, (D, rows), 0) == source).astype(F32).astype(BF)
        rows_b = jnp.concatenate([rows_a_ref[...], rows_b_ref[...]], axis=0)
        group = rows_b.astype(F32)
        scale = lax.rsqrt(jnp.sum(group * group, axis=1, keepdims=True) * (1.0 / D) + EPS)
        gain = dot_f(gains_ref[...].astype(BF), select)[0:1, :]
        left1 = (dot_f(rows_b, select_d) * scale * gain).astype(BF)
        left2 = dot_f(tokens([ref[...] for ref in grad_h1_refs]), select).astype(BF)
        right = tokens([ref[:count, :] for ref in grads_refs])
        extra = tokens([ref[count:, :256] for ref in grads_refs])
        spot = lax.broadcasted_iota(jnp.int32, (extra.shape[0], rows), 1)
        block = spot // padded
        here = lax.broadcasted_iota(jnp.int32, spot.shape, 0) % (extra.shape[0] // n_sub)
        wanted = jnp.where(spot % padded == own, block % n_far * 2 + block // n_far, -1)
        spots = (here == wanted).astype(F32).astype(BF)
        q_term = dot_0(left1, right)
        start = q_term[:, :256] + dot_0(spots, extra)
        o_term = dot_0(left2, tokens([ref[...] for ref in att_refs]))
        mixed = o_term[:, :128] + q_term[:, half_ff + 256 :]
        for ref, at in ((keep_ref, 0), (send_ref, rows // 2)):
            to = slice(at, at + rows // 2)
            ref[:, :256] = start[to, :].astype(BF)
            ref[:, 256:half_ff] = q_term[to, 256:half_ff].astype(BF)
            ref[:, half_ff : half_ff + 256] = q_term[to, half_ff : half_ff + 256].astype(BF)
            ref[:, half_ff + 256 : half_ff + 384] = mixed[to, :].astype(BF)
            ref[:, half_ff + 384 :] = o_term[to, 128:].astype(BF)

    return kernel


VMEM = pl.BlockSpec(memory_space=pltpu.VMEM)
SMEM = pl.BlockSpec(memory_space=pltpu.SMEM)


def run_kernel(kernel, outs, args, scratch=(), name=None):
    return pl.pallas_call(
        kernel,
        out_shape=[jax.ShapeDtypeStruct(shape, kind) for shape, kind in outs],
        in_specs=[SMEM] + [VMEM] * (len(args) - 1),
        out_specs=[VMEM] * len(outs),
        scratch_shapes=scratch,
        compiler_params=pltpu.CompilerParams(vmem_limit_bytes=56 << 20),
        cost_estimate=pl.CostEstimate(flops=1000, transcendentals=0, bytes_accessed=1000),
        name=name,
    )(*args)


def body(rows, cotangent, lengths, gains, attn_weight, gate_weight, up_weight, down_weight):
    count = rows.shape[0]
    n_fsdp = lax.axis_size("fsdp")
    n_sub = lax.axis_size("sub")
    n_all = n_fsdp * n_sub
    n_far = n_fsdp // 2
    own = D // n_all
    padded = -(-(own + 1) // 16) * 16
    wide = n_all * padded
    half_ff = FF // 2
    quarter = FF // 4
    share = gains.shape[0]
    kv_width = KV * HD
    my_fsdp = lax.axis_index("fsdp")
    my_sub = lax.axis_index("sub")
    my_y = my_sub // 2
    my_c = my_sub % 2

    column = jnp.arange(wide, dtype=jnp.int32)
    place = column // padded
    inner = column % padded
    rel = (place // n_sub) % n_far * 2 + place // (n_sub * n_far)
    real = inner < own
    source = jnp.where(real, ((rel ^ my_fsdp) * n_sub + place % n_sub) * own + inner, -1)
    spread_mat = (jnp.arange(D, dtype=jnp.int32)[:, None] == source[None, :]).astype(BF)

    def padded_block(flat):
        return jnp.pad(flat.reshape(own, FF), ((0, padded - own), (0, 0)))

    def columns(value, index, width):
        return lax.dynamic_slice_in_dim(value, index * width, width, axis=value.ndim - 1)

    position, live, allowed = layout(lengths, count)
    cosine, sine = rope_tables(position, HD)
    cosine = jnp.concatenate([cosine, cosine], axis=1)
    sine = jnp.concatenate([sine, sine], axis=1)
    seg = allowed.astype(F32)
    rows32 = mm(rows, spread_mat)

    owner = ((rel ^ my_fsdp) * n_sub + place % n_sub)[None, :]

    attn_block = padded_block(attn_weight)
    attn_block = attn_block.at[own, :share].set(gains)
    far = [swap(attn_block, "fsdp", 2 * k) for k in range(1, n_far)]
    mlp_block = jnp.stack([padded_block(w) for w in (gate_weight, up_weight, down_weight)])
    sent = columns(mlp_block, 1 - my_y, half_ff)
    came = swap(sent, "sub", 2)
    cot = (live * after(cotangent, sent).astype(F32)).astype(BF)
    cot_y = swap(cot, "sub", 2)
    mlp_block = put2(columns(mlp_block, my_y, half_ff), came, my_y, 1)
    came = swap(columns(mlp_block, 1 - my_c, quarter), "sub", 1)
    mlp_block = put2(columns(mlp_block, my_c, quarter), came, my_c, 2)
    mlp_block = mlp_block.reshape(3, n_sub * padded, quarter)
    far, mlp_block, cot, cot_y = meet(far, mlp_block, cot, cot_y)

    attn_far = jnp.stack([attn_block] + list(far))
    half0 = attn_far[:, :, :half_ff]
    half1 = attn_far[:, :, half_ff:]
    gate_up = mlp_block[:2]
    down = mlp_block[2]
    x0, y1, near = swap(half0, "fsdp", 1), swap(half1, "sub", 2), swap(gate_up, "fsdp", 2)
    cot = jnp.concatenate([cot, cot_y])
    cot_c = swap(cot, "sub", 1)
    tables = (owner, inner[None, :])
    angles = (cosine, sine, seg)
    half0, half1, gate_up, down, x0, y1, near, rows32, cot, cot_c, tables, angles = meet(
        half0, half1, gate_up, down, x0, y1, near, rows32, cot, cot_c, tables, angles
    )

    half0 = jnp.stack([half0, x0])
    half1 = put2(half1, y1, my_y, 1)
    y0, x1, third = swap(half0, "sub", 2), swap(half1, "fsdp", 1), swap(gate_up, "fsdp", 4)
    down_x = swap(down, "fsdp", 1)
    cot_all = mm(jnp.concatenate([cot, cot_c]), spread_mat).astype(BF)
    half0, half1, gate_up, down, down_x, near, y0, x1, third, cot_all = meet(
        half0, half1, gate_up, down, down_x, near, y0, x1, third, cot_all
    )

    half0 = put2(half0, y0, my_y, 2).reshape(wide // 2, half_ff)
    half1 = jnp.stack([half1, x1]).reshape(wide // 2, half_ff)
    c0, c1, last = swap(half0, "sub", 1), swap(half1, "sub", 1), swap(third, "fsdp", 2)
    down = jnp.stack([down, down_x])
    gate_up_a = jnp.stack([gate_up, near])
    gate_up_xa = swap(gate_up_a, "fsdp", 1)
    rows_y = swap(rows, "sub", 2)
    half0, half1, c0, c1, third, last, down, rows_y = meet(half0, half1, c0, c1, third, last, down, rows_y)
    rows_all = jnp.concatenate([rows, rows_y])

    gate_up_b = jnp.stack([third, last])
    gate_up_xb = swap(gate_up_b, "fsdp", 1)
    down_near, down_third = swap(down, "fsdp", 2), swap(down, "fsdp", 4)
    by_fsdp = [(f % 2) * n_far * n_sub + (f // 2) * n_sub for f in range(n_fsdp)]
    my_place = jnp.stack([my_fsdp, my_c, my_sub])
    tall = (count, wide)
    forward = run_kernel(
        make_forward(n_fsdp, own, padded, share, by_fsdp),
        [
            ((count, half_ff - 256), BF),
            ((count, half_ff), BF),
            ((count, 384), BF),
            ((count * GROUP, KV), F32),
            (tall, F32),
            (tall, BF),
            ((2, wide), F32),
            ((wide, half_ff), BF),
            ((wide, half_ff), BF),
        ],
        (my_place, rows32, *tables, *angles, half0, c0, half1, c1),
        name="attn_forward",
    )
    att, qk, values, logsum, hidden1, input2, gains_p, attn_q, attn_o = forward

    in2_y = swap(input2, "sub", 2)
    input2, in2_y, down_near, down_third, gate_up_xa, gate_up_xb = meet(
        input2, in2_y, down_near, down_third, gate_up_xa, gate_up_xb
    )
    down_last = swap(down_third, "fsdp", 2)
    in2_all = jnp.stack([input2, in2_y])
    in2_c = swap(in2_all, "sub", 1)
    rows_c = swap(rows_all, "sub", 1)
    in2_c, rows_c = meet(in2_c, rows_c)
    att_y = swap(after(att, in2_c), "sub", 2)
    in2_all = jnp.stack([in2_all, in2_c]).reshape(4 * count, wide)
    gate_up_all = jnp.concatenate([gate_up_a, gate_up_b, gate_up_xa, gate_up_xb])
    gate_w = gate_up_all[:, 0].reshape(wide, quarter)
    up_w = gate_up_all[:, 1].reshape(wide, quarter)
    gate = mm(in2_all, gate_w)
    up = mm(in2_all, up_w)
    sigma = jax.nn.sigmoid(gate)
    active = gate * sigma
    hidden = (active * up).astype(BF)
    down_term = term(cot_all, hidden).reshape(2, n_far, n_sub * padded, quarter)
    hidden, down_term, down_last = meet(hidden, down_term, down_last)
    down_w = jnp.stack([down, down_near, down_third, down_last])
    down_w = down_w.transpose(1, 0, 2, 3).reshape(wide, quarter)
    down_near_came = swap(far_pair(down_term, 1, 1), "fsdp", 2)
    grad_hidden = mm(cot_all, down_w)
    grad_gate = (grad_hidden * up * sigma * (1.0 + gate * (1.0 - sigma))).astype(BF)
    grad_up = (grad_hidden * active).astype(BF)
    grad_in2 = (mm_t(grad_gate, gate_w) + mm_t(grad_up, up_w)).astype(BF).reshape(2, 2 * count, wide)
    in2_terms = after(in2_all, grad_in2)
    gate_up_term = [
        term(in2_terms, grad).reshape(2, n_far, n_sub * padded, quarter) for grad in (grad_gate, grad_up)
    ]
    gate_up_x_came = [swap(part[1], "fsdp", 1) for part in gate_up_term]
    result = mm_t(hidden, down_w).astype(BF).reshape(2, 2 * count, wide)

    came = swap(grad_in2[1], "sub", 1)
    came, att_y = meet(came, att_y)
    atts = [att, att_y, swap(att, "sub", 1), swap(att_y, "sub", 1)]
    grad_in2 = add2(grad_in2[0], came).reshape(2, count, wide)
    grad_in2_y = swap(grad_in2[1], "sub", 2)
    down_held = add2(far_pair(down_term, 1, 0), down_near_came)
    grad_in2_y, result, down_held, atts = meet(grad_in2_y, result, down_held, atts)
    down_far_came = swap(down_held[:, 1], "fsdp", 4)
    grad_h1, grad_h1b, gain2_term = run_kernel(
        norm_kernel,
        [(tall, F32), (tall, BF), ((1, wide), F32)],
        (my_place, grad_in2[0], grad_in2_y, cot_all, hidden1, gains_p),
        name="norm_backward",
    )
    grad_h1_y = swap(grad_h1b, "sub", 2)
    grads, input_grad = run_kernel(
        make_backward(n_fsdp, own),
        [((count + 16, half_ff + 384), BF), (tall, F32)],
        (
            my_place, grad_h1, grad_h1b, gain2_term, rows32, gains_p, *tables, *angles,
            qk, values, logsum, attn_q, attn_o,
        ),
        scratch=[pltpu.VMEM((count, half_ff), F32)],
        name="attn_backward",
    )

    grads_y = swap(grads, "sub", 2)
    grads, grad_h1_y, gate_up_x_came, down_far_came = meet(
        grads, grad_h1_y, gate_up_x_came, down_far_came
    )
    grads_c = swap(grads, "sub", 1)
    grad_h1_c, grad_h1_yc = swap(grad_h1b, "sub", 1), swap(grad_h1_y, "sub", 1)
    down_held = add2(down_held[:, 0], down_far_came)
    down_x_came = swap(down_held[1], "fsdp", 1)
    gate_up_x_came, down_held = meet(gate_up_x_came, down_held)
    gate_up_held = jnp.stack([add2(part[0], came) for part, came in zip(gate_up_term, gate_up_x_came)])
    gate_up_near = swap(far_pair(gate_up_held, 1, 1), "fsdp", 2)
    grads_y, grads_c, grad_h1_c, grad_h1_yc, down_x_came = meet(
        grads_y, grads_c, grad_h1_c, grad_h1_yc, down_x_came
    )

    grads_yc = swap(grads_y, "sub", 1)
    attn_keep, attn_send = run_kernel(
        make_terms(n_far, n_sub, own, padded, count),
        [((n_far * padded, FF), BF)] * 2,
        (
            my_place, rows_all, rows_c, gains_p, *atts, grad_h1b, grad_h1_y, grad_h1_c, grad_h1_yc, grads, grads_y, grads_c, grads_yc,
        ),
        name="attn_terms",
    )

    attn_x = swap(attn_send, "fsdp", 1)
    gate_up_held = add2(far_pair(gate_up_held, 1, 0), after(gate_up_near, attn_send))
    gate_up_far = swap(gate_up_held[:, 1], "fsdp", 4)
    res_c = swap(after(result[1], attn_send), "sub", 1)
    result = add2(result[0], res_c).reshape(2, count, wide)
    res_y = swap(result[1], "sub", 2)
    input_grad = after(input_grad, attn_send)
    input_grad = lax.dot_general(
        input_grad,
        spread_mat.astype(F32),
        (((1,), (1,)), ((), ())),
        precision=lax.Precision.HIGHEST,
    )
    attn_x, gate_up_far, input_grad, res_y = meet(attn_x, gate_up_far, input_grad, res_y)

    def side_by_side(mine, came, bit):
        first = bit == 0
        return jnp.concatenate([jnp.where(first, mine, came), jnp.where(first, came, mine)], axis=-1)

    attn_held = add2(attn_keep, attn_x).reshape(n_far, padded, FF)
    attn_near = swap(far_pair(attn_held, 0, 1), "fsdp", 2)
    down_own = add2(down_held[0], down_x_came)[None]
    mlp_own = jnp.concatenate([add2(gate_up_held[:, 0], gate_up_far), down_own])
    mlp_own = mlp_own.reshape(3, 2, 2, padded, quarter)
    mlp_c = swap(pick(mlp_own, 1 - my_c, 2), "sub", 1)
    attn_near, mlp_c = meet(attn_near, mlp_c)
    attn_held = add2(far_pair(attn_held, 0, 0), attn_near)
    attn_held, mlp_c = meet(attn_held, mlp_c)
    mlp_own = side_by_side(pick(mlp_own, my_c, 2), mlp_c, my_c)
    mlp_y = swap(pick(mlp_own, 1 - my_y, 1), "sub", 2)
    attn_far = swap(attn_held[1], "fsdp", 4)
    result = hidden1 + result[0].astype(F32) + res_y.astype(F32)
    output = mm_t((live * result).astype(BF), spread_mat).astype(BF)
    mlp_own = side_by_side(pick(mlp_own, my_y, 1), mlp_y, my_y)

    def flat(part):
        return part[:own].astype(F32).reshape(-1)

    mlp_flat = [flat(mlp_own[i]) for i in range(3)]
    attn_far, mlp_flat, output = meet(attn_far, mlp_flat, output)
    attn_own = add2(attn_held[0], attn_far)
    gain_grad = attn_own[own, :share].astype(F32)
    return (
        output,
        input_grad,
        flat(attn_own),
        *mlp_flat,
        gain_grad,
    )


def solution(mesh):
    n_fsdp, n_sub = mesh.shape["fsdp"], mesh.shape["sub"]
    n_all = n_fsdp * n_sub
    by_rows = (
        n_fsdp == 8 and D % n_all == 0 and n_fsdp & (n_fsdp - 1) == 0 and n_fsdp > 1 and n_sub == 4 and D // n_fsdp % (D // n_all) == 0
    )
    in_specs = (
        P(("fsdp", "sub"), None),
        P(("fsdp", "sub"), None),
        P(("fsdp", "sub")),
        P("fsdp"),
        P(("fsdp", "sub")),
        P(("fsdp", "sub")),
        P(("fsdp", "sub")),
        P(("fsdp", "sub")),
    )
    out_specs = (
        P(("fsdp", "sub"), None),
        P(("fsdp", "sub"), None),
        P(("fsdp", "sub")),
        P(("fsdp", "sub")),
        P(("fsdp", "sub")),
        P(("fsdp", "sub")),
        P("fsdp"),
    )
    return jax.shard_map(body if by_rows else plain_body, mesh=mesh, in_specs=in_specs, out_specs=out_specs, check_vma=False)
```

```python
import jax
import jax.numpy as jnp
from jax import lax
from jax.experimental import pallas as pl
from jax.experimental.pallas import tpu as pltpu
from jax.sharding import PartitionSpec as P

D = 960
KV = 5
HD = 64
FF = 2560
GROUP = 3


EPS = 1e-05
THETA = 100000.0
NEG = -1e30
piece_width = 64


def rope_tables(position, width):
    half = jnp.arange(width // 2, dtype=jnp.float32)
    inverse = jnp.exp(-(2.0 * half / width) * jnp.log(jnp.float32(THETA)))
    angle = position.astype(jnp.float32)[:, None] * inverse[None, :]
    cosine = jnp.concatenate([jnp.cos(angle), jnp.cos(angle)], axis=1)
    sine = jnp.concatenate([jnp.sin(angle), jnp.sin(angle)], axis=1)
    return (cosine, sine)


def rotate(values, cosine, sine):
    half = values.shape[-1] // 2
    turned = jnp.concatenate([-values[..., half:], values[..., :half]], axis=-1)
    return values * cosine + turned * sine


def unrotate(grads, cosine, sine):
    half = grads.shape[-1] // 2
    scaled = grads * sine
    return grads * cosine + jnp.concatenate([scaled[..., half:], -scaled[..., :half]], axis=-1)


def norm_forward(values):
    scale = lax.rsqrt(jnp.mean(values * values, axis=1, keepdims=True) + EPS)
    return (values * scale, scale)


def norm_backward(grad_in, normed, scale, gain):
    gain_term = jnp.sum(grad_in * normed, axis=0)
    inner = grad_in * gain[None, :]
    back = scale * (inner - normed * jnp.mean(inner * normed, axis=1, keepdims=True))
    return (back, gain_term)


def layout(block_lengths, count):
    slots = jnp.arange(count, dtype=jnp.int32)
    first = block_lengths[0]
    second = block_lengths[1]
    segment = (slots >= first).astype(jnp.int32) + (slots >= first + second).astype(jnp.int32)
    position = (
        slots - first * (segment >= 1).astype(jnp.int32) - second * (segment >= 2).astype(jnp.int32)
    )
    live = (segment < 2).astype(jnp.float32)[:, None]
    allowed = (segment[:, None] == segment[None, :]) & (slots[None, :] <= slots[:, None])
    return (position, live, allowed)


def masked_scores(queries, keys, allowed):
    scores = jnp.einsum(
        "qkgd,jkd->kgqj", queries, keys, preferred_element_type=jnp.float32
    ) * HD ** (-0.5)
    return jnp.where(allowed[None, None], scores, NEG)


def attend(projected, cosine, sine, allowed, count):
    kv_width = KV * HD
    queries = rotate(
        projected[:, :D].reshape(count, KV, GROUP, HD),
        cosine[:, None, None, :],
        sine[:, None, None, :],
    ).astype(jnp.bfloat16)
    keys = rotate(
        projected[:, D : D + kv_width].reshape(count, KV, HD), cosine[:, None, :], sine[:, None, :]
    ).astype(jnp.bfloat16)
    values = projected[:, D + kv_width :].reshape(count, KV, HD).astype(jnp.bfloat16)
    scores = masked_scores(queries, keys, allowed)
    top = jnp.max(scores, axis=-1, keepdims=True)
    expo = jnp.exp(scores - top)
    total = jnp.sum(expo, axis=-1, keepdims=True)
    logsum = top + jnp.log(total)
    weights = (expo / total).astype(jnp.bfloat16)
    attended = (
        jnp.einsum("kgqj,jkd->qkgd", weights, values, preferred_element_type=jnp.float32)
        .reshape(count, D)
        .astype(jnp.bfloat16)
    )
    return (queries, keys, values, logsum, attended)


def attend_back(grad_att, queries, keys, values, logsum, allowed, cosine, sine, count):
    kv_width = KV * HD
    probs = jnp.exp(masked_scores(queries, keys, allowed) - logsum)
    probs_b = probs.astype(jnp.bfloat16)
    value_grad = jnp.einsum("kgqj,qkgd->jkd", probs_b, grad_att, preferred_element_type=jnp.float32)
    prob_grad = jnp.einsum("qkgd,jkd->kgqj", grad_att, values, preferred_element_type=jnp.float32)
    delta = jnp.sum(probs * prob_grad, axis=-1, keepdims=True)
    score_grad = (probs * (prob_grad - delta) * HD ** (-0.5)).astype(jnp.bfloat16)
    query_grad = jnp.einsum("kgqj,jkd->qkgd", score_grad, keys, preferred_element_type=jnp.float32)
    key_grad = jnp.einsum("kgqj,qkgd->jkd", score_grad, queries, preferred_element_type=jnp.float32)
    query_grad = unrotate(query_grad, cosine[:, None, None, :], sine[:, None, None, :])
    key_grad = unrotate(key_grad, cosine[:, None, :], sine[:, None, :])
    return jnp.concatenate(
        [
            query_grad.reshape(count, D),
            key_grad.reshape(count, kv_width),
            value_grad.reshape(count, kv_width),
        ],
        axis=1,
    ).astype(jnp.bfloat16)


def collect(attn_flat, gate_flat, up_flat, down_flat):
    whole = (
        lax.all_gather(attn_flat, ("fsdp", "sub"), axis=0, tiled=True),
        lax.all_gather(gate_flat, ("fsdp", "sub"), axis=0, tiled=True),
        lax.all_gather(up_flat, ("fsdp", "sub"), axis=0, tiled=True),
        lax.all_gather(down_flat, ("fsdp", "sub"), axis=0, tiled=True),
    )
    return tuple((piece.reshape(D, FF) for piece in whole))


def flat_terms(pair_lists, count):
    results = []
    for pairs in pair_lists:
        blocks = [
            jnp.dot(left.T, right, preferred_element_type=jnp.float32) for left, right in pairs
        ]
        joined = blocks[0] if len(blocks) == 1 else jnp.concatenate(blocks, axis=1)
        results.append(joined.reshape(-1).reshape(count, piece_width))
    return jnp.concatenate(results, axis=1)


def split_owned(owned):
    return tuple(
        (
            owned[:, index * piece_width : (index + 1) * piece_width].reshape(-1)
            for index in range(4)
        )
    )


def spread(pair_lists):
    share = D * FF // (piece_width * lax.axis_size("fsdp") * lax.axis_size("sub"))
    owned = lax.psum_scatter(
        flat_terms(pair_lists, share * lax.axis_size(("fsdp", "sub"))),
        ("fsdp", "sub"),
        scatter_dimension=0,
        tiled=True,
    )
    return split_owned(owned)


def flat_path(
    rows32,
    cotangent,
    live,
    allowed,
    cosine,
    sine,
    gain_attn,
    gain_mlp,
    normed1,
    scale1,
    input1,
    flats,
):
    count = rows32.shape[0]
    q_width = D + 2 * KV * HD
    attn_mat, gate_mat, up_mat, down_mat = collect(flats[0], flats[1], flats[2], flats[3])
    projected = jnp.dot(input1, attn_mat[:, :q_width], preferred_element_type=jnp.float32)
    queries, keys, values, logsum, attended = attend(projected, cosine, sine, allowed, count)
    hidden1 = rows32 + jnp.dot(
        attended, attn_mat[:, q_width:].T, preferred_element_type=jnp.float32
    )
    normed2, scale2 = norm_forward(hidden1)
    input2 = (normed2 * gain_mlp[None, :]).astype(jnp.bfloat16)
    gate = jnp.dot(input2, gate_mat, preferred_element_type=jnp.float32)
    up = jnp.dot(input2, up_mat, preferred_element_type=jnp.float32)
    sigma = jax.nn.sigmoid(gate)
    active = gate * sigma
    hidden = (active * up).astype(jnp.bfloat16)
    result = hidden1 + jnp.dot(hidden, down_mat.T, preferred_element_type=jnp.float32)
    output = (live * result).astype(jnp.bfloat16)
    attn_back, gate_back, up_back, down_back = collect(flats[0], flats[1], flats[2], flats[3])
    grad_out = live * cotangent.astype(jnp.float32)
    grad_outb = grad_out.astype(jnp.bfloat16)
    grad_hidden = jnp.dot(grad_outb, down_back, preferred_element_type=jnp.float32)
    grad_gate = (grad_hidden * up * sigma * (1.0 + gate * (1.0 - sigma))).astype(jnp.bfloat16)
    grad_up = (grad_hidden * active).astype(jnp.bfloat16)
    grad_in2 = jnp.dot(grad_gate, gate_back.T, preferred_element_type=jnp.float32) + jnp.dot(
        grad_up, up_back.T, preferred_element_type=jnp.float32
    )
    back2, gain2_term = norm_backward(grad_in2, normed2, scale2, gain_mlp)
    grad_h1 = grad_out + back2
    grad_h1b = grad_h1.astype(jnp.bfloat16)
    grad_att = (
        jnp.dot(grad_h1b, attn_back[:, q_width:], preferred_element_type=jnp.float32)
        .astype(jnp.bfloat16)
        .reshape(count, KV, GROUP, HD)
    )
    proj_grad = attend_back(grad_att, queries, keys, values, logsum, allowed, cosine, sine, count)
    grad_in1 = jnp.dot(proj_grad, attn_back[:, :q_width].T, preferred_element_type=jnp.float32)
    back1, gain1_term = norm_backward(grad_in1, normed1, scale1, gain_attn)
    input_grad = grad_h1 + back1
    pair_lists = (
        ((input1, proj_grad), (grad_h1b, attended)),
        ((input2, grad_gate),),
        ((input2, grad_up),),
        ((grad_outb, hidden),),
    )
    owned = spread(pair_lists)
    return (output, input_grad, owned, gain1_term, gain2_term)


def plain_body(rows, cotangent, lengths, gains, attn_weight, gate_weight, up_weight, down_weight):
    count = rows.shape[0]
    position, live, allowed = layout(lengths, count)
    cosine, sine = rope_tables(position, HD)
    full_gains = lax.all_gather(gains, "fsdp", axis=0, tiled=True).astype(jnp.float32)
    gain_attn = full_gains[:D]
    gain_mlp = full_gains[D:]
    rows32 = rows.astype(jnp.float32)
    normed1, scale1 = norm_forward(rows32)
    input1 = (normed1 * gain_attn[None, :]).astype(jnp.bfloat16)
    flats = (attn_weight, gate_weight, up_weight, down_weight)
    output, input_grad, owned, gain1_term, gain2_term = flat_path(
        rows32,
        cotangent,
        live,
        allowed,
        cosine,
        sine,
        gain_attn,
        gain_mlp,
        normed1,
        scale1,
        input1,
        flats,
    )
    gain_total = lax.psum(jnp.concatenate([gain1_term, gain2_term]), ("fsdp", "sub"))
    share = gains.shape[0]
    gain_grad = lax.dynamic_slice_in_dim(gain_total, lax.axis_index("fsdp") * share, share)
    return (output, input_grad, owned[0], owned[1], owned[2], owned[3], gain_grad)


BF = jnp.bfloat16
F32 = jnp.float32


def swap(value, axis, bit):
    return lax.ppermute(value, axis, [(i, i ^ bit) for i in range(lax.axis_size(axis))])


def meet(*values):
    return lax.optimization_barrier(values)


def after(value, *done):
    return lax.optimization_barrier((value, *done))[0]


def add2(kept, came):
    return (kept.astype(F32) + came.astype(F32)).astype(BF)


def far_pair(value, axis, odd):
    shape = value.shape
    value = value.reshape(shape[:axis] + (shape[axis] // 2, 2) + shape[axis + 1 :])
    return lax.index_in_dim(value, odd, axis + 1, keepdims=False)


def pick(value, index, axis):
    return lax.dynamic_index_in_dim(value, index, axis, keepdims=False)


def put2(own, came, bit, axis):
    first = bit == 0
    return jnp.stack([jnp.where(first, own, came), jnp.where(first, came, own)], axis=axis)


def mm(a, b):
    return jnp.dot(a, b, preferred_element_type=F32)


def mm_t(a, b):
    return lax.dot_general(a, b, (((1,), (1,)), ((), ())), preferred_element_type=F32)


def term(a, b):
    return lax.dot_general(a, b, (((0,), (0,)), ((), ())), preferred_element_type=F32).astype(BF)


def dot_f(a, b):
    return lax.dot_general(a, b, (((1,), (0,)), ((), ())), preferred_element_type=F32)


def dot_t(a, b):
    return lax.dot_general(a, b, (((1,), (1,)), ((), ())), preferred_element_type=F32)


def dot_0(a, b):
    return lax.dot_general(a, b, (((0,), (0,)), ((), ())), preferred_element_type=F32)


def stacked(parts):
    return jnp.concatenate(parts, axis=0)


def norm_rows(values):
    mean = jnp.sum(values * values, axis=1, keepdims=True) * (1.0 / D)
    scale = lax.rsqrt(mean + EPS)
    return values * scale, scale


def norm_rows_back(grad_in, normed, scale, gain):
    gain_term = jnp.sum(grad_in * normed, axis=0, keepdims=True)
    inner = grad_in * gain
    mean = jnp.sum(inner * normed, axis=1, keepdims=True) * (1.0 / D)
    return scale * (inner - normed * mean), gain_term


def first_half(shape):
    return lax.broadcasted_iota(jnp.int32, shape, 1) % HD < HD // 2


def gain_masks(owner, my_fsdp, n_fsdp, own, share):
    wide = owner.shape[1]
    per = share // own
    place = lax.broadcasted_iota(jnp.int32, (n_fsdp, wide), 0) ^ my_fsdp
    group = owner // per
    return place == group, place == group + n_fsdp // 2


def slot_matrix(owner, inner, own, height):
    per = D * 2 // 8 // own
    slot = jnp.where(inner < own, owner % per * own + inner, -1)
    return (lax.broadcasted_iota(jnp.int32, (height, owner.shape[1]), 0) == slot).astype(F32).astype(BF)


def make_forward(n_fsdp, own, padded, share, by_fsdp):
    kv_width = KV * HD

    def kernel(
        place_ref, rows_ref, owner_ref, inner_ref, cos_ref, sin_ref, seg_ref,
        own_q_ref, came_q_ref, own_o_ref, came_o_ref,
        att_ref, qk_ref, v_ref, logsum_ref, hidden1_ref, input2_ref, gains_ref, attn_q_ref, attn_o_ref,
    ):
        core = place_ref[1]
        for p in range(own_q_ref.shape[0] // padded):
            here = pl.ds(pl.multiple_of((2 * p + core) * padded, padded), padded)
            there = pl.ds(pl.multiple_of((2 * p + 1 - core) * padded, padded), padded)
            block = slice(p * padded, (p + 1) * padded)
            attn_q_ref[here, :] = own_q_ref[block, :]
            attn_q_ref[there, :] = came_q_ref[block, :]
            attn_o_ref[here, :] = own_o_ref[block, :]
            attn_o_ref[there, :] = came_o_ref[block, :]
        pieces = jnp.concatenate(
            [attn_q_ref[p * padded + own : p * padded + own + 1, :share].astype(F32) for p in by_fsdp], axis=0
        ).astype(BF)
        owner = owner_ref[...]
        first, second = gain_masks(owner, place_ref[0], n_fsdp, own, share)
        spots = dot_f(pieces, slot_matrix(owner, inner_ref[...], own, share))
        gain1 = jnp.sum(jnp.where(first, spots, 0.0), axis=0, keepdims=True)
        gain2 = jnp.sum(jnp.where(second, spots, 0.0), axis=0, keepdims=True)
        gains_ref[0:1, :] = gain1
        gains_ref[1:2, :] = gain2
        rows = rows_ref[...]
        normed, _ = norm_rows(rows)
        input1 = (normed * gain1).astype(BF)
        projected = dot_f(input1, attn_q_ref[...])
        cosine = cos_ref[...]
        sine = sin_ref[...]
        low = first_half(cosine.shape)
        for i in range(projected.shape[1] // 128):
            part = projected[:, 128 * i : 128 * (i + 1)]
            turned = jnp.where(low, -pltpu.roll(part, 96, 1), pltpu.roll(part, 32, 1))
            qk_ref[:, 128 * i : 128 * (i + 1)] = (part * cosine + turned * sine).astype(BF)
        values = dot_f(input1, attn_o_ref[:, :384]).astype(BF)
        v_ref[...] = values
        count = rows.shape[0]
        allowed = stacked([seg_ref[...]] * GROUP) > 0.0
        att_ref[:, :128] = jnp.zeros((count, 128), BF)
        shift = kv_width - 256
        for k in range(KV):
            keys = qk_ref[:, D + HD * k : D + HD * (k + 1)]
            value = values[:, HD * k : HD * (k + 1)]
            heads = [HD * (GROUP * k + g) for g in range(GROUP)]
            queries = stacked([qk_ref[:, h : h + HD] for h in heads])
            scores = jnp.where(allowed, dot_t(queries, keys) * HD ** (-0.5), NEG)
            top = jnp.max(scores, axis=1, keepdims=True)
            expo = jnp.exp(scores - top)
            total = jnp.sum(expo, axis=1, keepdims=True)
            logsum_ref[:, k : k + 1] = top + jnp.log(total)
            weights = (expo / total).astype(BF)
            attended = dot_f(weights, value).astype(BF)
            for g, h in enumerate(heads):
                att_ref[:, shift + h : shift + h + HD] = attended[count * g : count * (g + 1), :]
        hidden1 = rows + dot_t(att_ref[...], attn_o_ref[:, 256:])
        hidden1_ref[...] = hidden1
        normed2, _ = norm_rows(hidden1)
        input2_ref[...] = (normed2 * gain2).astype(BF)

    return kernel


def norm_kernel(
    place_ref, grad_a_ref, grad_b_ref, grad_out_ref, hidden1_ref, gains_ref,
    grad_h1_ref, grad_h1b_ref, gain2_ref,
):
    grad_in2 = grad_a_ref[...].astype(F32) + grad_b_ref[...].astype(F32)
    normed2, scale2 = norm_rows(hidden1_ref[...])
    back2, gain2_term = norm_rows_back(grad_in2, normed2, scale2, gains_ref[1:2, :])
    grad_h1 = grad_out_ref[: hidden1_ref.shape[0], :].astype(F32) + back2
    grad_h1_ref[...] = grad_h1
    grad_h1b_ref[...] = grad_h1.astype(BF)
    gain2_ref[...] = gain2_term


def make_backward(n_fsdp, own):
    kv_width = KV * HD

    def kernel(
        place_ref, grad_h1_ref, grad_h1b_ref, gain2_ref, rows_ref, gains_ref, owner_ref, inner_ref,
        cos_ref, sin_ref, seg_ref, qk_ref, v_ref, logsum_ref, attn_q_ref, attn_o_ref,
        grads_ref, input_grad_ref,
        turn_ref,
    ):
        count = rows_ref.shape[0]
        qk_width = turn_ref.shape[1]
        grad_att = dot_f(grad_h1b_ref[...], attn_o_ref[...]).astype(BF)
        allowed = stacked([seg_ref[...]] * GROUP) > 0.0
        grads_ref[:count, qk_width:] = jnp.zeros((count, 384), BF)
        for k in range(KV):
            keys = qk_ref[:, D + HD * k : D + HD * (k + 1)]
            value = v_ref[:, HD * k : HD * (k + 1)]
            heads = [HD * (GROUP * k + g) for g in range(GROUP)]
            queries = stacked([qk_ref[:, h : h + HD] for h in heads])
            grad = stacked([grad_att[:, kv_width + h : kv_width + h + HD] for h in heads])
            scores = jnp.where(allowed, dot_t(queries, keys) * HD ** (-0.5), NEG)
            probs = jnp.exp(scores - logsum_ref[:, k : k + 1])
            value_grad = dot_0(probs.astype(BF), grad)
            prob_grad = dot_t(grad, value)
            delta = jnp.sum(probs * prob_grad, axis=1, keepdims=True)
            score_grad = (probs * (prob_grad - delta) * HD ** (-0.5)).astype(BF)
            query_grad = dot_f(score_grad, keys)
            for g, h in enumerate(heads):
                turn_ref[:, h : h + HD] = query_grad[count * g : count * (g + 1), :]
            turn_ref[:, D + HD * k : D + HD * (k + 1)] = dot_0(score_grad, queries)
            grads_ref[:count, qk_width + HD * k : qk_width + HD * (k + 1)] = value_grad.astype(BF)
        cosine = cos_ref[...]
        sine = sin_ref[...]
        low = first_half(cosine.shape)
        for i in range(qk_width // 128):
            part = turn_ref[:, 128 * i : 128 * (i + 1)]
            scaled = part * sine
            turned = jnp.where(low, pltpu.roll(scaled, 96, 1), -pltpu.roll(scaled, 32, 1))
            grads_ref[:count, 128 * i : 128 * (i + 1)] = (part * cosine + turned).astype(BF)
        owner = owner_ref[...]
        inner = inner_ref[...]
        grad_in1 = dot_t(grads_ref[:count, :qk_width], attn_q_ref[...]) * jnp.where(inner < own, 1.0, 0.0)
        grad_in1 = grad_in1 + dot_t(grads_ref[:count, qk_width:], attn_o_ref[:, :384])
        normed1, scale1 = norm_rows(rows_ref[...])
        back1, gain1_term = norm_rows_back(grad_in1, normed1, scale1, gains_ref[0:1, :])
        input_grad_ref[...] = grad_h1_ref[...] + back1
        first, second = gain_masks(owner, place_ref[0], n_fsdp, own, D * 2 // n_fsdp)
        both = jnp.where(first, gain1_term, 0.0) + jnp.where(second, gain2_ref[...], 0.0)
        gain_rows = dot_t(both.astype(BF), slot_matrix(owner, inner, own, 256))
        extra = grads_ref.shape[0] - count
        grads_ref[count:, :] = jnp.zeros((extra, grads_ref.shape[1]), BF)
        gain_rows = jnp.concatenate([gain_rows, jnp.zeros((extra - n_fsdp, 256), F32)], axis=0)
        grads_ref[count:, :256] = gain_rows.astype(BF)

    return kernel


def make_terms(n_far, n_sub, own, padded, count):
    def kernel(place_ref, rows_a_ref, rows_b_ref, gains_ref, select_d_ref, *refs):
        att_refs = refs[:n_sub]
        grad_h1_refs = refs[n_sub : 2 * n_sub]
        grads_refs = refs[2 * n_sub : 3 * n_sub]
        keep_ref, send_ref = refs[3 * n_sub :]
        half_ff = FF // 2
        rows = keep_ref.shape[0] * 2
        wide = grad_h1_refs[0].shape[1]

        def tokens(pieces):
            return jnp.concatenate(pieces, axis=0)

        spot = lax.broadcasted_iota(jnp.int32, (wide, rows), 1)
        source = (spot // padded * n_sub + place_ref[2]) * padded + spot % padded
        select = (lax.broadcasted_iota(jnp.int32, (wide, rows), 0) == source).astype(F32).astype(BF)
        rows_b = jnp.concatenate([rows_a_ref[...], rows_b_ref[...]], axis=0)
        group = rows_b.astype(F32)
        scale = lax.rsqrt(jnp.sum(group * group, axis=1, keepdims=True) * (1.0 / D) + EPS)
        gain = dot_f(gains_ref[...].astype(BF), select)[0:1, :]
        left1 = (dot_f(rows_b, select_d_ref[...]) * scale * gain).astype(BF)
        left2 = dot_f(tokens([ref[...] for ref in grad_h1_refs]), select).astype(BF)
        right = tokens([ref[:count, :] for ref in grads_refs])
        extra = tokens([ref[count:, :256] for ref in grads_refs])
        spot = lax.broadcasted_iota(jnp.int32, (extra.shape[0], rows), 1)
        block = spot // padded
        here = lax.broadcasted_iota(jnp.int32, spot.shape, 0) % (extra.shape[0] // n_sub)
        wanted = jnp.where(spot % padded == own, block % n_far * 2 + block // n_far, -1)
        spots = (here == wanted).astype(F32).astype(BF)
        q_term = dot_0(left1, right)
        start = q_term[:, :256] + dot_0(spots, extra)
        o_term = dot_0(left2, tokens([ref[...] for ref in att_refs]))
        mixed = o_term[:, :128] + q_term[:, half_ff + 256 :]
        for ref, at in ((keep_ref, 0), (send_ref, rows // 2)):
            to = slice(at, at + rows // 2)
            ref[:, :256] = start[to, :].astype(BF)
            ref[:, 256:half_ff] = q_term[to, 256:half_ff].astype(BF)
            ref[:, half_ff : half_ff + 256] = q_term[to, half_ff : half_ff + 256].astype(BF)
            ref[:, half_ff + 256 : half_ff + 384] = mixed[to, :].astype(BF)
            ref[:, half_ff + 384 :] = o_term[to, 128:].astype(BF)

    return kernel


VMEM = pl.BlockSpec(memory_space=pltpu.VMEM)
SMEM = pl.BlockSpec(memory_space=pltpu.SMEM)


def run_kernel(kernel, outs, args, scratch=(), name=None):
    return pl.pallas_call(
        kernel,
        out_shape=[jax.ShapeDtypeStruct(shape, kind) for shape, kind in outs],
        in_specs=[SMEM] + [VMEM] * (len(args) - 1),
        out_specs=[VMEM] * len(outs),
        scratch_shapes=scratch,
        compiler_params=pltpu.CompilerParams(vmem_limit_bytes=56 << 20),
        cost_estimate=pl.CostEstimate(flops=1000, transcendentals=0, bytes_accessed=1000),
        name=name,
    )(*args)


def body(rows, cotangent, lengths, gains, attn_weight, gate_weight, up_weight, down_weight):
    count = rows.shape[0]
    n_fsdp = lax.axis_size("fsdp")
    n_sub = lax.axis_size("sub")
    n_all = n_fsdp * n_sub
    n_far = n_fsdp // 2
    own = D // n_all
    padded = -(-(own + 1) // 16) * 16
    wide = n_all * padded
    half_ff = FF // 2
    quarter = FF // 4
    share = gains.shape[0]
    kv_width = KV * HD
    my_fsdp = lax.axis_index("fsdp")
    my_sub = lax.axis_index("sub")
    my_y = my_sub // 2
    my_c = my_sub % 2

    column = jnp.arange(wide, dtype=jnp.int32)
    place = column // padded
    inner = column % padded
    rel = (place // n_sub) % n_far * 2 + place // (n_sub * n_far)
    real = inner < own
    source = jnp.where(real, ((rel ^ my_fsdp) * n_sub + place % n_sub) * own + inner, -1)
    spread_mat = (jnp.arange(D, dtype=jnp.int32)[:, None] == source[None, :]).astype(BF)

    def padded_block(flat):
        return jnp.pad(flat.reshape(own, FF), ((0, padded - own), (0, 0)))

    def columns(value, index, width):
        return lax.dynamic_slice_in_dim(value, index * width, width, axis=value.ndim - 1)

    position, live, allowed = layout(lengths, count)
    cosine, sine = rope_tables(position, HD)
    cosine = jnp.concatenate([cosine, cosine], axis=1)
    sine = jnp.concatenate([sine, sine], axis=1)
    seg = allowed.astype(F32)
    rows32 = mm(rows, spread_mat)

    owner = ((rel ^ my_fsdp) * n_sub + place % n_sub)[None, :]
    spot = jnp.arange(wide // n_sub, dtype=jnp.int32)
    block = spot // padded
    target = ((block % n_far * 2 + block // n_far) ^ my_fsdp) * n_sub + my_sub
    target = jnp.where(spot % padded < own, target * own + spot % padded, -1)
    own_select = (jnp.arange(D, dtype=jnp.int32)[:, None] == target[None, :]).astype(BF)

    attn_block = padded_block(attn_weight)
    attn_block = attn_block.at[own, :share].set(gains)
    far = [swap(attn_block, "fsdp", 2 * k) for k in range(1, n_far)]
    mlp_block = jnp.stack([padded_block(w) for w in (gate_weight, up_weight, down_weight)])
    sent = columns(mlp_block, 1 - my_y, half_ff)
    came = swap(sent, "sub", 2)
    cot = (live * after(cotangent, sent).astype(F32)).astype(BF)
    cot_y = swap(cot, "sub", 2)
    mlp_block = put2(columns(mlp_block, my_y, half_ff), came, my_y, 1)
    came = swap(columns(mlp_block, 1 - my_c, quarter), "sub", 1)
    mlp_block = put2(columns(mlp_block, my_c, quarter), came, my_c, 2)
    mlp_block = mlp_block.reshape(3, n_sub * padded, quarter)
    far, mlp_block, cot, cot_y = meet(far, mlp_block, cot, cot_y)

    attn_far = jnp.stack([attn_block] + list(far))
    half0 = attn_far[:, :, :half_ff]
    half1 = attn_far[:, :, half_ff:]
    gate_up = mlp_block[:2]
    down = mlp_block[2]
    x0, y1, near = swap(half0, "fsdp", 1), swap(half1, "sub", 2), swap(gate_up, "fsdp", 2)
    cot = jnp.concatenate([cot, cot_y])
    cot_c = swap(cot, "sub", 1)
    tables = (owner, inner[None, :])
    angles = (cosine, sine, seg)
    half0, half1, gate_up, down, x0, y1, near, rows32, cot, cot_c, tables, angles, own_select = meet(
        half0, half1, gate_up, down, x0, y1, near, rows32, cot, cot_c, tables, angles, own_select
    )

    half0 = jnp.stack([half0, x0])
    half1 = put2(half1, y1, my_y, 1)
    y0, x1, third = swap(half0, "sub", 2), swap(half1, "fsdp", 1), swap(gate_up, "fsdp", 4)
    down_x = swap(down, "fsdp", 1)
    cot_all = mm(jnp.concatenate([cot, cot_c]), spread_mat).astype(BF)
    half0, half1, gate_up, down, down_x, near, y0, x1, third, cot_all = meet(
        half0, half1, gate_up, down, down_x, near, y0, x1, third, cot_all
    )

    half0 = put2(half0, y0, my_y, 2).reshape(wide // 2, half_ff)
    half1 = jnp.stack([half1, x1]).reshape(wide // 2, half_ff)
    c0, c1, last = swap(half0, "sub", 1), swap(half1, "sub", 1), swap(third, "fsdp", 2)
    down = jnp.stack([down, down_x])
    gate_up_a = jnp.stack([gate_up, near])
    gate_up_xa = swap(gate_up_a, "fsdp", 1)
    rows_y = swap(rows, "sub", 2)
    half0, half1, c0, c1, third, last, down, rows_y = meet(half0, half1, c0, c1, third, last, down, rows_y)
    rows_all = jnp.concatenate([rows, rows_y])

    gate_up_b = jnp.stack([third, last])
    gate_up_xb = swap(gate_up_b, "fsdp", 1)
    down_near, down_third = swap(down, "fsdp", 2), swap(down, "fsdp", 4)
    by_fsdp = [(f % 2) * n_far * n_sub + (f // 2) * n_sub for f in range(n_fsdp)]
    my_place = jnp.stack([my_fsdp, my_c, my_sub])
    tall = (count, wide)
    forward = run_kernel(
        make_forward(n_fsdp, own, padded, share, by_fsdp),
        [
            ((count, half_ff - 256), BF),
            ((count, half_ff), BF),
            ((count, 384), BF),
            ((count * GROUP, KV), F32),
            (tall, F32),
            (tall, BF),
            ((2, wide), F32),
            ((wide, half_ff), BF),
            ((wide, half_ff), BF),
        ],
        (my_place, rows32, *tables, *angles, half0, c0, half1, c1),
        name="attn_forward",
    )
    att, qk, values, logsum, hidden1, input2, gains_p, attn_q, attn_o = forward

    in2_y = swap(input2, "sub", 2)
    input2, in2_y, down_near, down_third, gate_up_xa, gate_up_xb = meet(
        input2, in2_y, down_near, down_third, gate_up_xa, gate_up_xb
    )
    down_last = swap(down_third, "fsdp", 2)
    in2_all = jnp.stack([input2, in2_y])
    in2_c = swap(in2_all, "sub", 1)
    rows_c = swap(rows_all, "sub", 1)
    in2_c, rows_c = meet(in2_c, rows_c)
    att_y = swap(after(att, in2_c), "sub", 2)
    in2_all = jnp.stack([in2_all, in2_c]).reshape(4 * count, wide)
    gate_up_all = jnp.concatenate([gate_up_a, gate_up_b, gate_up_xa, gate_up_xb])
    gate_w = gate_up_all[:, 0].reshape(wide, quarter)
    up_w = gate_up_all[:, 1].reshape(wide, quarter)
    gate = mm(in2_all, gate_w)
    up = mm(in2_all, up_w)
    sigma = jax.nn.sigmoid(gate)
    active = gate * sigma
    hidden = (active * up).astype(BF)
    down_term = term(cot_all, hidden).reshape(2, n_far, n_sub * padded, quarter)
    hidden, down_term, down_last = meet(hidden, down_term, down_last)
    down_w = jnp.stack([down, down_near, down_third, down_last])
    down_w = down_w.transpose(1, 0, 2, 3).reshape(wide, quarter)
    down_near_came = swap(far_pair(down_term, 1, 1), "fsdp", 2)
    grad_hidden = mm(cot_all, down_w)
    grad_gate = (grad_hidden * up * sigma * (1.0 + gate * (1.0 - sigma))).astype(BF)
    grad_up = (grad_hidden * active).astype(BF)
    grad_in2 = (mm_t(grad_gate, gate_w) + mm_t(grad_up, up_w)).astype(BF).reshape(2, 2 * count, wide)
    in2_terms = after(in2_all, grad_in2)
    gate_up_term = [
        term(in2_terms, grad).reshape(2, n_far, n_sub * padded, quarter) for grad in (grad_gate, grad_up)
    ]
    gate_up_x_came = [swap(part[1], "fsdp", 1) for part in gate_up_term]
    result = mm_t(hidden, down_w).astype(BF).reshape(2, 2 * count, wide)

    came = swap(grad_in2[1], "sub", 1)
    came, att_y = meet(came, att_y)
    atts = [att, att_y, swap(att, "sub", 1), swap(att_y, "sub", 1)]
    grad_in2 = add2(grad_in2[0], came).reshape(2, count, wide)
    grad_in2_y = swap(grad_in2[1], "sub", 2)
    down_held = add2(far_pair(down_term, 1, 0), down_near_came)
    grad_in2_y, result, down_held, atts = meet(grad_in2_y, result, down_held, atts)
    down_far_came = swap(down_held[:, 1], "fsdp", 4)
    grad_h1, grad_h1b, gain2_term = run_kernel(
        norm_kernel,
        [(tall, F32), (tall, BF), ((1, wide), F32)],
        (my_place, grad_in2[0], grad_in2_y, cot_all, hidden1, gains_p),
        name="norm_backward",
    )
    grad_h1_y = swap(grad_h1b, "sub", 2)
    grads, input_grad = run_kernel(
        make_backward(n_fsdp, own),
        [((count + 16, half_ff + 384), BF), (tall, F32)],
        (
            my_place, grad_h1, grad_h1b, gain2_term, rows32, gains_p, *tables, *angles,
            qk, values, logsum, attn_q, attn_o,
        ),
        scratch=[pltpu.VMEM((count, half_ff), F32)],
        name="attn_backward",
    )

    grads_y = swap(grads, "sub", 2)
    grads, grad_h1_y, gate_up_x_came, down_far_came = meet(
        grads, grad_h1_y, gate_up_x_came, down_far_came
    )
    grads_c = swap(grads, "sub", 1)
    grad_h1_c, grad_h1_yc = swap(grad_h1b, "sub", 1), swap(grad_h1_y, "sub", 1)
    down_held = add2(down_held[:, 0], down_far_came)
    down_x_came = swap(down_held[1], "fsdp", 1)
    gate_up_x_came, down_held = meet(gate_up_x_came, down_held)
    gate_up_held = jnp.stack([add2(part[0], came) for part, came in zip(gate_up_term, gate_up_x_came)])
    gate_up_near = swap(far_pair(gate_up_held, 1, 1), "fsdp", 2)
    grads_y, grads_c, grad_h1_c, grad_h1_yc, down_x_came = meet(
        grads_y, grads_c, grad_h1_c, grad_h1_yc, down_x_came
    )

    grads_yc = swap(grads_y, "sub", 1)
    attn_keep, attn_send = run_kernel(
        make_terms(n_far, n_sub, own, padded, count),
        [((n_far * padded, FF), BF)] * 2,
        (
            my_place, rows_all, rows_c, gains_p, own_select, *atts, grad_h1b, grad_h1_y, grad_h1_c, grad_h1_yc, grads, grads_y, grads_c, grads_yc,
        ),
        name="attn_terms",
    )

    attn_x = swap(attn_send, "fsdp", 1)
    gate_up_held = add2(far_pair(gate_up_held, 1, 0), after(gate_up_near, attn_send))
    gate_up_far = swap(gate_up_held[:, 1], "fsdp", 4)
    res_c = swap(after(result[1], attn_send), "sub", 1)
    result = add2(result[0], res_c).reshape(2, count, wide)
    res_y = swap(result[1], "sub", 2)
    input_grad = after(input_grad, attn_send)
    input_grad = lax.dot_general(
        input_grad,
        spread_mat.astype(F32),
        (((1,), (1,)), ((), ())),
        precision=lax.Precision.HIGHEST,
    )
    attn_x, gate_up_far, input_grad, res_y = meet(attn_x, gate_up_far, input_grad, res_y)

    def side_by_side(mine, came, bit):
        first = bit == 0
        return jnp.concatenate([jnp.where(first, mine, came), jnp.where(first, came, mine)], axis=-1)

    attn_held = add2(attn_keep, attn_x).reshape(n_far, padded, FF)
    attn_near = swap(far_pair(attn_held, 0, 1), "fsdp", 2)
    down_own = add2(down_held[0], down_x_came)[None]
    mlp_own = jnp.concatenate([add2(gate_up_held[:, 0], gate_up_far), down_own])
    mlp_own = mlp_own.reshape(3, 2, 2, padded, quarter)
    mlp_c = swap(pick(mlp_own, 1 - my_c, 2), "sub", 1)
    attn_near, mlp_c = meet(attn_near, mlp_c)
    attn_held = add2(far_pair(attn_held, 0, 0), attn_near)
    attn_held, mlp_c = meet(attn_held, mlp_c)
    mlp_own = side_by_side(pick(mlp_own, my_c, 2), mlp_c, my_c)
    mlp_y = swap(pick(mlp_own, 1 - my_y, 1), "sub", 2)
    attn_far = swap(attn_held[1], "fsdp", 4)
    result = hidden1 + result[0].astype(F32) + res_y.astype(F32)
    output = mm_t((live * result).astype(BF), spread_mat).astype(BF)
    mlp_own = side_by_side(pick(mlp_own, my_y, 1), mlp_y, my_y)

    def flat(part):
        return part[:own].astype(F32).reshape(-1)

    mlp_flat = [flat(mlp_own[i]) for i in range(3)]
    attn_far, mlp_flat, output = meet(attn_far, mlp_flat, output)
    attn_own = add2(attn_held[0], attn_far)
    gain_grad = attn_own[own, :share].astype(F32)
    return (
        output,
        input_grad,
        flat(attn_own),
        *mlp_flat,
        gain_grad,
    )


def solution(mesh):
    n_fsdp, n_sub = mesh.shape["fsdp"], mesh.shape["sub"]
    n_all = n_fsdp * n_sub
    by_rows = (
        n_fsdp == 8 and D % n_all == 0 and n_fsdp & (n_fsdp - 1) == 0 and n_fsdp > 1 and n_sub == 4 and D // n_fsdp % (D // n_all) == 0
    )
    in_specs = (
        P(("fsdp", "sub"), None),
        P(("fsdp", "sub"), None),
        P(("fsdp", "sub")),
        P("fsdp"),
        P(("fsdp", "sub")),
        P(("fsdp", "sub")),
        P(("fsdp", "sub")),
        P(("fsdp", "sub")),
    )
    out_specs = (
        P(("fsdp", "sub"), None),
        P(("fsdp", "sub"), None),
        P(("fsdp", "sub")),
        P(("fsdp", "sub")),
        P(("fsdp", "sub")),
        P(("fsdp", "sub")),
        P("fsdp"),
    )
    return jax.shard_map(body if by_rows else plain_body, mesh=mesh, in_specs=in_specs, out_specs=out_specs, check_vma=False)
```
